32 devices in a mesh: dp: 16 (over z, y, core), head: 2 (over x).
Axes of the slice: x: 2, y: 2, z: 4, core: 2. Of those that a mesh axis runs over, the one named last changes fastest.
Arguments:
- tokens: bfloat16 [16, 256, 512], P('dp', 'head'), may hold values from -6 to 6
- lengths: int32 [16], P('dp'), may hold values from 32 to 256, as said below
- cotangent: bfloat16 [16, 256, 512], P('dp', 'head'), may hold values from -6 to 6
- glu_weight: bfloat16 [512, 1024], replicated, may hold values from -0.25 to 0.25
- glu_bias: bfloat16 [1024], replicated, may hold values from -1.75 to 1.75
- norm_gain: bfloat16 [4, 512], replicated, may hold values from 0.25 to 1.75
- norm_bias: bfloat16 [4, 512], replicated, may hold values from -1.75 to 1.75
- mid_gain: bfloat16 [2048], replicated, may hold values from 0.25 to 1.75
- mid_bias: bfloat16 [2048], replicated, may hold values from -1.75 to 1.75
- left_weight: bfloat16 [512, 2048], replicated, may hold values from -0.25 to 0.25
- left_bias: bfloat16 [2048], replicated, may hold values from -1.75 to 1.75
- conv_weight: bfloat16 [3, 512, 256], replicated, may hold values from -0.15625 to 0.15625
- conv_bias: bfloat16 [256], replicated, may hold values from -1.75 to 1.75
- depth_weight: bfloat16 [9, 2048], replicated, may hold values from -2 to 2
- point_weight: bfloat16 [2048, 256], replicated, may hold values from -0.125 to 0.125
- point_bias: bfloat16 [256], replicated, may hold values from -1.75 to 1.75
- qkv_weight: bfloat16 [512, 1536], replicated, may hold values from -0.375 to 0.375
- out_weight: bfloat16 [512, 512], replicated, may hold values from -1 to 1
- ffn_in_weight: bfloat16 [512, 2048], replicated, may hold values from -0.25 to 0.25
- ffn_in_bias: bfloat16 [2048], replicated, may hold values from -1.75 to 1.75
- ffn_out_weight: bfloat16 [2048, 512], replicated, may hold values from -0.125 to 0.125
- ffn_out_bias: bfloat16 [512], replicated, may hold values from -1.75 to 1.75
Outputs:
- out_tokens: bfloat16 [16, 256, 512], P('dp', 'head')
- grad_tokens: float32 [16, 256, 512], P('dp', 'head')
- grad_glu_weight: float32 [512, 1024], P('dp')
- grad_glu_bias: float32 [1024], P('dp')
- grad_norm_gain: float32 [4, 512], P(None, 'dp')
- grad_norm_bias: float32 [4, 512], P(None, 'dp')
- grad_mid_gain: float32 [2048], P('dp')
- grad_mid_bias: float32 [2048], P('dp')
- grad_left_weight: float32 [512, 2048], P('dp')
- grad_left_bias: float32 [2048], P('dp')
- grad_conv_weight: float32 [3, 512, 256], P(None, 'dp')
- grad_conv_bias: float32 [256], replicated
- grad_depth_weight: float32 [9, 2048], P(None, 'dp')
- grad_point_weight: float32 [2048, 256], P('dp')
- grad_point_bias: float32 [256], replicated
- grad_qkv_weight: float32 [512, 1536], P('dp')
- grad_out_weight: float32 [512, 512], P('dp')
- grad_ffn_in_weight: float32 [512, 2048], P('dp')
- grad_ffn_in_bias: float32 [2048], P('dp')
- grad_ffn_out_weight: float32 [2048, 512], P('dp')
- grad_ffn_out_bias: float32 [512], P('dp')
The draws below stay inside these ranges and needn't reach their ends.
Inputs may be any that keep to these rules, and one draw needn't show every extreme that they name: `lengths`: counted from the start of the row; some row is full.
All inputs are finite; a program needn't handle non-finite values.
Results may differ from the reference program's by a relative error of at most 0.03.
The reference program's roundings to bfloat16 on the way count: a program that leaves them out, or rounds other values in their place, can miss the bound.
Values may be sent and summed in bfloat16 or wider, within the bound.
No kernel may reach another device: no remote copies, remote signals or barrier semaphores. Data moves between devices by JAX's collectives and lax.ppermute only.
A program may use at most 128 MiB of HBM per device.

```python
import jax
import jax.numpy as jnp
from jax import lax

D = 512
HEADS = 8
HEAD_DIM = 64
FF = 2048
HALF = 256
SEQ = 256
ROWS = 16


def draw_lengths(key, part):
    counts = jax.random.randint(key, (ROWS,), SEQ // 8, SEQ + 1, dtype=jnp.int32)
    return counts.at[0].set(SEQ)


def draw_cotangent(key, part):
    offset_key = jax.random.fold_in(key, 11)
    noise_key = jax.random.fold_in(key, 12)
    offset = jax.random.uniform(offset_key, (D,), jnp.float32, -1.0, 1.0)
    noise = jax.random.normal(noise_key, (ROWS, SEQ, D), jnp.float32)
    return jnp.clip(noise + offset, -6.0, 6.0).astype(jnp.bfloat16)


def level_of(key, dims, pieces, low, high):
    def one(axis_at, shards_of):
        steps = jax.random.uniform(jax.random.fold_in(jax.random.fold_in(key, 6), axis_at), (shards_of,), jnp.float32, low / len(pieces), high / len(pieces))
        return jnp.repeat(jnp.exp(steps), dims[axis_at] // shards_of).reshape((-1,) + (1,) * (len(dims) - axis_at - 1))

    level = one(*pieces[0])
    for cut in pieces[1:]:
        level = level * one(*cut)
    return level


def normal_values(own_key, shape, width, bound, split=(), held_as=jnp.bfloat16):
    values = jax.random.normal(own_key, shape, jnp.float32) * width
    if len(split) > 0:
        values = level_of(own_key, shape, split, -0.22, 0.18) * values
    return jnp.clip(values, min=-bound, max=bound).astype(held_as)


def setup_inputs(seed: int = 0) -> dict:
    splits = jax.random.split(jax.random.key(seed), 23)
    return {
        "tokens": normal_values(splits[0], (ROWS, SEQ, D), 1.0, 6.0, ((0, 16), (1, 2))),
        "lengths": draw_lengths(jax.random.fold_in(splits[22], 71), 0),
        "cotangent": draw_cotangent(jax.random.fold_in(splits[22], 71), 0),
        "glu_weight": normal_values(splits[3], (D, 2 * D), D ** -0.5, 0.25),
        "glu_bias": normal_values(splits[4], (2 * D,), 0.3, 1.75),
        "norm_gain": jnp.clip(1.0 + 0.15 * jax.random.normal(splits[5], (4, D), jnp.float32), 0.25, 1.75).astype(jnp.bfloat16),
        "norm_bias": normal_values(splits[6], (4, D), 0.3, 1.75),
        "mid_gain": jnp.clip(1.0 + 0.15 * jax.random.normal(splits[7], (FF,), jnp.float32), 0.25, 1.75).astype(jnp.bfloat16),
        "mid_bias": normal_values(splits[8], (FF,), 0.3, 1.75),
        "left_weight": normal_values(splits[9], (D, FF), D ** -0.5, 0.25),
        "left_bias": normal_values(splits[10], (FF,), 0.3, 1.75),
        "conv_weight": normal_values(splits[11], (3, D, HALF), (3 * D) ** -0.5, 0.15625),
        "conv_bias": normal_values(splits[12], (HALF,), 0.3, 1.75),
        "depth_weight": normal_values(splits[13], (9, FF), 9 ** -0.5, 2.0),
        "point_weight": normal_values(splits[14], (FF, HALF), FF ** -0.5, 0.125),
        "point_bias": normal_values(splits[15], (HALF,), 0.3, 1.75),
        "qkv_weight": normal_values(splits[16], (D, 3 * D), (D // 2) ** -0.5, 0.375),
        "out_weight": normal_values(splits[17], (D, D), (D // 16) ** -0.5, 1.0),
        "ffn_in_weight": normal_values(splits[18], (D, FF), D ** -0.5, 0.25),
        "ffn_in_bias": normal_values(splits[19], (FF,), 0.3, 1.75),
        "ffn_out_weight": normal_values(splits[20], (FF, D), FF ** -0.5, 0.125),
        "ffn_out_bias": normal_values(splits[21], (D,), 0.3, 1.75),
    }


EPSILON = 1e-06
HIGHEST = lax.Precision.HIGHEST

@jax.custom_vjp
def low(v):
    return lax.optimization_barrier(v.astype(jnp.bfloat16)).astype(jnp.float32)

@jax.custom_vjp
def low_back(v):
    return v

def low_keep(v):
    return (low(v), None)

def low_pass(kept, grad):
    return (grad,)

def back_keep(v):
    return (v, None)

def back_low(kept, grad):
    return (low(grad),)
low.defvjp(low_keep, low_pass)
low_back.defvjp(back_keep, back_low)

def layer_norm(inputs, gain_vec, bias_vec):
    average = lax.optimization_barrier(jnp.mean(inputs, axis=-1, keepdims=True))
    centred = inputs - average
    spread = lax.optimization_barrier(jnp.mean(centred * centred, axis=-1, keepdims=True))
    return centred * lax.rsqrt(spread + EPSILON) * gain_vec + bias_vec

def shifted(inputs, offset):
    length = inputs.shape[1]
    if offset == 0:
        return inputs
    padding = jnp.zeros_like(inputs[:, :abs(offset)])
    if offset > 0:
        return jnp.concatenate([inputs[:, offset:], padding], axis=1)
    return jnp.concatenate([padding, inputs[:, :length + offset]], axis=1)

def dense(inputs, weight):
    return jnp.einsum('btd,de->bte', inputs, weight, precision=HIGHEST)

def rectify(inputs):
    return jnp.where(inputs > 0.0, inputs, 0.0)

def softmax_rows(scores):
    largest = lax.optimization_barrier(jnp.max(scores, axis=-1, keepdims=True))
    raised = jnp.exp(scores - largest)
    return raised / lax.optimization_barrier(jnp.sum(raised, axis=-1, keepdims=True))

def forward(stream_in, params, valid_mask, keys_open):
    glu_weight, glu_bias, norm_gain, norm_bias, mid_gain, mid_bias, left_weight, left_bias, conv_weight, conv_bias, depth_weight, point_weight, point_bias, qkv_weight, out_weight, ffn_in_weight, ffn_in_bias, ffn_out_weight, ffn_out_bias = params
    batch_rows = stream_in.shape[0]
    columns = valid_mask[:, :, None]
    first_norm = low(layer_norm(stream_in, norm_gain[0], norm_bias[0]))
    joined = low_back(dense(first_norm, glu_weight) + glu_bias)
    after_glu = stream_in + joined[..., :D] * jax.nn.sigmoid(joined[..., D:])
    second_norm = low(layer_norm(after_glu, norm_gain[1], norm_bias[1]) * columns)
    left_branch = rectify(low_back(dense(second_norm, left_weight) + left_bias))
    window = jnp.concatenate([shifted(second_norm, -1), second_norm, shifted(second_norm, 1)], axis=-1)
    right_branch = rectify(low_back(dense(window, conv_weight.reshape(3 * D, HALF)) + conv_bias))
    combined = left_branch + jnp.pad(right_branch, ((0, 0), (0, 0), (0, FF - HALF)))
    third_norm = layer_norm(combined, mid_gain, mid_bias) * columns
    depthwise = shifted(third_norm, -4) * depth_weight[0]
    for offset in range(1, 9):
        depthwise = depthwise + shifted(third_norm, offset - 4) * depth_weight[offset]
    separable = low_back(dense(low(depthwise), point_weight) + point_bias)
    after_conv = after_glu + jnp.pad(separable, ((0, 0), (0, 0), (0, D - HALF)))
    fourth_norm = low(layer_norm(after_conv, norm_gain[2], norm_bias[2]))
    packed = low(low_back(dense(fourth_norm, qkv_weight)))
    shaped = packed.reshape(batch_rows, SEQ, 3, HEADS, HEAD_DIM)
    scores = jnp.einsum('bqhd,bkhd->bhqk', shaped[:, :, 0], shaped[:, :, 1], precision=HIGHEST) * HEAD_DIM ** (-0.5)
    scores = low_back(jnp.where(keys_open[:, None, None, :], scores, -1000000000.0))
    context = jnp.einsum('bhqk,bkhd->bqhd', low(softmax_rows(scores)), shaped[:, :, 2], precision=HIGHEST)
    context = low(low_back(context.reshape(batch_rows, SEQ, D)))
    after_attn = after_conv + low_back(dense(context, out_weight))
    fifth_norm = low(layer_norm(after_attn, norm_gain[3], norm_bias[3]))
    hidden = low(rectify(low_back(dense(fifth_norm, ffn_in_weight) + ffn_in_bias)))
    return after_attn + low_back(dense(hidden, ffn_out_weight) + ffn_out_bias)

def reference(tokens, lengths, cotangent, glu_weight, glu_bias, norm_gain, norm_bias, mid_gain, mid_bias, left_weight, left_bias, conv_weight, conv_bias, depth_weight, point_weight, point_bias, qkv_weight, out_weight, ffn_in_weight, ffn_in_bias, ffn_out_weight, ffn_out_bias):
    params = tuple((member.astype(jnp.float32) for member in (glu_weight, glu_bias, norm_gain, norm_bias, mid_gain, mid_bias, left_weight, left_bias, conv_weight, conv_bias, depth_weight, point_weight, point_bias, qkv_weight, out_weight, ffn_in_weight, ffn_in_bias, ffn_out_weight, ffn_out_bias)))
    group_rows = 16
    blocks = ROWS // group_rows
    streams = tokens.astype(jnp.float32).reshape(blocks, group_rows, SEQ, D)
    cotans = cotangent.astype(jnp.float32).reshape(blocks, group_rows, SEQ, D)
    counts = lengths.reshape(blocks, group_rows)
    positions = jnp.arange(SEQ, dtype=jnp.int32)

    def advance(carried, batch_in):
        stream_part, cotan_part, count_part = batch_in
        keys_open = positions[None, :] < count_part[:, None]
        valid_mask = keys_open.astype(jnp.float32)
        output, pullback = jax.vjp(lambda inputs, weights: forward(inputs, weights, valid_mask, keys_open), stream_part, params)
        grad_in, grad_params = pullback(cotan_part)
        carried = jax.tree.map(jnp.add, carried, grad_params)
        return (carried, (output.astype(jnp.bfloat16), grad_in))
    start_sums = jax.tree.map(jnp.zeros_like, params)
    grad_sums, (outputs, grads_in) = lax.scan(advance, start_sums, (streams, cotans, counts))
    return (outputs.reshape(ROWS, SEQ, D), grads_in.reshape(ROWS, SEQ, D), grad_sums[0], grad_sums[1], grad_sums[2], grad_sums[3], grad_sums[4], grad_sums[5], grad_sums[6], grad_sums[7], grad_sums[8], grad_sums[9], grad_sums[10], grad_sums[11], grad_sums[12], grad_sums[13], grad_sums[14], grad_sums[15], grad_sums[16], grad_sums[17], grad_sums[18])
```

```python
import jax
import jax.numpy as jnp
from jax import lax
from jax.sharding import PartitionSpec as P

HEAD_DIM = 64


EPSILON = 1e-06


def layer_norm(inputs, gain_vec, bias_vec):
    average = jnp.mean(inputs, axis=-1, keepdims=True)
    centred = inputs - average
    spread = jnp.mean(centred * centred, axis=-1, keepdims=True)
    return centred * lax.rsqrt(spread + EPSILON) * gain_vec + bias_vec


def project(inputs, weight):
    return jnp.dot(inputs, weight, preferred_element_type=jnp.float32)


def project_back(incoming, weight):
    return jnp.einsum("te,de->td", incoming, weight, preferred_element_type=jnp.float32)


def weight_grad(inputs, incoming):
    return jnp.einsum("td,te->de", inputs, incoming, preferred_element_type=jnp.float32).astype(
        jnp.bfloat16
    )


def token_sum(incoming):
    return jnp.sum(incoming.astype(jnp.float32), axis=0)


def norm_back(inputs, gain_vec, bias_vec, incoming):
    unused, pullback = jax.vjp(layer_norm, inputs, gain_vec, bias_vec)
    return pullback(incoming)


def shifted(cells, offset):
    if offset == 0:
        return cells
    blank = jnp.zeros_like(cells[: abs(offset)])
    if offset > 0:
        return jnp.concatenate([cells[offset:], blank], axis=0)
    return jnp.concatenate([blank, cells[:offset]], axis=0)


def per_device(
    tokens,
    lengths,
    cotangent,
    glu_weight,
    glu_bias,
    norm_gain,
    norm_bias,
    mid_gain,
    mid_bias,
    left_weight,
    left_bias,
    conv_weight,
    conv_bias,
    depth_weight,
    point_weight,
    point_bias,
    qkv_weight,
    out_weight,
    ffn_in_weight,
    ffn_in_bias,
    ffn_out_weight,
    ffn_out_bias,
):
    row_count, part_len, width = tokens.shape
    assert row_count == 1 and lax.axis_size("head") == 2
    seq_len = part_len * 2
    shards = lax.axis_size("dp")
    heads = width // HEAD_DIM
    half_width = conv_weight.shape[2]
    ffn_width = left_weight.shape[1]
    scale = HEAD_DIM ** (-0.5)
    side = lax.axis_index("head")
    swap = [(0, 1), (1, 0)]
    bf16 = jnp.bfloat16

    def whole_row(part):
        other = lax.ppermute(part, "head", swap)
        return jnp.where(
            side == 0,
            jnp.concatenate([part, other], axis=0),
            jnp.concatenate([other, part], axis=0),
        )

    def own_tokens(full):
        return lax.dynamic_slice_in_dim(full, side * part_len, part_len, axis=0)[None]

    def own_columns(full):
        count = full.shape[1] // 2
        return lax.dynamic_slice_in_dim(full, side * count, count, axis=1)

    tokens = whole_row(tokens[0])
    cotangent = whole_row(cotangent[0])
    keys_valid = jnp.arange(seq_len, dtype=jnp.int32) < lengths[0]
    columns = keys_valid.astype(jnp.float32)[:, None]
    keys_open = keys_valid[None, None, :]
    gains = norm_gain.astype(jnp.float32)
    shifts = norm_bias.astype(jnp.float32)
    mid_gains = mid_gain.astype(jnp.float32)
    mid_shifts = mid_bias.astype(jnp.float32)
    taps = depth_weight.astype(jnp.float32)
    conv_flat = conv_weight.reshape(3 * width, half_width)
    stream_in = tokens.astype(jnp.float32)
    first_norm = layer_norm(stream_in, gains[0], shifts[0]).astype(bf16)
    joined = project(first_norm, glu_weight) + glu_bias.astype(jnp.float32)
    values_part = joined[..., :width]
    gate_part = jax.nn.sigmoid(joined[..., width:])
    after_glu = stream_in + values_part * gate_part
    second_norm = (layer_norm(after_glu, gains[1], shifts[1]) * columns).astype(bf16)
    left_pre = project(second_norm, left_weight) + left_bias.astype(jnp.float32)
    window = jnp.concatenate([shifted(second_norm, -1), second_norm, shifted(second_norm, 1)], axis=-1)
    right_pre = project(window, conv_flat) + conv_bias.astype(jnp.float32)
    combined = jnp.where(left_pre > 0.0, left_pre, 0.0) + jnp.pad(
        jnp.where(right_pre > 0.0, right_pre, 0.0), ((0, 0), (0, ffn_width - half_width))
    )
    third_norm = layer_norm(combined, mid_gains, mid_shifts) * columns
    depthwise = shifted(third_norm, -4) * taps[0]
    for offset in range(1, 9):
        depthwise = depthwise + shifted(third_norm, offset - 4) * taps[offset]
    depth_low = depthwise.astype(bf16)
    separable = project(depth_low, point_weight) + point_bias.astype(jnp.float32)
    after_conv = after_glu + jnp.pad(separable, ((0, 0), (0, width - half_width)))
    fourth_norm = layer_norm(after_conv, gains[2], shifts[2]).astype(bf16)
    packed = project(fourth_norm, qkv_weight).astype(bf16)
    shaped = packed.reshape(seq_len, 3, heads, HEAD_DIM)
    queries = shaped[:, 0]
    keyset = shaped[:, 1]
    valueset = shaped[:, 2]
    scores = jnp.einsum("qhd,khd->hqk", queries, keyset, preferred_element_type=jnp.float32) * scale
    scores = jnp.where(keys_open, scores, -1000000000.0)
    largest = jnp.max(scores, axis=-1, keepdims=True)
    raised = jnp.exp(scores - largest)
    probs = raised / jnp.sum(raised, axis=-1, keepdims=True)
    probs_low = probs.astype(bf16)
    context = jnp.einsum("hqk,khd->qhd", probs_low, valueset, preferred_element_type=jnp.float32)
    context = context.astype(bf16).reshape(seq_len, width)
    after_attn = after_conv + project(context, out_weight)
    fifth_norm = layer_norm(after_attn, gains[3], shifts[3]).astype(bf16)
    hidden_pre = project(fifth_norm, ffn_in_weight) + ffn_in_bias.astype(jnp.float32)
    hidden = jnp.where(hidden_pre > 0.0, hidden_pre, 0.0).astype(bf16)
    block_out = own_tokens(after_attn) + project(own_tokens(hidden)[0], ffn_out_weight)[None] + ffn_out_bias.astype(jnp.float32)

    grad_stream = cotangent.astype(jnp.float32)
    g_ffn_out = weight_grad(hidden, own_columns(cotangent))
    g_ffn_out_bias = token_sum(cotangent)
    d_hidden = jnp.where(hidden_pre > 0.0, project_back(cotangent, ffn_out_weight), 0.0).astype(bf16)
    g_ffn_in = weight_grad(fifth_norm, own_columns(d_hidden))
    g_ffn_in_bias = token_sum(d_hidden)
    d_fifth, gain_three, shift_three = norm_back(
        after_attn, gains[3], shifts[3], project_back(d_hidden, ffn_in_weight)
    )
    d_after_attn = grad_stream + d_fifth
    d_attn = d_after_attn.astype(bf16)
    g_out = weight_grad(context, own_columns(d_attn))
    d_context = project_back(d_attn, out_weight).astype(bf16).reshape(seq_len, heads, HEAD_DIM)
    d_values = jnp.einsum("hqk,qhd->khd", probs_low, d_context, preferred_element_type=jnp.float32)
    d_probs = jnp.einsum("qhd,khd->hqk", d_context, valueset, preferred_element_type=jnp.float32)
    delta = jnp.sum(d_probs * probs, axis=-1, keepdims=True)
    d_scores = (probs * (d_probs - delta)).astype(bf16)
    d_queries = jnp.einsum("hqk,khd->qhd", d_scores, keyset, preferred_element_type=jnp.float32) * scale
    d_keys = jnp.einsum("hqk,qhd->khd", d_scores, queries, preferred_element_type=jnp.float32) * scale
    d_packed = jnp.stack([d_queries, d_keys, d_values], axis=1).astype(bf16)
    d_packed = d_packed.reshape(seq_len, 3 * width)
    g_qkv = weight_grad(fourth_norm, own_columns(d_packed))
    d_fourth, gain_two, shift_two = norm_back(
        after_conv, gains[2], shifts[2], project_back(d_packed, qkv_weight)
    )
    d_after_conv = d_after_attn + d_fourth
    d_sep = d_after_conv[..., :half_width].astype(bf16)
    g_point = weight_grad(depth_low, own_columns(d_sep))
    g_point_bias = token_sum(d_sep)
    d_depth = project_back(d_sep, point_weight)
    g_depth = []
    d_third = None
    for offset in range(9):
        moved = shifted(d_depth, 4 - offset)
        g_depth.append(jnp.sum(moved * third_norm, axis=0))
        term = moved * taps[offset]
        d_third = term if d_third is None else d_third + term
    g_depth = jnp.stack(g_depth)
    d_third = d_third * columns
    d_combined, g_mid_gain, g_mid_bias = norm_back(combined, mid_gains, mid_shifts, d_third)
    d_left = jnp.where(left_pre > 0.0, d_combined, 0.0).astype(bf16)
    d_right = jnp.where(right_pre > 0.0, d_combined[..., :half_width], 0.0).astype(bf16)
    g_left = weight_grad(second_norm, own_columns(d_left))
    g_left_bias = token_sum(d_left)
    g_conv = weight_grad(window, own_columns(d_right))
    g_conv_bias = token_sum(d_right)
    d_window = project_back(d_right, conv_flat)
    d_second = project_back(d_left, left_weight) + d_window[..., width : 2 * width]
    d_second = d_second + shifted(d_window[..., :width], 1) + shifted(d_window[..., 2 * width :], -1)
    d_second = d_second * columns
    d_norm_one, gain_one, shift_one = norm_back(after_glu, gains[1], shifts[1], d_second)
    d_after_glu = d_after_conv + d_norm_one
    d_values_part = d_after_glu * gate_part
    d_gate_part = d_after_glu * values_part * gate_part * (1.0 - gate_part)
    d_joined = jnp.concatenate([d_values_part, d_gate_part], axis=-1).astype(bf16)
    g_glu = weight_grad(first_norm, own_columns(d_joined))
    g_glu_bias = token_sum(d_joined)
    d_norm_zero, gain_zero, shift_zero = norm_back(
        stream_in, gains[0], shifts[0], project_back(d_joined, glu_weight)
    )
    grad_input = own_tokens(d_after_glu + d_norm_zero)
    g_gains = jnp.stack([gain_zero, gain_one, gain_two, gain_three])
    g_shifts = jnp.stack([shift_zero, shift_one, shift_two, shift_three])

    lanes = 128

    def by_rows(grad):
        return grad.reshape(shards, -1, lanes)

    def by_columns(grad):
        return jnp.moveaxis(grad.reshape(-1, shards, grad.shape[-1] // shards), 1, 0).reshape(shards, -1)

    large = [
        by_rows(g_ffn_out),
        by_rows(g_ffn_in),
        by_rows(g_out),
        by_rows(g_qkv),
        by_rows(g_point),
        by_rows(g_left),
        jnp.moveaxis(g_conv.reshape(3, shards, width // shards, half_width // 2), 1, 0).reshape(
            shards, -1, lanes
        ),
        by_rows(g_glu),
    ]
    small = [
        by_columns(g[None] if g.ndim == 1 else g)
        for g in (
            g_glu_bias,
            g_gains,
            g_shifts,
            g_mid_gain,
            g_mid_bias,
            g_left_bias,
            g_depth,
            g_ffn_in_bias,
            g_ffn_out_bias,
        )
    ] + [
        jnp.broadcast_to(g[None], (shards, half_width)) for g in (g_conv_bias, g_point_bias)
    ]
    small_sizes = [s.shape[1] for s in small]
    small = jnp.concatenate(small, axis=1).astype(bf16)
    filler = -small.shape[1] % (16 * lanes)
    small = jnp.pad(small, ((0, 0), (0, filler))).reshape(shards, -1, lanes)
    buffer = jnp.concatenate(large + [small], axis=1)
    total = lax.psum_scatter(buffer, "dp", scatter_dimension=0, tiled=True)[0]
    large_rows = sum(g.shape[1] for g in large)
    mine = total[:large_rows]
    theirs = lax.ppermute(mine, "head", swap)
    lefts = jnp.where(side == 0, mine, theirs).astype(jnp.float32)
    rights = jnp.where(side == 0, theirs, mine).astype(jnp.float32)
    joined_up = []
    start = 0
    for grad, shape in zip(
        large,
        (
            (ffn_width // shards, width // 2),
            (width // shards, ffn_width // 2),
            (width // shards, width // 2),
            (width // shards, 3 * width // 2),
            (ffn_width // shards, half_width // 2),
            (width // shards, ffn_width // 2),
            (3, width // shards, half_width // 2),
            (width // shards, width),
        ),
    ):
        stop = start + grad.shape[1]
        joined_up.append(
            jnp.concatenate([lefts[start:stop].reshape(shape), rights[start:stop].reshape(shape)], axis=-1)
        )
        start = stop
    ffn_out, ffn_in, out, qkv, point, left, conv, glu = joined_up
    flat = total[large_rows:].reshape(-1).astype(jnp.float32)
    pieces = []
    start = 0
    for size in small_sizes:
        pieces.append(flat[start : start + size])
        start += size
    (
        s_glu_bias,
        s_gains,
        s_shifts,
        s_mid_gain,
        s_mid_bias,
        s_left_bias,
        s_depth,
        s_ffn_in_bias,
        s_ffn_out_bias,
        s_conv_bias,
        s_point_bias,
    ) = pieces
    return (
        block_out.astype(bf16),
        grad_input,
        glu,
        s_glu_bias,
        s_gains.reshape(4, -1),
        s_shifts.reshape(4, -1),
        s_mid_gain,
        s_mid_bias,
        left,
        s_left_bias,
        conv,
        s_conv_bias,
        s_depth.reshape(9, -1),
        point,
        s_point_bias,
        qkv,
        out,
        ffn_in,
        s_ffn_in_bias,
        ffn_out,
        s_ffn_out_bias,
    )


def solution(mesh):
    return jax.shard_map(
        per_device,
        mesh=mesh,
        in_specs=(P("dp", "head", None), P("dp"), P("dp", "head", None)) + (P(),) * 19,
        out_specs=(
            P("dp", "head", None),
            P("dp", "head", None),
            P("dp", None),
            P("dp"),
            P(None, "dp"),
            P(None, "dp"),
            P("dp"),
            P("dp"),
            P("dp", None),
            P("dp"),
            P(None, "dp", None),
            P(),
            P(None, "dp"),
            P("dp", None),
            P(),
            P("dp", None),
            P("dp", None),
            P("dp", None),
            P("dp"),
            P("dp", None),
            P("dp"),
        ),
        check_vma=False,
    )
```

```python
import functools

import jax
import jax.numpy as jnp
from jax import lax
from jax.experimental import pallas as pl
from jax.experimental.pallas import tpu as pltpu
from jax.sharding import PartitionSpec as P

HEAD_DIM = 64
EPSILON = 1e-06
LANES = 128
TILE = 256
GROUPS = 16
F32 = jnp.float32
BF16 = jnp.bfloat16
VMEM_BYTES = 50 * 1024 * 1024


def mm(a, b):
    return lax.dot_general(a, b, (((1,), (0,)), ((), ())), preferred_element_type=F32)


def mm_nt(a, b):
    return lax.dot_general(a, b, (((1,), (1,)), ((), ())), preferred_element_type=F32)


def mm_tn(a, b):
    return lax.dot_general(a, b, (((0,), (0,)), ((), ())), preferred_element_type=F32)


def mean(v):
    return jnp.mean(v, axis=-1, keepdims=True)


def normalized(v):
    centred = v - mean(v)
    rate = lax.rsqrt(mean(centred * centred) + EPSILON)
    return centred * rate, rate


def norm_back(vhat, rate, gained):
    return (gained - mean(gained) - vhat * mean(gained * vhat)) * rate


def sum_tokens(v):
    return jnp.sum(v, axis=0, keepdims=True)


def row_blocks(total, step, body, carry=0):
    def visit(i, c):
        return body(pl.multiple_of(i * step, step), c)

    return lax.fori_loop(0, total // step, visit, carry)


def valid_rows(start, count, length):
    places = start + lax.broadcasted_iota(jnp.int32, (count, 1), 0)
    return (places < length).astype(F32)


def col(n, width=TILE):
    return slice(n * width, (n + 1) * width)


def place_rows(meta, grad, keep, send, at, rows):
    def visit(p, c):
        for slot, out in ((2, keep), (2 + GROUPS // 2, send)):
            block = meta[slot + p]
            out[p, at : at + rows, :] = grad[
                pl.ds(pl.multiple_of(block * rows, rows), rows), :
            ].astype(BF16)
        return c

    lax.fori_loop(0, GROUPS // 2, visit, 0)


def for_slots(meta, keep, send, body):
    def visit(p, c):
        for slot, out in ((2, keep), (2 + GROUPS // 2, send)):
            body(p, meta[slot + p], out)
        return c

    lax.fori_loop(0, GROUPS // 2, visit, 0)


def forward_kernel(
    meta,
    mine,
    other,
    cot_mine,
    cot_other,
    vec,
    gains,
    shifts,
    depth_w,
    glu_w,
    left_w,
    conv_w,
    point_w,
    qkv_w,
    out_w,
    ffn_in_w,
    ffn_out_w,
    out_tokens,
    stream,
    first,
    joined,
    after_glu,
    second,
    left_pre,
    right_pre,
    depth_low,
    after_conv,
    fourth,
    packed,
    probs,
    context,
    d_after,
    small,
    keep,
    send,
    third,
    sides,
    after_attn,
    fifth,
    hidden,
    cot,
    d_hidden,
    d_fifth,
    grad,
):
    part, width = mine.shape
    seq = 2 * part
    ffn = left_w.shape[1]
    half = conv_w.shape[2]
    side = meta[0]
    length = meta[1]
    own = pl.ds(pl.multiple_of(side * part, part), part)
    opposite = pl.ds(pl.multiple_of((1 - side) * part, part), part)
    stream[own, :] = mine[...]
    stream[opposite, :] = other[...]
    cot[own, :] = cot_mine[...]
    cot[opposite, :] = cot_other[...]
    gain = [gains[k : k + 1, :].astype(F32) for k in range(4)]
    shift = [shifts[k : k + 1, :].astype(F32) for k in range(4)]

    def first_rows(r, c):
        rows = pl.ds(r, 64)
        vhat, _ = normalized(stream[rows, :].astype(F32))
        first[rows, :] = (vhat * gain[0] + shift[0]).astype(BF16)
        return c

    row_blocks(seq, 64, first_rows)
    for n in range(2 * width // TILE):
        joined[:, col(n)] = mm(first[...], glu_w[:, col(n)]) + vec[4:5, col(n)]

    def glu_rows(r, c):
        rows = pl.ds(r, 32)
        gate = jax.nn.sigmoid(joined[rows, width:])
        joined[rows, width:] = gate
        v = stream[rows, :].astype(F32) + joined[rows, :width] * gate
        after_glu[rows, :] = v
        vhat, _ = normalized(v)
        second[rows, :] = ((vhat * gain[1] + shift[1]) * valid_rows(r, 32, length)).astype(BF16)
        return c

    row_blocks(seq, 32, glu_rows)
    blank = jnp.zeros((8, half), F32)
    for k in range(2):
        sides[k, 0:8, :] = blank
        sides[k, 8 + seq : 16 + seq, :] = blank
    sides[0, 8 : 8 + seq, :] = mm(second[...], conv_w[0])
    sides[1, 8 : 8 + seq, :] = mm(second[...], conv_w[2])
    right_pre[...] = mm(second[...], conv_w[1]) + vec[4:5, 2 * width : 2 * width + half]
    right_pre[...] = right_pre[...] + sides[0, 7 : 7 + seq, :] + sides[1, 9 : 9 + seq, :]
    for n in range(ffn // TILE):
        left_pre[:, col(n)] = mm(second[...], left_w[:, col(n)]) + vec[2:3, col(n)]
    chunks = ffn // LANES
    edge = jnp.zeros((8, LANES), F32)
    for k in range(chunks):
        third[k, 0:8, :] = edge
        third[k, 8 + seq : 16 + seq, :] = edge

    def mid_rows(r, c):
        rows = pl.ds(r, 16)
        vhat, _ = normalized(combine(left_pre[rows, :], right_pre[rows, :]))
        v = (vhat * vec[0:1, :] + vec[1:2, :]) * valid_rows(r, 16, length)
        for k in range(chunks):
            third[k, pl.ds(pl.multiple_of(8 + r, 8), 16), :] = v[:, col(k, LANES)]
        return c

    row_blocks(seq, 16, mid_rows)

    def depth_lanes(k, c):
        lanes = pl.ds(pl.multiple_of(k * LANES, LANES), LANES)
        taps = depth_w[:, lanes].astype(F32)
        total = third[k, 4 : 4 + seq, :] * taps[0:1, :]
        for j in range(1, 9):
            total = total + third[k, 4 + j : 4 + j + seq, :] * taps[j : j + 1, :]
        depth_low[:, lanes] = total.astype(BF16)
        return c

    lax.fori_loop(0, chunks, depth_lanes, 0)
    after_conv[:, :half] = (
        after_glu[:, :half] + mm(depth_low[...], point_w[...]) + vec[4:5, 2 * width + half : 2 * width + 2 * half]
    )
    after_conv[:, half:] = after_glu[:, half:]

    def fourth_rows(r, c):
        rows = pl.ds(r, 64)
        vhat, _ = normalized(after_conv[rows, :])
        fourth[rows, :] = (vhat * gain[2] + shift[2]).astype(BF16)
        return c

    row_blocks(seq, 64, fourth_rows)
    for n in range(3 * width // TILE):
        packed[:, col(n)] = mm(fourth[...], qkv_w[:, col(n)]).astype(BF16)

    low_lanes = lax.broadcasted_iota(jnp.int32, (1, LANES), 1) < HEAD_DIM
    scale = HEAD_DIM ** (-0.5)

    def head_pair(p, c):
        lanes = pl.ds(pl.multiple_of(p * LANES, LANES), LANES)
        q = packed[:, lanes].astype(F32)
        k = packed[:, pl.ds(pl.multiple_of(width + p * LANES, LANES), LANES)]
        v = packed[:, pl.ds(pl.multiple_of(2 * width + p * LANES, LANES), LANES)]
        open_keys = lax.broadcasted_iota(jnp.int32, (1, seq), 1) < length
        results = []
        for e in range(2):
            q_one = jnp.where(low_lanes if e == 0 else ~low_lanes, q, 0.0).astype(BF16)
            s = jnp.where(open_keys, mm_nt(q_one, k) * scale, -1000000000.0)
            raised = jnp.exp(s - jnp.max(s, axis=-1, keepdims=True))
            chance = raised / jnp.sum(raised, axis=-1, keepdims=True)
            probs[2 * p + e] = chance
            results.append(mm(chance.astype(BF16), v))
        context[:, lanes] = jnp.where(low_lanes, results[0], results[1]).astype(BF16)
        return c

    lax.fori_loop(0, width // LANES, head_pair, 0)
    for n in range(width // TILE):
        after_attn[:, col(n)] = after_conv[:, col(n)] + mm(context[...], out_w[:, col(n)])

    def fifth_rows(r, c):
        rows = pl.ds(r, 64)
        vhat, _ = normalized(after_attn[rows, :])
        fifth[rows, :] = (vhat * gain[3] + shift[3]).astype(BF16)
        return c

    row_blocks(seq, 64, fifth_rows)
    for n in range(ffn // TILE):
        pre = mm(fifth[...], ffn_in_w[:, col(n)]) + vec[3:4, col(n)]
        hidden[:, col(n)] = jnp.where(pre > 0.0, pre, 0.0).astype(BF16)
    for n in range(width // TILE):
        out_tokens[:, col(n)] = (
            after_attn[own, col(n)]
            + mm(hidden[own, :], ffn_out_w[:, col(n)])
            + vec[4:5, 3 * width + n * TILE : 3 * width + (n + 1) * TILE]
        ).astype(BF16)

    for n in range(ffn // TILE):
        back = mm_nt(cot[...], ffn_out_w[col(n), :])
        back = jnp.where(hidden[:, col(n)].astype(F32) > 0.0, back, 0.0).astype(BF16)
        d_hidden[:, col(n)] = back
        small[0:1, col(n)] = sum_tokens(back.astype(F32))
    for n in range(width // TILE):
        d_fifth[:, col(n)] = mm_nt(d_hidden[...], ffn_in_w[col(n), :])

    def fifth_back(r, c):
        g_gain, g_shift, g_out = c
        rows = pl.ds(r, 32)
        vhat, rate = normalized(after_attn[rows, :])
        e = d_fifth[rows, :]
        given = cot[rows, :].astype(F32)
        d_after[rows, :] = given + norm_back(vhat, rate, e * gain[3])
        return g_gain + sum_tokens(e * vhat), g_shift + sum_tokens(e), g_out + sum_tokens(given)

    nothing = jnp.zeros((1, width), F32)
    g_gain, g_shift, g_out = row_blocks(seq, 32, fifth_back, (nothing,) * 3)
    small[1:2, 0:width] = g_gain
    small[1:2, width : 2 * width] = g_shift
    small[1:2, 2 * width : 3 * width] = g_out

    cot_half = cot[:, pl.ds(pl.multiple_of(side * (width // 2), width // 2), width // 2)]
    per_row = ffn // GROUPS

    def ffn_out_slot(p, block, out):
        out[p, 0:per_row, :] = mm_tn(
            hidden[:, pl.ds(pl.multiple_of(block * per_row, per_row), per_row)], cot_half
        ).astype(BF16)

    for_slots(meta, keep, send, ffn_out_slot)
    rows = width // GROUPS
    for j in range(ffn // 2 // TILE):
        at = pl.multiple_of(side * (ffn // 2) + j * TILE, TILE)
        grad[...] = mm_tn(fifth[...], d_hidden[:, pl.ds(at, TILE)])
        place_rows(meta, grad, keep, send, per_row + j * rows, rows)


def combine(left_pre, right_pre):
    half = right_pre.shape[1]
    left = jnp.maximum(left_pre, 0.0)
    return jnp.concatenate([left[:, :half] + jnp.maximum(right_pre, 0.0), left[:, half:]], axis=1)


def attention_back_kernel(
    meta,
    gains,
    d_after,
    packed,
    probs,
    context,
    fourth,
    after_conv,
    depth_low,
    qkv_w,
    out_w,
    d_after_conv,
    small,
    keep,
    send,
    d_attn,
    d_context,
    d_packed,
    d_fourth,
    d_sep,
    grad,
):
    seq, width = d_after.shape
    side = meta[0]
    half = d_sep.shape[1]
    ffn = depth_low.shape[1]
    rows = width // GROUPS
    d_attn[...] = d_after[...].astype(BF16)
    for n in range(width // TILE):
        d_context[:, col(n)] = mm_nt(d_attn[...], out_w[col(n), :]).astype(BF16)
    low_lanes = lax.broadcasted_iota(jnp.int32, (1, LANES), 1) < HEAD_DIM
    scale = HEAD_DIM ** (-0.5)

    def head_pair(p, c):
        lanes = pl.ds(pl.multiple_of(p * LANES, LANES), LANES)
        k_lanes = pl.ds(pl.multiple_of(width + p * LANES, LANES), LANES)
        v_lanes = pl.ds(pl.multiple_of(2 * width + p * LANES, LANES), LANES)
        q = packed[:, lanes]
        k = packed[:, k_lanes]
        v = packed[:, v_lanes]
        given = d_context[:, lanes]
        wide = given.astype(F32)
        dq, dk, dv = [], [], []
        for e in range(2):
            one = jnp.where(low_lanes if e == 0 else ~low_lanes, wide, 0.0).astype(BF16)
            chance = probs[2 * p + e]
            d_probs = mm_nt(one, v)
            delta = jnp.sum(d_probs * chance, axis=-1, keepdims=True)
            d_scores = (chance * (d_probs - delta)).astype(BF16)
            dv.append(mm_tn(chance.astype(BF16), given))
            dq.append(mm(d_scores, k))
            dk.append(mm_tn(d_scores, q))
        d_packed[:, lanes] = (jnp.where(low_lanes, dq[0], dq[1]) * scale).astype(BF16)
        d_packed[:, k_lanes] = (jnp.where(low_lanes, dk[0], dk[1]) * scale).astype(BF16)
        d_packed[:, v_lanes] = jnp.where(low_lanes, dv[0], dv[1]).astype(BF16)
        return c

    lax.fori_loop(0, width // LANES, head_pair, 0)
    for n in range(width // TILE):
        d_fourth[:, col(n)] = mm_nt(d_packed[...], qkv_w[col(n), :])
    gain = gains[2:3, :].astype(F32)

    def fourth_back(r, c):
        g_gain, g_shift, g_point = c
        block = pl.ds(r, 32)
        vhat, rate = normalized(after_conv[block, :])
        e = d_fourth[block, :]
        total = d_after[block, :] + norm_back(vhat, rate, e * gain)
        d_after_conv[block, :] = total
        sep = total[:, :half].astype(BF16)
        d_sep[block, :] = sep
        return (
            g_gain + sum_tokens(e * vhat),
            g_shift + sum_tokens(e),
            g_point + sum_tokens(sep.astype(F32)),
        )

    nothing = jnp.zeros((1, width), F32)
    g_gain, g_shift, g_point = row_blocks(
        seq, 32, fourth_back, (nothing, nothing, jnp.zeros((1, half), F32))
    )
    small[0:1, 0:width] = g_gain
    small[0:1, width : 2 * width] = g_shift
    small[0:1, 2 * width : 2 * width + half] = g_point

    at = pl.multiple_of(side * (width // 2), width // 2)
    grad[...] = mm_tn(context[...], d_attn[:, pl.ds(at, width // 2)])
    place_rows(meta, grad, keep, send, 0, rows)
    for j in range(3 * width // 2 // TILE):
        at = pl.multiple_of(side * (3 * width // 2) + j * TILE, TILE)
        grad[...] = mm_tn(fourth[...], d_packed[:, pl.ds(at, TILE)])
        place_rows(meta, grad, keep, send, (1 + j) * rows, rows)
    sep_half = d_sep[:, pl.ds(pl.multiple_of(side * (half // 2), half // 2), half // 2)]
    per_row = ffn // GROUPS

    def point_slot(p, block, out):
        g = mm_tn(
            depth_low[:, pl.ds(pl.multiple_of(block * per_row, per_row), per_row)], sep_half
        ).astype(BF16)
        out[p, 4 * rows : 4 * rows + per_row // 2, 0:LANES] = g[: per_row // 2]
        out[p, 4 * rows : 4 * rows + per_row // 2, LANES : 2 * LANES] = g[per_row // 2 :]

    for_slots(meta, keep, send, point_slot)


def conv_back_kernel(
    meta,
    vec,
    depth_w,
    d_after_conv,
    left_pre,
    right_pre,
    second,
    point_w,
    left_w,
    conv_w,
    d_second,
    small,
    keep,
    send,
    vhat3,
    third,
    d_depth,
    d_third,
    rates,
    sums,
    d_left,
    d_right,
    taps_right,
    grad,
    grad_conv,
):
    seq, width = d_after_conv.shape
    ffn = left_pre.shape[1]
    half = right_pre.shape[1]
    side = meta[0]
    length = meta[1]
    chunks = ffn // LANES
    edge = jnp.zeros((8, LANES), F32)
    for k in range(chunks):
        d_depth[k, 0:8, :] = edge
        d_depth[k, 8 + seq : 16 + seq, :] = edge
    d_sep = d_after_conv[:, :half].astype(BF16)
    for n in range(ffn // TILE):
        block = mm_nt(d_sep, point_w[col(n), :])
        for m in range(TILE // LANES):
            d_depth[n * (TILE // LANES) + m, 8 : 8 + seq, :] = block[:, col(m, LANES)]

    def mid_rows(r, c):
        rows = pl.ds(r, 16)
        vhat, rate = normalized(combine(left_pre[rows, :], right_pre[rows, :]))
        v = (vhat * vec[0:1, :] + vec[1:2, :]) * valid_rows(r, 16, length)
        rates[rows, :] = jnp.broadcast_to(rate, (16, LANES))
        for k in range(chunks):
            third[k, rows, :] = v[:, col(k, LANES)]
            vhat3[k, rows, :] = vhat[:, col(k, LANES)]
        return c

    row_blocks(seq, 16, mid_rows)
    sums[...] = jnp.zeros(sums.shape, F32)
    valid = valid_rows(0, seq, length)

    def depth_lanes(k, c):
        lanes = pl.ds(pl.multiple_of(k * LANES, LANES), LANES)
        taps = depth_w[:, lanes].astype(F32)
        total = None
        here = third[k]
        for j in range(9):
            moved = d_depth[k, 12 - j : 12 - j + seq, :]
            small[j : j + 1, lanes] = sum_tokens(moved * here)
            term = moved * taps[j : j + 1, :]
            total = term if total is None else total + term
        total = total * valid
        vhat = vhat3[k]
        small[9:10, lanes] = sum_tokens(total * vhat)
        small[10:11, lanes] = sum_tokens(total)
        gained = total * vec[0:1, lanes]
        d_third[k] = gained
        sums[0] = sums[0] + gained
        sums[1] = sums[1] + gained * vhat
        return c

    lax.fori_loop(0, chunks, depth_lanes, 0)
    inverse = 1.0 / ffn
    sums[0] = jnp.broadcast_to(jnp.sum(sums[0], axis=-1, keepdims=True) * inverse, (seq, LANES))
    sums[1] = jnp.broadcast_to(jnp.sum(sums[1], axis=-1, keepdims=True) * inverse, (seq, LANES))

    def combined_lanes(k):
        return (d_third[k] - sums[0] - vhat3[k] * sums[1]) * rates[...]

    def left_lanes(k, c):
        lanes = pl.ds(pl.multiple_of(k * LANES, LANES), LANES)
        v = jnp.where(left_pre[:, lanes] > 0.0, combined_lanes(k), 0.0).astype(BF16)
        d_left[:, lanes] = v
        small[11:12, lanes] = sum_tokens(v.astype(F32))
        return c

    lax.fori_loop(0, chunks, left_lanes, 0)
    blank = jnp.zeros((8, half), F32)
    d_right[0:8, :] = blank
    d_right[8 + seq : 16 + seq, :] = blank
    for k in range(half // LANES):
        v = jnp.where(right_pre[:, col(k, LANES)] > 0.0, combined_lanes(k), 0.0).astype(BF16)
        v = v.astype(F32)
        d_right[8 : 8 + seq, col(k, LANES)] = v
        small[12:13, col(k, LANES)] = sum_tokens(v)
    taps_right[0] = d_right[9 : 9 + seq, :].astype(BF16)
    taps_right[1] = d_right[8 : 8 + seq, :].astype(BF16)
    taps_right[2] = d_right[7 : 7 + seq, :].astype(BF16)
    for n in range(width // TILE):
        total = mm_nt(d_left[...], left_w[col(n), :])
        for tap in range(3):
            total = total + mm_nt(taps_right[tap], conv_w[tap, col(n), :])
        d_second[:, col(n)] = total * valid

    rows = width // GROUPS
    for j in range(ffn // 2 // TILE):
        at = pl.multiple_of(side * (ffn // 2) + j * TILE, TILE)
        grad[...] = mm_tn(second[...], d_left[:, pl.ds(at, TILE)])
        place_rows(meta, grad, keep, send, j * rows, rows)
    start = ffn // 2 // TILE * rows
    half_lanes = pl.ds(pl.multiple_of(side * (half // 2), half // 2), half // 2)
    for tap in range(3):
        grad_conv[tap] = mm_tn(second[...], taps_right[tap, :, half_lanes])

    def conv_slot(p, block, out):
        at = pl.multiple_of(block * rows, rows)
        middle = pl.multiple_of(block * rows + rows // 2, rows // 2)
        h = rows // 2
        out[p, start : start + rows, 0:LANES] = grad_conv[0, pl.ds(at, rows), :].astype(BF16)
        out[p, start + rows : start + rows + h, 0:LANES] = grad_conv[1, pl.ds(at, h), :].astype(BF16)
        out[p, start : start + h, LANES : 2 * LANES] = grad_conv[1, pl.ds(middle, h), :].astype(BF16)
        out[p, start + h : start + h + rows, LANES : 2 * LANES] = grad_conv[
            2, pl.ds(at, rows), :
        ].astype(BF16)

    for_slots(meta, keep, send, conv_slot)


def glu_back_kernel(
    meta,
    gains,
    d_second,
    d_after_conv,
    after_glu,
    joined,
    first,
    stream,
    glu_w,
    small_ffn,
    small_attn,
    small_conv,
    grad_tokens,
    keep,
    send,
    d_joined,
    d_after_glu,
    d_first,
    rolled,
    blocks,
    grad,
):
    seq, width = d_second.shape
    part = seq // 2
    side = meta[0]
    gain = [gains[k : k + 1, :].astype(F32) for k in range(2)]

    def glu_rows(r, c):
        g_gain, g_shift, g_value, g_gate = c
        rows = pl.ds(r, 32)
        vhat, rate = normalized(after_glu[rows, :])
        e = d_second[rows, :]
        total = d_after_conv[rows, :] + norm_back(vhat, rate, e * gain[1])
        d_after_glu[rows, :] = total
        value = joined[rows, :width]
        gate = joined[rows, width:]
        d_value = (total * gate).astype(BF16)
        d_gate = (total * value * gate * (1.0 - gate)).astype(BF16)
        d_joined[rows, :width] = d_value
        d_joined[rows, width:] = d_gate
        return (
            g_gain + sum_tokens(e * vhat),
            g_shift + sum_tokens(e),
            g_value + sum_tokens(d_value.astype(F32)),
            g_gate + sum_tokens(d_gate.astype(F32)),
        )

    nothing = jnp.zeros((1, width), F32)
    gain_one, shift_one, g_value, g_gate = row_blocks(seq, 32, glu_rows, (nothing,) * 4)
    for n in range(width // TILE):
        d_first[:, col(n)] = mm_nt(d_joined[...], glu_w[col(n), :])

    def first_back(r, c):
        g_gain, g_shift = c
        rows = pl.ds(r, 32)
        vhat, rate = normalized(stream[rows, :].astype(F32))
        e = d_first[rows, :]
        d_after_glu[rows, :] = d_after_glu[rows, :] + norm_back(vhat, rate, e * gain[0])
        return g_gain + sum_tokens(e * vhat), g_shift + sum_tokens(e)

    gain_zero, shift_zero = row_blocks(seq, 32, first_back, (nothing,) * 2)
    grad_tokens[...] = d_after_glu[pl.ds(pl.multiple_of(side * part, part), part), :]

    rows = width // GROUPS
    for j in range(width // TILE):
        at = pl.multiple_of(side * width + j * TILE, TILE)
        grad[...] = mm_tn(first[...], d_joined[:, pl.ds(at, TILE)])
        place_rows(meta, grad, keep, send, j * rows, rows)

    blocks[...] = jnp.zeros(blocks.shape, F32)
    rolled[...] = jnp.zeros(rolled.shape, F32)
    vectors = (
        (gain_zero, gain_one, small_attn[0:1, 0:width], small_ffn[1:2, 0:width]),
        (shift_zero, shift_one, small_attn[0:1, width : 2 * width], small_ffn[1:2, width : 2 * width]),
    )
    tiles = width // LANES
    lane = lax.broadcasted_iota(jnp.int32, (8, LANES), 1)
    quarter = LANES // tiles
    for kind, four in enumerate(vectors):
        for k, vector in enumerate(four):
            for t in range(tiles):
                rolled[kind, 8 * k + t : 8 * k + t + 1, :] = vector[:, col(t, LANES)]
        for q in range(tiles):
            total = jnp.zeros((8, LANES), F32)
            for k in range(4):
                moved = pltpu.roll(rolled[kind, 8 * k : 8 * k + 8, :], (quarter * (k - q)) % LANES, 1)
                total = jnp.where((lane >= quarter * k) & (lane < quarter * (k + 1)), moved, total)
            for t in range(tiles):
                blocks[tiles * t + q, 13 + kind : 14 + kind, 0:LANES] = total[t : t + 1, :]
    lane = lane[0:1, :]
    g_out = small_ffn[1:2, 2 * width : 3 * width]
    for s in range(GROUPS):
        source = g_value if s < GROUPS // 2 else g_gate
        place = (s % (GROUPS // 2)) * (2 * width // GROUPS)
        block = source[:, place // LANES * LANES : place // LANES * LANES + LANES]
        glu_part = block if place % LANES == 0 else pltpu.roll(block, LANES - place % LANES, 1)
        place = s * (width // GROUPS)
        block = g_out[:, place // LANES * LANES : place // LANES * LANES + LANES]
        moved = (LANES // 2 - place % LANES) % LANES
        out_part = block if moved == 0 else pltpu.roll(block, moved, 1)
        blocks[s, 15:16, 0:LANES] = jnp.where(
            lane < LANES // 2, glu_part, jnp.where(lane < LANES // 2 + quarter, out_part, 0.0)
        )
        blocks[s, 0:12, 0:LANES] = small_conv[0:12, col(s, LANES)]
        blocks[s, 12:13, 0:LANES] = small_ffn[0:1, col(s, LANES)]
        for k in range(2):
            blocks[s, k : k + 1, LANES : 2 * LANES] = small_conv[12:13, col(k, LANES)]
            blocks[s, 2 + k : 3 + k, LANES : 2 * LANES] = small_attn[
                0:1, 2 * width + k * LANES : 2 * width + (k + 1) * LANES
            ]
    start = width // TILE * rows

    def small_slot(p, block, out):
        out[p, start : start + 16, :] = blocks[block].astype(BF16)

    for_slots(meta, keep, send, small_slot)


def finish_early_kernel(meta, mine_ffn, other_ffn, mine_attn, other_attn, ffn_out, ffn_in, out, qkv, point):
    side = meta[0]
    for who, ffn_grads, attn_grads in ((side, mine_ffn, mine_attn), (1 - side, other_ffn, other_attn)):
        per_row, width = ffn_out.shape
        rows = ffn_in.shape[0]
        at = pl.ds(pl.multiple_of(who * TILE, TILE), TILE)
        ffn_out[:, at] = ffn_grads[0:per_row, :].astype(F32)
        out[:, at] = attn_grads[0:rows, :].astype(F32)
        count = ffn_in.shape[1] // 2 // TILE
        for j in range(count):
            at = pl.ds(pl.multiple_of((who * count + j) * TILE, TILE), TILE)
            ffn_in[:, at] = ffn_grads[per_row + j * rows : per_row + (j + 1) * rows, :].astype(F32)
        count = qkv.shape[1] // 2 // TILE
        for j in range(count):
            at = pl.ds(pl.multiple_of((who * count + j) * TILE, TILE), TILE)
            qkv[:, at] = attn_grads[(1 + j) * rows : (2 + j) * rows, :].astype(F32)
        at = pl.ds(pl.multiple_of(who * LANES, LANES), LANES)
        start = 4 * rows
        point[0 : per_row // 2, at] = attn_grads[start : start + per_row // 2, 0:LANES].astype(F32)
        point[per_row // 2 :, at] = attn_grads[start : start + per_row // 2, LANES : 2 * LANES].astype(F32)


def finish_late_kernel(
    meta,
    mine_conv,
    other_conv,
    mine_glu,
    other_glu,
    left,
    conv,
    glu,
    gains,
    shifts,
    depth,
    vectors,
):
    side = meta[0]
    rows = left.shape[0]
    h = rows // 2
    for who, conv_grads, glu_grads in ((side, mine_conv, mine_glu), (1 - side, other_conv, other_glu)):
        count = left.shape[1] // 2 // TILE
        for j in range(count):
            at = pl.ds(pl.multiple_of((who * count + j) * TILE, TILE), TILE)
            left[:, at] = conv_grads[j * rows : (j + 1) * rows, :].astype(F32)
        start = count * rows
        at = pl.ds(pl.multiple_of(who * LANES, LANES), LANES)
        low = conv_grads[start : start + 3 * h, 0:LANES].astype(F32)
        high = conv_grads[start : start + 3 * h, LANES : 2 * LANES].astype(F32)
        conv[0, :, at] = low[0:rows]
        conv[1, 0:h, at] = low[rows:]
        conv[1, h:rows, at] = high[0:h]
        conv[2, :, at] = high[h:]
        count = glu.shape[1] // 2 // TILE
        for j in range(count):
            at = pl.ds(pl.multiple_of((who * count + j) * TILE, TILE), TILE)
            glu[:, at] = glu_grads[j * rows : (j + 1) * rows, :].astype(F32)
    start = glu.shape[1] // 2 // TILE * rows
    block = mine_glu[start : start + 16, :].astype(F32)
    depth[...] = block[0:9, 0:LANES]
    for k in range(4):
        gains[k : k + 1, :] = block[13:14, k * rows : (k + 1) * rows]
        shifts[k : k + 1, :] = block[14:15, k * rows : (k + 1) * rows]
    vectors[...] = block


def call(kernel, outs, scratch, *args):
    smem = pl.BlockSpec(memory_space=pltpu.SMEM)
    vmem = pl.BlockSpec(memory_space=pltpu.VMEM)
    return pl.pallas_call(
        kernel,
        out_shape=tuple(jax.ShapeDtypeStruct(shape, dtype) for shape, dtype in outs),
        in_specs=[smem] + [vmem] * (len(args) - 1),
        out_specs=(vmem,) * len(outs),
        scratch_shapes=[pltpu.VMEM(shape, dtype) for shape, dtype in scratch],
        compiler_params=pltpu.CompilerParams(vmem_limit_bytes=VMEM_BYTES),
        name=kernel.__name__,
    )(*args)


def per_device(
    tokens,
    lengths,
    cotangent,
    glu_weight,
    glu_bias,
    norm_gain,
    norm_bias,
    mid_gain,
    mid_bias,
    left_weight,
    left_bias,
    conv_weight,
    conv_bias,
    depth_weight,
    point_weight,
    point_bias,
    qkv_weight,
    out_weight,
    ffn_in_weight,
    ffn_in_bias,
    ffn_out_weight,
    ffn_out_bias,
):
    row_count, part, width = tokens.shape
    assert row_count == 1 and lax.axis_size("head") == 2
    seq = 2 * part
    shards = lax.axis_size("dp")
    below = shards // GROUPS
    assert below * GROUPS == shards
    heads = width // HEAD_DIM
    half = conv_weight.shape[2]
    ffn = left_weight.shape[1]
    side = lax.axis_index("head")
    group = lax.axis_index("dp") // below
    swap = [(0, 1), (1, 0)]
    slots = []
    for bit in (0, 1):
        for p in range(GROUPS // 2):
            slots.append(bit | ((p >> 2) & 1) << 1 | ((p >> 1) & 1) << 2 | (p & 1) << 3)
    meta = jnp.concatenate(
        [
            jnp.stack([side.astype(jnp.int32), lengths[0]]),
            group.astype(jnp.int32) ^ jnp.array(slots, jnp.int32),
        ]
    )

    mine = tokens[0]
    cot_mine = cotangent[0]
    other = lax.ppermute(mine, "head", swap)
    cot_other = lax.ppermute(cot_mine, "head", swap)
    vec = (
        jnp.concatenate(
            [mid_gain, mid_bias, left_bias, ffn_in_bias, glu_bias, conv_bias, point_bias, ffn_out_bias]
        )
        .astype(F32)
        .reshape(5, ffn)
    )

    def slot_outs(rows):
        return [((GROUPS // 2, rows, TILE), BF16)] * 2

    rows = width // GROUPS
    per_row = ffn // GROUPS
    ffn_rows = per_row + ffn // 2 // TILE * rows
    (
        out_tokens,
        stream,
        first,
        joined,
        after_glu,
        second,
        left_pre,
        right_pre,
        depth_low,
        after_conv,
        fourth,
        packed,
        probs,
        context,
        d_after,
        small_ffn,
        keep_ffn,
        send_ffn,
    ) = call(
        forward_kernel,
        [
            ((part, width), BF16),
            ((seq, width), BF16),
            ((seq, width), BF16),
            ((seq, 2 * width), F32),
            ((seq, width), F32),
            ((seq, width), BF16),
            ((seq, ffn), F32),
            ((seq, half), F32),
            ((seq, ffn), BF16),
            ((seq, width), F32),
            ((seq, width), BF16),
            ((seq, 3 * width), BF16),
            ((heads, seq, seq), F32),
            ((seq, width), BF16),
            ((seq, width), F32),
            ((8, ffn), F32),
        ]
        + slot_outs(ffn_rows),
        [
            ((ffn // LANES, seq + 16, LANES), F32),
            ((2, seq + 16, half), F32),
            ((seq, width), F32),
            ((seq, width), BF16),
            ((seq, ffn), BF16),
            ((seq, width), BF16),
            ((seq, ffn), BF16),
            ((seq, width), F32),
            ((width, TILE), F32),
        ],
        meta,
        mine,
        other,
        cot_mine,
        cot_other,
        vec,
        norm_gain,
        norm_bias,
        depth_weight,
        glu_weight,
        left_weight,
        conv_weight,
        point_weight,
        qkv_weight,
        out_weight,
        ffn_in_weight,
        ffn_out_weight,
    )
    d_after_conv, small_attn, keep_attn, send_attn = call(
        attention_back_kernel,
        [((seq, width), F32), ((8, ffn), F32)] + slot_outs(4 * rows + per_row // 2),
        [
            ((seq, width), BF16),
            ((seq, width), BF16),
            ((seq, 3 * width), BF16),
            ((seq, width), F32),
            ((seq, half), BF16),
            ((width, TILE), F32),
        ],
        meta,
        norm_gain,
        d_after,
        packed,
        probs,
        context,
        fourth,
        after_conv,
        depth_low,
        qkv_weight,
        out_weight,
    )
    d_second, small_conv, keep_conv, send_conv = call(
        conv_back_kernel,
        [((seq, width), F32), ((16, ffn), F32)] + slot_outs(ffn // 2 // TILE * rows + 3 * rows // 2),
        [
            ((ffn // LANES, seq, LANES), F32),
            ((ffn // LANES, seq, LANES), F32),
            ((ffn // LANES, seq + 16, LANES), F32),
            ((ffn // LANES, seq, LANES), F32),
            ((seq, LANES), F32),
            ((2, seq, LANES), F32),
            ((seq, ffn), BF16),
            ((seq + 16, half), F32),
            ((3, seq, half), BF16),
            ((width, TILE), F32),
            ((3, width, LANES), F32),
        ],
        meta,
        vec,
        depth_weight,
        d_after_conv,
        left_pre,
        right_pre,
        second,
        point_weight,
        left_weight,
        conv_weight,
    )
    grad_tokens, keep_glu, send_glu = call(
        glu_back_kernel,
        [((part, width), F32)] + slot_outs(width // TILE * rows + 16),
        [
            ((seq, 2 * width), BF16),
            ((seq, width), F32),
            ((seq, width), F32),
            ((2, 32, LANES), F32),
            ((GROUPS, 16, 2 * LANES), F32),
            ((width, TILE), F32),
        ],
        meta,
        norm_gain,
        d_second,
        d_after_conv,
        after_glu,
        joined,
        first,
        stream,
        glu_weight,
        small_ffn,
        small_attn,
        small_conv,
    )

    def reduced(keep, send):
        count = GROUPS // 2
        for bit in range(4):
            step = below << bit
            got = lax.ppermute(send, "dp", [(i, i ^ step) for i in range(shards)])
            count = count // 2

            def total(piece):
                return (keep[piece].astype(F32) + got[piece].astype(F32)).astype(BF16)

            if count == 0:
                keep = total(slice(0, 1))
            else:
                send = total(slice(count, 2 * count))
                keep = total(slice(0, count))
        keep = keep[0]
        step = 1
        while step < below:
            keep = keep + lax.ppermute(keep, "dp", [(i, i ^ step) for i in range(shards)])
            step *= 2
        return keep

    mine_ffn = reduced(keep_ffn, send_ffn)
    other_ffn = lax.ppermute(mine_ffn, "head", swap)
    mine_attn = reduced(keep_attn, send_attn)
    other_attn = lax.ppermute(mine_attn, "head", swap)
    mine_conv = reduced(keep_conv, send_conv)
    other_conv = lax.ppermute(mine_conv, "head", swap)
    mine_glu = reduced(keep_glu, send_glu)
    other_glu = lax.ppermute(mine_glu, "head", swap)
    ffn_out, ffn_in, out, qkv, point = call(
        finish_early_kernel,
        [
            ((per_row, width), F32),
            ((rows, ffn), F32),
            ((rows, width), F32),
            ((rows, 3 * width), F32),
            ((per_row, half), F32),
        ],
        [],
        meta,
        mine_ffn,
        other_ffn,
        mine_attn,
        other_attn,
    )
    left, conv, glu, gains, shifts, depth, vectors = call(
        finish_late_kernel,
        [
            ((rows, ffn), F32),
            ((3, rows, half), F32),
            ((rows, 2 * width), F32),
            ((4, rows), F32),
            ((4, rows), F32),
            ((9, LANES), F32),
            ((16, 2 * LANES), F32),
        ],
        [],
        meta,
        mine_conv,
        other_conv,
        mine_glu,
        other_glu,
    )
    results = (
        (glu, 0),
        (vectors[15, 0 : 2 * rows], 0),
        (gains, 1),
        (shifts, 1),
        (vectors[9, 0:LANES], 0),
        (vectors[10, 0:LANES], 0),
        (left, 0),
        (vectors[11, 0:LANES], 0),
        (conv, 1),
        (vectors[0:2, LANES:].reshape(-1), None),
        (depth, 1),
        (point, 0),
        (vectors[2:4, LANES:].reshape(-1), None),
        (qkv, 0),
        (out, 0),
        (ffn_in, 0),
        (vectors[12, 0:LANES], 0),
        (ffn_out, 0),
        (vectors[15, 2 * rows : 3 * rows], 0),
    )
    final = []
    for value, axis in results:
        if axis is not None and below > 1:
            size = value.shape[axis] // below
            value = lax.dynamic_slice_in_dim(value, lax.axis_index("dp") % below * size, size, axis)
        final.append(value)
    return (out_tokens[None], grad_tokens[None], *final)


def solution(mesh):
    return jax.shard_map(
        per_device,
        mesh=mesh,
        in_specs=(P("dp", "head", None), P("dp"), P("dp", "head", None)) + (P(),) * 19,
        out_specs=(
            P("dp", "head", None),
            P("dp", "head", None),
            P("dp", None),
            P("dp"),
            P(None, "dp"),
            P(None, "dp"),
            P("dp"),
            P("dp"),
            P("dp", None),
            P("dp"),
            P(None, "dp", None),
            P(),
            P(None, "dp"),
            P("dp", None),
            P(),
            P("dp", None),
            P("dp", None),
            P("dp", None),
            P("dp"),
            P("dp", None),
            P("dp"),
        ),
        check_vma=False,
    )
```

```python
import functools

import jax
import jax.numpy as jnp
from jax import lax
from jax.experimental import pallas as pl
from jax.experimental.pallas import tpu as pltpu
from jax.sharding import PartitionSpec as P

HEAD_DIM = 64
EPSILON = 1e-06
LANES = 128
TILE = 256
GROUPS = 16
F32 = jnp.float32
BF16 = jnp.bfloat16
VMEM_BYTES = 40 * 1024 * 1024
FFN_BITS = (2, 1, 3)
ATTN_BITS = (1, 2, 3)
CONV_BITS = (1, 2, 3)
GLU_BITS = (1, 2, 3)


def mm(a, b):
    return lax.dot_general(a, b, (((1,), (0,)), ((), ())), preferred_element_type=F32)


def mm_nt(a, b):
    return lax.dot_general(a, b, (((1,), (1,)), ((), ())), preferred_element_type=F32)


def mm_tn(a, b):
    return lax.dot_general(a, b, (((0,), (0,)), ((), ())), preferred_element_type=F32)


def mean(v):
    return jnp.mean(v, axis=-1, keepdims=True)


def normalized(v):
    centred = v - mean(v)
    rate = lax.rsqrt(mean(centred * centred) + EPSILON)
    return centred * rate, rate


def norm_back(vhat, rate, gained):
    return (gained - mean(gained) - vhat * mean(gained * vhat)) * rate


def sum_tokens(v):
    return jnp.sum(v, axis=0, keepdims=True)


def part_sums(v):
    return jnp.sum(v.reshape(v.shape[0] // 8, 8, v.shape[1]), axis=0)


def row_blocks(total, step, body, carry=0, unroll=1):
    def visit(i, c):
        return body(pl.multiple_of(i * step, step), c)

    return lax.fori_loop(0, total // step, visit, carry, unroll=unroll)


def valid_rows(start, count, length):
    places = start + lax.broadcasted_iota(jnp.int32, (count, 1), 0)
    return (places < length).astype(F32)


def col(n, width=TILE):
    return slice(n * width, (n + 1) * width)


def vector(ref):
    return ref[...].astype(F32).reshape(1, ref.shape[0])


def slot_block(p, sent, bits):
    group = lax.axis_index("dp") // (lax.axis_size("dp") // GROUPS)
    wanted = ((p >> 2) & 1) << bits[0] | ((p >> 1) & 1) << bits[1] | (p & 1) << bits[2]
    return group ^ (wanted | sent)


def for_slots(keep, send, bits, body):
    def visit(p, c):
        for sent, out in ((0, keep), (1, send)):
            body(p, slot_block(p, sent, bits), out)
        return c

    lax.fori_loop(0, GROUPS // 2, visit, 0)


def place_rows(grad, keep, send, bits, at, rows):
    def one(p, block, out):
        out[p, at : at + rows, :] = grad[pl.ds(pl.multiple_of(block * rows, rows), rows), :].astype(BF16)

    for_slots(keep, send, bits, one)


def forward_kernel(
    lengths,
    other,
    cot_other,
    far,
    out_tokens,
    stream,
    first,
    joined,
    after_glu,
    second,
    left_pre,
    right_pre,
    depth_low,
    after_conv,
    fourth,
    packed,
    probs,
    context,
    d_after,
    small,
    keep,
    send,
    third,
    sides,
    after_attn,
    fifth,
    hidden,
    cot,
    d_hidden,
    d_fifth,
    grad,
):
    part, width = other.shape
    seq = 2 * part
    ffn = left_pre.shape[1]
    half = right_pre.shape[1]
    side = lax.axis_index("head")
    length = lengths[0]
    own = pl.ds(pl.multiple_of(side * part, part), part)
    opposite = pl.ds(pl.multiple_of((1 - side) * part, part), part)
    (
        mine,
        gains,
        shifts,
        glu_bias,
        glu_w,
        conv_bias,
        conv_w,
        left_bias,
        left_w,
        mid_gain,
        mid_bias,
        depth_w,
        point_bias,
        point_w,
        qkv_w,
        out_w,
        ffn_in_bias,
        ffn_in_w,
        ffn_out_bias,
        ffn_out_w,
        cot_mine,
    ) = far
    stream[opposite, :] = other[...]
    cot[opposite, :] = cot_other[...]
    stream[own, :] = mine()[...]
    gains, shifts = gains(), shifts()
    gain = [gains[k : k + 1, :].astype(F32) for k in range(4)]
    shift = [shifts[k : k + 1, :].astype(F32) for k in range(4)]

    def first_rows(r, c):
        rows = pl.ds(r, 64)
        vhat, _ = normalized(stream[rows, :].astype(F32))
        first[rows, :] = (vhat * gain[0] + shift[0]).astype(BF16)
        return c

    row_blocks(seq, 64, first_rows, unroll=2)
    glu_b, glu_w = vector(glu_bias()), glu_w()
    for n in range(2 * width // TILE):
        joined[:, col(n)] = mm(first[...], glu_w[:, col(n)]) + glu_b[:, col(n)]

    def glu_rows(r, c):
        rows = pl.ds(r, 32)
        gate = jax.nn.sigmoid(joined[rows, width:])
        joined[rows, width:] = gate
        v = stream[rows, :].astype(F32) + joined[rows, :width] * gate
        after_glu[rows, :] = v
        vhat, _ = normalized(v)
        second[rows, :] = ((vhat * gain[1] + shift[1]) * valid_rows(r, 32, length)).astype(BF16)
        return c

    row_blocks(seq, 32, glu_rows, unroll=2)
    blank = jnp.zeros((8, half), F32)
    for k in range(2):
        sides[k, 0:8, :] = blank
        sides[k, 8 + seq : 16 + seq, :] = blank
    conv_w = conv_w()
    sides[0, 8 : 8 + seq, :] = mm(second[...], conv_w[0])
    sides[1, 8 : 8 + seq, :] = mm(second[...], conv_w[2])
    right_pre[...] = mm(second[...], conv_w[1]) + vector(conv_bias())
    right_pre[...] = right_pre[...] + sides[0, 7 : 7 + seq, :] + sides[1, 9 : 9 + seq, :]
    left_b, left_w = vector(left_bias()), left_w()
    for n in range(ffn // TILE):
        left_pre[:, col(n)] = mm(second[...], left_w[:, col(n)]) + left_b[:, col(n)]
    mid_g, mid_b, depth_w = vector(mid_gain()), vector(mid_bias()), depth_w()
    chunks = ffn // LANES
    edge = jnp.zeros((8, LANES), F32)
    for k in range(chunks):
        third[k, 0:8, :] = edge
        third[k, 8 + seq : 16 + seq, :] = edge

    def mid_rows(r, c):
        rows = pl.ds(r, 16)
        vhat, _ = normalized(combine(left_pre[rows, :], right_pre[rows, :]))
        v = (vhat * mid_g + mid_b) * valid_rows(r, 16, length)
        for k in range(chunks):
            third[k, pl.ds(pl.multiple_of(8 + r, 8), 16), :] = v[:, col(k, LANES)]
        return c

    row_blocks(seq, 16, mid_rows, unroll=2)

    def depth_lanes(k, c):
        lanes = pl.ds(pl.multiple_of(k * LANES, LANES), LANES)
        taps = depth_w[:, lanes].astype(F32)
        total = third[k, 4 : 4 + seq, :] * taps[0:1, :]
        for j in range(1, 9):
            total = total + third[k, 4 + j : 4 + j + seq, :] * taps[j : j + 1, :]
        depth_low[:, lanes] = total.astype(BF16)
        return c

    lax.fori_loop(0, chunks, depth_lanes, 0)
    after_conv[:, :half] = (
        after_glu[:, :half] + mm(depth_low[...], point_w()[...]) + vector(point_bias())
    )
    after_conv[:, half:] = after_glu[:, half:]

    def fourth_rows(r, c):
        rows = pl.ds(r, 64)
        vhat, _ = normalized(after_conv[rows, :])
        fourth[rows, :] = (vhat * gain[2] + shift[2]).astype(BF16)
        return c

    row_blocks(seq, 64, fourth_rows, unroll=2)
    qkv_w = qkv_w()
    for n in range(3 * width // TILE):
        packed[:, col(n)] = mm(fourth[...], qkv_w[:, col(n)]).astype(BF16)

    low_lanes = lax.broadcasted_iota(jnp.int32, (1, LANES), 1) < HEAD_DIM
    scale = HEAD_DIM ** (-0.5)

    def head_pair(p, c):
        lanes = pl.ds(pl.multiple_of(p * LANES, LANES), LANES)
        q = packed[:, lanes].astype(F32) * scale
        k = packed[:, pl.ds(pl.multiple_of(width + p * LANES, LANES), LANES)]
        v = packed[:, pl.ds(pl.multiple_of(2 * width + p * LANES, LANES), LANES)]
        open_keys = lax.broadcasted_iota(jnp.int32, (seq, 1), 0) < length
        results = []
        for e in range(2):
            q_one = jnp.where(low_lanes if e == 0 else ~low_lanes, q, 0.0).astype(BF16)
            s = jnp.where(open_keys, mm_nt(k, q_one), -1000000000.0)
            raised = jnp.exp(s - jnp.max(s, axis=0, keepdims=True))
            chance = raised * (1.0 / jnp.sum(raised, axis=0, keepdims=True))
            probs[2 * p + e] = chance
            results.append(mm_tn(v, chance.astype(BF16)))
        both = jnp.concatenate([results[0][:HEAD_DIM], results[1][HEAD_DIM:]], axis=0)
        context[:, lanes] = both.T.astype(BF16)
        return c

    lax.fori_loop(0, width // LANES, head_pair, 0)
    out_w = out_w()
    for n in range(width // TILE):
        after_attn[:, col(n)] = after_conv[:, col(n)] + mm(context[...], out_w[:, col(n)])

    def fifth_rows(r, c):
        rows = pl.ds(r, 64)
        vhat, _ = normalized(after_attn[rows, :])
        fifth[rows, :] = (vhat * gain[3] + shift[3]).astype(BF16)
        return c

    row_blocks(seq, 64, fifth_rows, unroll=2)
    ffn_in_b, ffn_in_w = vector(ffn_in_bias()), ffn_in_w()
    for n in range(ffn // TILE):
        pre = mm(fifth[...], ffn_in_w[:, col(n)]) + ffn_in_b[:, col(n)]
        hidden[:, col(n)] = jnp.where(pre > 0.0, pre, 0.0).astype(BF16)
    ffn_out_b, ffn_out_w = vector(ffn_out_bias()), ffn_out_w()
    for n in range(width // TILE):
        out_tokens[:, col(n)] = (
            after_attn[own, col(n)]
            + mm(hidden[own, :], ffn_out_w[:, col(n)])
            + ffn_out_b[:, col(n)]
        ).astype(BF16)

    cot[own, :] = cot_mine()[...]
    for n in range(ffn // TILE):
        back = mm_nt(cot[...], ffn_out_w[col(n), :])
        back = jnp.where(hidden[:, col(n)].astype(F32) > 0.0, back, 0.0).astype(BF16)
        d_hidden[:, col(n)] = back
        small[0:1, col(n)] = sum_tokens(back.astype(F32))
    for n in range(width // TILE):
        d_fifth[:, col(n)] = mm_nt(d_hidden[...], ffn_in_w[col(n), :])

    cot_half = cot[:, pl.ds(pl.multiple_of(side * (width // 2), width // 2), width // 2)]
    per_row = ffn // GROUPS
    sums = [jnp.zeros((8, width), F32)] * 3
    for p in range(GROUPS // 2):
        block = slice(p * seq // 8, (p + 1) * seq // 8)
        vhat, rate = normalized(after_attn[block, :])
        e = d_fifth[block, :]
        given = cot[block, :].astype(F32)
        d_after[block, :] = given + norm_back(vhat, rate, e * gain[3])
        sums = [total + part_sums(v) for total, v in zip(sums, (e * vhat, e, given))]
        for sent, out in ((0, keep), (1, send)):
            at = pl.multiple_of(slot_block(p, sent, FFN_BITS) * per_row, per_row)
            out[p, 0:per_row, :] = mm_tn(hidden[:, pl.ds(at, per_row)], cot_half).astype(BF16)
    for k in range(3):
        small[1:2, k * width : (k + 1) * width] = sum_tokens(sums[k])

    rows = width // GROUPS
    for j in range(ffn // 2 // TILE):
        at = pl.multiple_of(side * (ffn // 2) + j * TILE, TILE)
        grad[...] = mm_tn(fifth[...], d_hidden[:, pl.ds(at, TILE)])
        place_rows(grad, keep, send, FFN_BITS, per_row + j * rows, rows)


def combine(left_pre, right_pre):
    half = right_pre.shape[1]
    left = jnp.maximum(left_pre, 0.0)
    return jnp.concatenate([left[:, :half] + jnp.maximum(right_pre, 0.0), left[:, half:]], axis=1)


def attention_back_kernel(
    d_after,
    packed,
    probs,
    context,
    fourth,
    after_conv,
    depth_low,
    far,
    d_after_conv,
    small,
    keep,
    send,
    d_attn,
    d_context,
    d_packed,
    d_fourth,
    d_sep,
    grad,
):
    seq, width = d_after.shape
    side = lax.axis_index("head")
    out_w, qkv_w, gains = far
    half = d_sep.shape[1]
    ffn = depth_low.shape[1]
    rows = width // GROUPS
    d_attn[...] = d_after[...].astype(BF16)
    out_w = out_w()
    for n in range(width // TILE):
        d_context[:, col(n)] = mm_nt(d_attn[...], out_w[col(n), :]).astype(BF16)
    low_lanes = lax.broadcasted_iota(jnp.int32, (1, LANES), 1) < HEAD_DIM
    scale = HEAD_DIM ** (-0.5)

    def head_pair(p, c):
        lanes = pl.ds(pl.multiple_of(p * LANES, LANES), LANES)
        k_lanes = pl.ds(pl.multiple_of(width + p * LANES, LANES), LANES)
        v_lanes = pl.ds(pl.multiple_of(2 * width + p * LANES, LANES), LANES)
        q = packed[:, lanes]
        k = packed[:, k_lanes]
        v = packed[:, v_lanes].astype(F32)
        given = d_context[:, lanes]
        dq, dk, dv = [], [], []
        for e in range(2):
            one = jnp.where(low_lanes if e == 0 else ~low_lanes, v, 0.0).astype(BF16)
            chance = probs[2 * p + e]
            d_probs = mm_nt(one, given)
            delta = jnp.sum(d_probs * chance, axis=0, keepdims=True)
            d_scores = (chance * (d_probs - delta)).astype(BF16)
            dv.append(mm(chance.astype(BF16), given))
            dk.append(mm(d_scores, q))
            dq.append(mm_tn(k, d_scores))
        both = jnp.concatenate([dq[0][:HEAD_DIM], dq[1][HEAD_DIM:]], axis=0)
        d_packed[:, lanes] = (both.T * scale).astype(BF16)
        d_packed[:, k_lanes] = (jnp.where(low_lanes, dk[0], dk[1]) * scale).astype(BF16)
        d_packed[:, v_lanes] = jnp.where(low_lanes, dv[0], dv[1]).astype(BF16)
        return c

    lax.fori_loop(0, width // LANES, head_pair, 0)
    qkv_w = qkv_w()
    for n in range(width // TILE):
        d_fourth[:, col(n)] = mm_nt(d_packed[...], qkv_w[col(n), :])
    gain = gains()[2:3, :].astype(F32)

    sums = [jnp.zeros((8, width), F32)] * 2
    g_point = jnp.zeros((8, half), F32)
    at = pl.multiple_of(side * (width // 2), width // 2)
    sides = [(context, d_attn, at)]
    for j in range(3 * width // 2 // TILE):
        sides.append((fourth, d_packed, pl.multiple_of(side * (3 * width // 2) + j * TILE, TILE)))
    for p in range(2 * len(sides)):
        block = slice(p * seq // 8, (p + 1) * seq // 8)
        vhat, rate = normalized(after_conv[block, :])
        e = d_fourth[block, :]
        total = d_after[block, :] + norm_back(vhat, rate, e * gain)
        d_after_conv[block, :] = total
        sep = total[:, :half].astype(BF16)
        d_sep[block, :] = sep
        sums = [total + part_sums(v) for total, v in zip(sums, (e * vhat, e))]
        g_point = g_point + part_sums(sep.astype(F32))
        values, incoming, at = sides[p // 2]
        part = slice(p % 2 * (width // 2), (p % 2 + 1) * (width // 2))
        grad[p // 2, part, :] = mm_tn(values[:, part], incoming[:, pl.ds(at, TILE)])
    small[0:1, 0:width] = sum_tokens(sums[0])
    small[0:1, width : 2 * width] = sum_tokens(sums[1])
    small[0:1, 2 * width : 2 * width + half] = sum_tokens(g_point)
    for j in range(len(sides)):
        place_rows(grad.at[j], keep, send, ATTN_BITS, j * rows, rows)
    sep_half = d_sep[:, pl.ds(pl.multiple_of(side * (half // 2), half // 2), half // 2)]
    per_row = ffn // GROUPS

    def point_slot(p, block, out):
        g = mm_tn(
            depth_low[:, pl.ds(pl.multiple_of(block * per_row, per_row), per_row)], sep_half
        ).astype(BF16)
        out[p, 4 * rows : 4 * rows + per_row // 2, 0:LANES] = g[: per_row // 2]
        out[p, 4 * rows : 4 * rows + per_row // 2, LANES : 2 * LANES] = g[per_row // 2 :]

    for_slots(keep, send, ATTN_BITS, point_slot)


def middle_back_kernel(
    lengths,
    d_after_conv,
    left_pre,
    right_pre,
    far,
    d_left,
    taps_right,
    small,
    vhat3,
    third,
    d_depth,
    d_third,
    rates,
    sums,
    d_right,
    mid_row,
):
    seq, width = d_after_conv.shape
    ffn = left_pre.shape[1]
    half = right_pre.shape[1]
    length = lengths[0]
    point_w, mid_gain, mid_bias, depth_w = far
    chunks = ffn // LANES
    edge = jnp.zeros((8, LANES), F32)
    for k in range(chunks):
        d_depth[k, 0:8, :] = edge
        d_depth[k, 8 + seq : 16 + seq, :] = edge
    d_sep = d_after_conv[:, :half].astype(BF16)
    point_w = point_w()
    for n in range(ffn // TILE):
        block = mm_nt(d_sep, point_w[col(n), :])
        for m in range(TILE // LANES):
            d_depth[n * (TILE // LANES) + m, 8 : 8 + seq, :] = block[:, col(m, LANES)]

    mid_g, mid_b, depth_w = vector(mid_gain()), vector(mid_bias()), depth_w()
    mid_row[...] = mid_g

    def mid_rows(r, c):
        rows = pl.ds(r, 16)
        vhat, rate = normalized(combine(left_pre[rows, :], right_pre[rows, :]))
        v = (vhat * mid_g + mid_b) * valid_rows(r, 16, length)
        rates[rows, :] = jnp.broadcast_to(rate, (16, LANES))
        for k in range(chunks):
            third[k, rows, :] = v[:, col(k, LANES)]
            vhat3[k, rows, :] = vhat[:, col(k, LANES)]
        return c

    row_blocks(seq, 16, mid_rows, unroll=2)
    sums[...] = jnp.zeros(sums.shape, F32)
    step = 64

    def depth_lanes(k, c):
        lanes = pl.ds(pl.multiple_of(k * LANES, LANES), LANES)
        taps = depth_w[:, lanes].astype(F32)
        mid_lanes = mid_row[0:1, lanes]
        totals = [jnp.zeros((8, LANES), F32)] * 11
        for r in range(0, seq, step):
            block = slice(r, r + step)
            here = third[k, block, :]
            total = None
            for j in range(9):
                moved = d_depth[k, 12 - j + r : 12 - j + r + step, :]
                totals[j] = totals[j] + part_sums(moved * here)
                term = moved * taps[j : j + 1, :]
                total = term if total is None else total + term
            total = total * valid_rows(r, step, length)
            vhat = vhat3[k, block, :]
            totals[9] = totals[9] + part_sums(total * vhat)
            totals[10] = totals[10] + part_sums(total)
            gained = total * mid_lanes
            d_third[k, block, :] = gained
            sums[0, block, :] = sums[0, block, :] + gained
            sums[1, block, :] = sums[1, block, :] + gained * vhat
        for j in range(11):
            small[j : j + 1, lanes] = sum_tokens(totals[j])
        return c

    lax.fori_loop(0, chunks, depth_lanes, 0)
    inverse = 1.0 / ffn
    sums[0] = jnp.broadcast_to(jnp.sum(sums[0], axis=-1, keepdims=True) * inverse, (seq, LANES))
    sums[1] = jnp.broadcast_to(jnp.sum(sums[1], axis=-1, keepdims=True) * inverse, (seq, LANES))

    def combined_lanes(k):
        return (d_third[k] - sums[0] - vhat3[k] * sums[1]) * rates[...]

    def left_lanes(k, c):
        lanes = pl.ds(pl.multiple_of(k * LANES, LANES), LANES)
        v = jnp.where(left_pre[:, lanes] > 0.0, combined_lanes(k), 0.0).astype(BF16)
        d_left[:, lanes] = v
        small[11:12, lanes] = sum_tokens(v.astype(F32))
        return c

    lax.fori_loop(0, chunks, left_lanes, 0)
    blank = jnp.zeros((8, half), F32)
    d_right[0:8, :] = blank
    d_right[8 + seq : 16 + seq, :] = blank
    for k in range(half // LANES):
        v = jnp.where(right_pre[:, col(k, LANES)] > 0.0, combined_lanes(k), 0.0).astype(BF16)
        v = v.astype(F32)
        d_right[8 : 8 + seq, col(k, LANES)] = v
        small[12:13, col(k, LANES)] = sum_tokens(v)
    taps_right[0] = d_right[9 : 9 + seq, :].astype(BF16)
    taps_right[1] = d_right[8 : 8 + seq, :].astype(BF16)
    taps_right[2] = d_right[7 : 7 + seq, :].astype(BF16)


def conv_back_kernel(
    lengths,
    d_left,
    taps_right,
    second,
    far,
    d_second,
    keep,
    send,
    grad,
    grad_conv,
):
    seq, width = d_second.shape
    ffn = d_left.shape[1]
    half = taps_right.shape[2]
    side = lax.axis_index("head")
    valid = valid_rows(0, seq, lengths[0])
    rows = width // GROUPS
    for j in range(ffn // 2 // TILE):
        at = pl.multiple_of(side * (ffn // 2) + j * TILE, TILE)
        grad[...] = mm_tn(second[...], d_left[:, pl.ds(at, TILE)])
        place_rows(grad, keep, send, CONV_BITS, j * rows, rows)
    start = ffn // 2 // TILE * rows
    half_lanes = pl.ds(pl.multiple_of(side * (half // 2), half // 2), half // 2)
    for tap in range(3):
        grad_conv[tap] = mm_tn(second[...], taps_right[tap, :, half_lanes])

    def conv_slot(p, block, out):
        at = pl.multiple_of(block * rows, rows)
        middle = pl.multiple_of(block * rows + rows // 2, rows // 2)
        h = rows // 2
        out[p, start : start + rows, 0:LANES] = grad_conv[0, pl.ds(at, rows), :].astype(BF16)
        out[p, start + rows : start + rows + h, 0:LANES] = grad_conv[1, pl.ds(at, h), :].astype(BF16)
        out[p, start : start + h, LANES : 2 * LANES] = grad_conv[1, pl.ds(middle, h), :].astype(BF16)
        out[p, start + h : start + h + rows, LANES : 2 * LANES] = grad_conv[
            2, pl.ds(at, rows), :
        ].astype(BF16)

    for_slots(keep, send, CONV_BITS, conv_slot)
    left_w, conv_w = (get() for get in far)
    for n in range(width // TILE):
        total = mm_nt(d_left[...], left_w[col(n), :])
        for tap in range(3):
            total = total + mm_nt(taps_right[tap], conv_w[tap, col(n), :])
        d_second[:, col(n)] = total * valid


def glu_back_kernel(
    d_second,
    d_after_conv,
    after_glu,
    joined,
    first,
    stream,
    small_ffn,
    small_attn,
    small_conv,
    far,
    grad_tokens,
    keep,
    send,
    d_joined,
    d_after_glu,
    d_first,
    rolled,
    blocks,
    grad,
):
    seq, width = d_second.shape
    part = seq // 2
    side = lax.axis_index("head")
    gains, glu_w = far
    gains = gains()
    gain = [gains[k : k + 1, :].astype(F32) for k in range(2)]

    def glu_rows(r, c):
        g_gain, g_shift, g_value, g_gate = c
        rows = pl.ds(r, 32)
        vhat, rate = normalized(after_glu[rows, :])
        e = d_second[rows, :]
        total = d_after_conv[rows, :] + norm_back(vhat, rate, e * gain[1])
        d_after_glu[rows, :] = total
        value = joined[rows, :width]
        gate = joined[rows, width:]
        d_value = (total * gate).astype(BF16)
        d_gate = (total * value * gate * (1.0 - gate)).astype(BF16)
        d_joined[rows, :width] = d_value
        d_joined[rows, width:] = d_gate
        return (
            g_gain + part_sums(e * vhat),
            g_shift + part_sums(e),
            g_value + part_sums(d_value.astype(F32)),
            g_gate + part_sums(d_gate.astype(F32)),
        )

    nothing = jnp.zeros((8, width), F32)
    sums = row_blocks(seq, 32, glu_rows, (nothing,) * 4, unroll=2)
    gain_one, shift_one, g_value, g_gate = (sum_tokens(v) for v in sums)
    glu_w = glu_w()
    for n in range(width // TILE):
        d_first[:, col(n)] = mm_nt(d_joined[...], glu_w[col(n), :])

    sums = [nothing] * 2
    rows = width // GROUPS
    columns = [pl.ds(pl.multiple_of(side * width + j * TILE, TILE), TILE) for j in range(width // TILE)]
    for p in range(8):
        block = slice(p * seq // 8, (p + 1) * seq // 8)
        vhat, rate = normalized(stream[block, :].astype(F32))
        e = d_first[block, :]
        d_after_glu[block, :] = d_after_glu[block, :] + norm_back(vhat, rate, e * gain[0])
        sums = [total + part_sums(v) for total, v in zip(sums, (e * vhat, e))]
        if p < 2 * len(columns):
            part_rows = slice(p % 2 * (width // 2), (p % 2 + 1) * (width // 2))
            grad[p // 2, part_rows, :] = mm_tn(first[:, part_rows], d_joined[:, columns[p // 2]])
    gain_zero, shift_zero = (sum_tokens(v) for v in sums)
    grad_tokens[...] = d_after_glu[pl.ds(pl.multiple_of(side * part, part), part), :]
    for j in range(len(columns)):
        place_rows(grad.at[j], keep, send, GLU_BITS, j * rows, rows)

    blocks[...] = jnp.zeros(blocks.shape, F32)
    rolled[...] = jnp.zeros(rolled.shape, F32)
    vectors = (
        (gain_zero, gain_one, small_attn[0:1, 0:width], small_ffn[1:2, 0:width]),
        (shift_zero, shift_one, small_attn[0:1, width : 2 * width], small_ffn[1:2, width : 2 * width]),
    )
    tiles = width // LANES
    lane = lax.broadcasted_iota(jnp.int32, (8, LANES), 1)
    quarter = LANES // tiles
    for kind, four in enumerate(vectors):
        for k, vector in enumerate(four):
            for t in range(tiles):
                rolled[kind, 8 * k + t : 8 * k + t + 1, :] = vector[:, col(t, LANES)]
        for q in range(tiles):
            total = jnp.zeros((8, LANES), F32)
            for k in range(4):
                moved = pltpu.roll(rolled[kind, 8 * k : 8 * k + 8, :], (quarter * (k - q)) % LANES, 1)
                total = jnp.where((lane >= quarter * k) & (lane < quarter * (k + 1)), moved, total)
            for t in range(tiles):
                blocks[tiles * t + q, 13 + kind : 14 + kind, 0:LANES] = total[t : t + 1, :]
    lane = lane[0:1, :]
    g_out = small_ffn[1:2, 2 * width : 3 * width]
    for s in range(GROUPS):
        source = g_value if s < GROUPS // 2 else g_gate
        place = (s % (GROUPS // 2)) * (2 * width // GROUPS)
        block = source[:, place // LANES * LANES : place // LANES * LANES + LANES]
        glu_part = block if place % LANES == 0 else pltpu.roll(block, LANES - place % LANES, 1)
        place = s * (width // GROUPS)
        block = g_out[:, place // LANES * LANES : place // LANES * LANES + LANES]
        moved = (LANES // 2 - place % LANES) % LANES
        out_part = block if moved == 0 else pltpu.roll(block, moved, 1)
        blocks[s, 15:16, 0:LANES] = jnp.where(
            lane < LANES // 2, glu_part, jnp.where(lane < LANES // 2 + quarter, out_part, 0.0)
        )
        blocks[s, 0:12, 0:LANES] = small_conv[0:12, col(s, LANES)]
        blocks[s, 12:13, 0:LANES] = small_ffn[0:1, col(s, LANES)]
        for k in range(2):
            blocks[s, k : k + 1, LANES : 2 * LANES] = small_conv[12:13, col(k, LANES)]
            blocks[s, 2 + k : 3 + k, LANES : 2 * LANES] = small_attn[
                0:1, 2 * width + k * LANES : 2 * width + (k + 1) * LANES
            ]
    start = width // TILE * rows

    def small_slot(p, block, out):
        out[p, start : start + 16, :] = blocks[block].astype(BF16)

    for_slots(keep, send, GLU_BITS, small_slot)


def add_kernel(*refs):
    *inputs, far, keep, send = refs
    at = 0
    for kept, got in zip(inputs[::2], inputs[1::2]):
        rows = kept.shape[1]
        for out, place in ((keep, 0), (send, 1)):
            total = kept[place].astype(F32) + got[place].astype(F32)
            out[0, at : at + rows, :] = total.astype(BF16)
        at += rows


def finish_early_kernel(mine, other, far, ffn_out, ffn_in, out, qkv, point):
    side = lax.axis_index("head")
    per_row, width = ffn_out.shape
    rows = ffn_in.shape[0]
    for who, grads in ((side, mine), (1 - side, other)):
        count = ffn_in.shape[1] // 2 // TILE
        at = pl.ds(pl.multiple_of(who * TILE, TILE), TILE)
        start = per_row + count * rows
        ffn_out[:, at] = grads[0:per_row, :].astype(F32)
        out[:, at] = grads[start : start + rows, :].astype(F32)
        for j in range(count):
            at = pl.ds(pl.multiple_of((who * count + j) * TILE, TILE), TILE)
            ffn_in[:, at] = grads[per_row + j * rows : per_row + (j + 1) * rows, :].astype(F32)
        count = qkv.shape[1] // 2 // TILE
        for j in range(count):
            at = pl.ds(pl.multiple_of((who * count + j) * TILE, TILE), TILE)
            qkv[:, at] = grads[start + (1 + j) * rows : start + (2 + j) * rows, :].astype(F32)
        start = start + (1 + count) * rows
        at = pl.ds(pl.multiple_of(who * LANES, LANES), LANES)
        point[0 : per_row // 2, at] = grads[start : start + per_row // 2, 0:LANES].astype(F32)
        point[per_row // 2 :, at] = grads[start : start + per_row // 2, LANES : 2 * LANES].astype(F32)


def finish_late_kernel(
    mine,
    other,
    far,
    left,
    conv,
    glu,
    gains,
    shifts,
    depth,
    mid_gain,
    mid_bias,
    left_bias,
    ffn_in_bias,
    glu_bias,
    ffn_out_bias,
    conv_bias,
    point_bias,
):
    side = lax.axis_index("head")
    rows = glu.shape[0]
    h = rows // 2
    count = left.shape[1] // 2 // TILE
    behind = count * rows + 3 * h
    wide = glu.shape[1] // 2 // TILE
    for who, grads in ((side, mine), (1 - side, other)):
        for j in range(count):
            at = pl.ds(pl.multiple_of((who * count + j) * TILE, TILE), TILE)
            left[:, at] = grads[j * rows : (j + 1) * rows, :].astype(F32)
        start = count * rows
        at = pl.ds(pl.multiple_of(who * LANES, LANES), LANES)
        low = grads[start : start + 3 * h, 0:LANES].astype(F32)
        high = grads[start : start + 3 * h, LANES : 2 * LANES].astype(F32)
        conv[0, :, at] = low[0:rows]
        conv[1, 0:h, at] = low[rows:]
        conv[1, h:rows, at] = high[0:h]
        conv[2, :, at] = high[h:]
        for j in range(wide):
            at = pl.ds(pl.multiple_of((who * wide + j) * TILE, TILE), TILE)
            glu[:, at] = grads[behind + j * rows : behind + (j + 1) * rows, :].astype(F32)
    start = behind + wide * rows
    block = mine[start : start + 16, :].astype(F32)
    depth[...] = block[0:9, 0:LANES]
    for k in range(4):
        gains[k : k + 1, :] = block[13:14, k * rows : (k + 1) * rows]
        shifts[k : k + 1, :] = block[14:15, k * rows : (k + 1) * rows]
    mid_gain[...] = block[9, 0:LANES]
    mid_bias[...] = block[10, 0:LANES]
    left_bias[...] = block[11, 0:LANES]
    ffn_in_bias[...] = block[12, 0:LANES]
    glu_bias[...] = block[15, 0 : 2 * rows]
    ffn_out_bias[...] = block[15, 2 * rows : 3 * rows]
    for k in range(2):
        conv_bias[col(k, LANES)] = block[k, LANES : 2 * LANES]
        point_bias[col(k, LANES)] = block[2 + k, LANES : 2 * LANES]


def call(kernel, outs, scratch, near, far, micros=2, scalars=0):
    smem = pl.BlockSpec(memory_space=pltpu.SMEM)
    vmem = pl.BlockSpec(memory_space=pltpu.VMEM)
    anywhere = pl.BlockSpec(memory_space=pltpu.HBM)

    def body(*refs):
        inputs = refs[: len(near)]
        sources = refs[len(near) : len(near) + len(far)]
        results = refs[len(near) + len(far) : len(near) + len(far) + len(outs)]
        rest = refs[len(near) + len(far) + len(outs) :]
        if not far:
            kernel(*inputs, (), *results, *rest)
            return
        *rest, done = rest
        buffers = rest[len(scratch) :]
        copies = [
            pltpu.make_async_copy(source, buffer, done.at[i])
            for i, (source, buffer) in enumerate(zip(sources, buffers))
        ]
        for copy in copies:
            copy.start()

        def fetched(copy, buffer):
            def get():
                copy.wait()
                return buffer

            return get

        kernel(*inputs, tuple(map(fetched, copies, buffers)), *results, *rest[: len(scratch)])

    temporaries = [pltpu.VMEM(shape, dtype) for shape, dtype in scratch]
    if far:
        temporaries += [pltpu.VMEM(v.shape, v.dtype) for v in far]
        temporaries.append(pltpu.SemaphoreType.DMA((len(far),)))
    return pl.pallas_call(
        body,
        out_shape=tuple(jax.ShapeDtypeStruct(shape, dtype) for shape, dtype in outs),
        in_specs=[smem] * scalars + [vmem] * (len(near) - scalars) + [anywhere] * len(far),
        out_specs=(vmem,) * len(outs),
        scratch_shapes=temporaries,
        compiler_params=pltpu.CompilerParams(vmem_limit_bytes=VMEM_BYTES),
        cost_estimate=pl.CostEstimate(
            flops=micros * 10**9, transcendentals=0, bytes_accessed=micros * 3 * 10**6
        ),
        name=kernel.__name__,
    )(*near, *[pltpu.with_memory_space_constraint(v, pltpu.HBM) for v in far])


def per_device(
    tokens,
    lengths,
    cotangent,
    glu_weight,
    glu_bias,
    norm_gain,
    norm_bias,
    mid_gain,
    mid_bias,
    left_weight,
    left_bias,
    conv_weight,
    conv_bias,
    depth_weight,
    point_weight,
    point_bias,
    qkv_weight,
    out_weight,
    ffn_in_weight,
    ffn_in_bias,
    ffn_out_weight,
    ffn_out_bias,
):
    row_count, part, width = tokens.shape
    assert row_count == 1 and lax.axis_size("head") == 2
    seq = 2 * part
    shards = lax.axis_size("dp")
    below = shards // GROUPS
    assert below * GROUPS == shards
    heads = width // HEAD_DIM
    half = conv_weight.shape[2]
    ffn = left_weight.shape[1]
    swap = [(0, 1), (1, 0)]
    mine = tokens[0]
    cot_mine = cotangent[0]
    other = lax.ppermute(mine, "head", swap)
    cot_other = lax.ppermute(cot_mine, "head", swap)

    def slot_outs(rows):
        return [((GROUPS // 2, rows, TILE), BF16)] * 2

    rows = width // GROUPS
    per_row = ffn // GROUPS
    ffn_rows = per_row + ffn // 2 // TILE * rows
    (
        out_tokens,
        stream,
        first_norm,
        joined,
        after_glu,
        second,
        left_pre,
        right_pre,
        depth_low,
        after_conv,
        fourth,
        packed,
        probs,
        context,
        d_after,
        small_ffn,
        keep_ffn,
        send_ffn,
    ) = call(
        forward_kernel,
        [
            ((part, width), BF16),
            ((seq, width), BF16),
            ((seq, width), BF16),
            ((seq, 2 * width), F32),
            ((seq, width), F32),
            ((seq, width), BF16),
            ((seq, ffn), F32),
            ((seq, half), F32),
            ((seq, ffn), BF16),
            ((seq, width), F32),
            ((seq, width), BF16),
            ((seq, 3 * width), BF16),
            ((heads, seq, seq), F32),
            ((seq, width), BF16),
            ((seq, width), F32),
            ((8, ffn), F32),
        ]
        + slot_outs(ffn_rows),
        [
            ((ffn // LANES, seq + 16, LANES), F32),
            ((2, seq + 16, half), F32),
            ((seq, width), F32),
            ((seq, width), BF16),
            ((seq, ffn), BF16),
            ((seq, width), BF16),
            ((seq, ffn), BF16),
            ((seq, width), F32),
            ((width, TILE), F32),
        ],
        [lengths, other, cot_other],
        [
            mine,
            norm_gain,
            norm_bias,
            glu_bias,
            glu_weight,
            conv_bias,
            conv_weight,
            left_bias,
            left_weight,
            mid_gain,
            mid_bias,
            depth_weight,
            point_bias,
            point_weight,
            qkv_weight,
            out_weight,
            ffn_in_bias,
            ffn_in_weight,
            ffn_out_bias,
            ffn_out_weight,
            cot_mine,
        ],
        micros=25,
        scalars=1,
    )
    class Chunk:
        def __init__(self, keep, send, bits):
            self.keep, self.send, self.bits = keep, send, list(bits)

        def start(self):
            if not self.bits:
                self.got = lax.ppermute(self.keep, "head", swap)
                return
            step = below << self.bits.pop(0)
            self.got = lax.ppermute(self.send, "dp", [(i, i ^ step) for i in range(shards)])

        def add(self):
            n = self.keep.shape[0] // 2

            def total(piece):
                return (self.keep[piece].astype(F32) + self.got[piece].astype(F32)).astype(BF16)

            if n > 0:
                self.keep, self.send = total(slice(0, n)), total(slice(n, 2 * n))
                return
            total = total(slice(0, 1))[0]
            step = 1
            while step < below:
                total = total + lax.ppermute(total, "dp", [(i, i ^ step) for i in range(shards)])
                step *= 2
            self.keep, self.send = total, total

    def wave(held, *chunks, joined=False):
        gots = [c.got for c in chunks]
        held, gots = lax.optimization_barrier((held, gots))
        for c, got in zip(chunks, gots):
            c.got = got
        if joined:
            total = ((1, sum(c.keep.shape[1] for c in chunks), TILE), BF16)
            pair = call(add_kernel, [total, total], [], [v for c in chunks for v in (c.keep, c.got)], [])
            chunks = [Chunk(*pair, chunks[0].bits)]
        else:
            for c in chunks:
                c.add()
        held, pairs = lax.optimization_barrier((held, [(c.keep, c.send) for c in chunks]))
        for c, pair in zip(chunks, pairs):
            c.keep, c.send = pair
            c.start()
        return (held, chunks[0]) if joined else held

    ffn_grads = Chunk(keep_ffn, send_ffn, (0, *FFN_BITS))
    ffn_grads.start()
    d_after_conv, small_attn, keep_attn, send_attn = call(
        attention_back_kernel,
        [((seq, width), F32), ((8, ffn), F32)] + slot_outs(4 * rows + per_row // 2),
        [
            ((seq, width), BF16),
            ((seq, width), BF16),
            ((seq, 3 * width), BF16),
            ((seq, width), F32),
            ((seq, half), BF16),
            ((4, width, TILE), F32),
        ],
        [d_after, packed, probs, context, fourth, after_conv, depth_low],
        [out_weight, qkv_weight, norm_gain],
        micros=10,
    )
    d_after_conv = wave(d_after_conv, ffn_grads)
    attn_grads = Chunk(keep_attn, send_attn, (0, *ATTN_BITS))
    attn_grads.start()
    d_after_conv = wave(d_after_conv, attn_grads)
    d_left, taps_right, small_conv = call(
        middle_back_kernel,
        [((seq, ffn), BF16), ((3, seq, half), BF16), ((16, ffn), F32)],
        [
            ((ffn // LANES, seq, LANES), F32),
            ((ffn // LANES, seq, LANES), F32),
            ((ffn // LANES, seq + 16, LANES), F32),
            ((ffn // LANES, seq, LANES), F32),
            ((seq, LANES), F32),
            ((2, seq, LANES), F32),
            ((seq + 16, half), F32),
            ((1, ffn), F32),
        ],
        [lengths, d_after_conv, left_pre, right_pre],
        [point_weight, mid_gain, mid_bias, depth_weight],
        micros=10,
        scalars=1,
    )
    d_left = wave(d_left, ffn_grads, attn_grads)
    d_second, keep_conv, send_conv = call(
        conv_back_kernel,
        [((seq, width), F32)] + slot_outs(ffn // 2 // TILE * rows + 3 * rows // 2),
        [((width, TILE), F32), ((3, width, LANES), F32)],
        [lengths, d_left, taps_right, second],
        [left_weight, conv_weight],
        micros=5,
        scalars=1,
    )
    conv_grads = Chunk(keep_conv, send_conv, (0, *CONV_BITS))
    conv_grads.start()
    d_second = wave(d_second, conv_grads)
    grad_tokens, keep_glu, send_glu = call(
        glu_back_kernel,
        [((part, width), F32)] + slot_outs(width // TILE * rows + 16),
        [
            ((seq, 2 * width), BF16),
            ((seq, width), F32),
            ((seq, width), F32),
            ((2, 32, LANES), F32),
            ((GROUPS, 16, 2 * LANES), F32),
            ((width // TILE, width, TILE), F32),
        ],
        [
            d_second,
            d_after_conv,
            after_glu,
            joined,
            first_norm,
            stream,
            small_ffn,
            small_attn,
            small_conv,
        ],
        [norm_gain, glu_weight],
        micros=7,
    )
    glu_grads = Chunk(keep_glu, send_glu, (0, *GLU_BITS))
    glu_grads.start()
    held, early = wave(grad_tokens, ffn_grads, attn_grads, joined=True)
    held = wave(held, glu_grads)
    held = wave(held, conv_grads)
    held = wave(held, glu_grads)
    held, late = wave(held, conv_grads, glu_grads, joined=True)
    held = wave(held, early)
    held, other = lax.optimization_barrier((held, early.got))
    grad_tokens = wave(held, late)
    ffn_out, ffn_in, out, qkv, point = call(
        finish_early_kernel,
        [
            ((per_row, width), F32),
            ((rows, ffn), F32),
            ((rows, width), F32),
            ((rows, 3 * width), F32),
            ((per_row, half), F32),
        ],
        [],
        [early.keep, other],
        [],
    )
    (
        left,
        conv,
        glu,
        g_gains,
        g_shifts,
        g_depth,
        g_mid_gain,
        g_mid_bias,
        g_left_bias,
        g_ffn_in_bias,
        g_glu_bias,
        g_ffn_out_bias,
        g_conv_bias,
        g_point_bias,
    ) = call(
        finish_late_kernel,
        [
            ((rows, ffn), F32),
            ((3, rows, half), F32),
            ((rows, 2 * width), F32),
            ((4, rows), F32),
            ((4, rows), F32),
            ((9, LANES), F32),
            ((LANES,), F32),
            ((LANES,), F32),
            ((LANES,), F32),
            ((LANES,), F32),
            ((2 * rows,), F32),
            ((rows,), F32),
            ((half,), F32),
            ((half,), F32),
        ],
        [],
        [late.keep, late.got],
        [],
    )
    results = (
        (glu, 0),
        (g_glu_bias, 0),
        (g_gains, 1),
        (g_shifts, 1),
        (g_mid_gain, 0),
        (g_mid_bias, 0),
        (left, 0),
        (g_left_bias, 0),
        (conv, 1),
        (g_conv_bias, None),
        (g_depth, 1),
        (point, 0),
        (g_point_bias, None),
        (qkv, 0),
        (out, 0),
        (ffn_in, 0),
        (g_ffn_in_bias, 0),
        (ffn_out, 0),
        (g_ffn_out_bias, 0),
    )
    final = []
    for value, axis in results:
        if axis is not None and below > 1:
            size = value.shape[axis] // below
            value = lax.dynamic_slice_in_dim(value, lax.axis_index("dp") % below * size, size, axis)
        final.append(value)
    return (out_tokens[None], grad_tokens[None], *final)


def solution(mesh):
    return jax.shard_map(
        per_device,
        mesh=mesh,
        in_specs=(P("dp", "head", None), P("dp"), P("dp", "head", None)) + (P(),) * 19,
        out_specs=(
            P("dp", "head", None),
            P("dp", "head", None),
            P("dp", None),
            P("dp"),
            P(None, "dp"),
            P(None, "dp"),
            P("dp"),
            P("dp"),
            P("dp", None),
            P("dp"),
            P(None, "dp", None),
            P(),
            P(None, "dp"),
            P("dp", None),
            P(),
            P("dp", None),
            P("dp", None),
            P("dp", None),
            P("dp"),
            P("dp", None),
            P("dp"),
        ),
        check_vma=False,
    )
```

```python
import functools

import jax
import jax.numpy as jnp
from jax import lax
from jax.experimental import pallas as pl
from jax.experimental.pallas import tpu as pltpu
from jax.sharding import PartitionSpec as P

HEAD_DIM = 64
EPSILON = 1e-06
LANES = 128
TILE = 256
GROUPS = 16
F32 = jnp.float32
BF16 = jnp.bfloat16
VMEM_BYTES = 28 * 1024 * 1024
FFN_BITS = (2, 1, 3)
ATTN_BITS = (1, 2, 3)
CONV_BITS = (1, 2, 3)
GLU_BITS = (2, 1, 3)


def mm(a, b):
    return lax.dot_general(a, b, (((1,), (0,)), ((), ())), preferred_element_type=F32)


def mm_nt(a, b):
    return lax.dot_general(a, b, (((1,), (1,)), ((), ())), preferred_element_type=F32)


def mm_tn(a, b):
    return lax.dot_general(a, b, (((0,), (0,)), ((), ())), preferred_element_type=F32)


def mean(v):
    return jnp.mean(v, axis=-1, keepdims=True)


def normalized(v):
    centred = v - mean(v)
    rate = lax.rsqrt(mean(centred * centred) + EPSILON)
    return centred * rate, rate


def norm_back(vhat, rate, gained):
    return (gained - mean(gained) - vhat * mean(gained * vhat)) * rate


def sum_tokens(v):
    return jnp.sum(v, axis=0, keepdims=True)


def part_sums(v):
    return jnp.sum(v.reshape(v.shape[0] // 8, 8, v.shape[1]), axis=0)


def row_blocks(total, step, body, carry=0, unroll=1):
    def visit(i, c):
        return body(pl.multiple_of(i * step, step), c)

    return lax.fori_loop(0, total // step, visit, carry, unroll=unroll)


def valid_rows(start, count, length):
    places = start + lax.broadcasted_iota(jnp.int32, (count, 1), 0)
    return (places < length).astype(F32)


def col(n, width=TILE):
    return slice(n * width, (n + 1) * width)


def vector(ref):
    return ref[...].astype(F32).reshape(1, ref.shape[0])


def slot_block(p, sent, bits):
    group = lax.axis_index("dp") // (lax.axis_size("dp") // GROUPS)
    wanted = ((p >> 2) & 1) << bits[0] | ((p >> 1) & 1) << bits[1] | (p & 1) << bits[2]
    return group ^ (wanted | sent)


def for_slots(keep, send, bits, body):
    count = GROUPS // 2 // len(send)
    for i, piece in enumerate(send):

        def visit(q, c, i=i, piece=piece):
            p = i * count + q
            body(p, slot_block(p, 0, bits), keep)
            body(q, slot_block(p, 1, bits), piece)
            return c

        lax.fori_loop(0, count, visit, 0)


def place_rows(grad, keep, send, bits, at, rows):
    def one(p, block, out):
        out[p, at : at + rows, :] = grad[pl.ds(pl.multiple_of(block * rows, rows), rows), :].astype(BF16)

    for_slots(keep, send, bits, one)


def gated(tokens, at, place, length, gain, shift, glu_b, glu_w, first, joined, after_glu, second):
    part, width = tokens.shape

    def first_rows(r, c):
        vhat, _ = normalized(tokens[pl.ds(r, 64), :].astype(F32))
        first[pl.ds(pl.multiple_of(at + r, 64), 64), :] = (vhat * gain[0] + shift[0]).astype(BF16)
        return c

    row_blocks(part, 64, first_rows, unroll=2)
    every = pl.ds(at, part)
    for n in range(2 * width // TILE):
        joined[every, col(n)] = mm(first[every, :], glu_w[:, col(n)]) + glu_b[:, col(n)]

    def glu_rows(r, c):
        rows = pl.ds(pl.multiple_of(at + r, 32), 32)
        gate = jax.nn.sigmoid(joined[rows, width:])
        joined[rows, width:] = gate
        v = tokens[pl.ds(r, 32), :].astype(F32) + joined[rows, :width] * gate
        after_glu[rows, :] = v
        vhat, _ = normalized(v)
        valid = valid_rows(place + r, 32, length)
        second[rows, :] = ((vhat * gain[1] + shift[1]) * valid).astype(BF16)
        return c

    row_blocks(part, 32, glu_rows, unroll=2)


def open_kernel(lengths, far, first, joined, after_glu, second):
    mine, gains, shifts, glu_bias, glu_w, conv_w, left_w, point_w = far
    part = first.shape[0]
    tokens, gains, shifts = mine(), gains(), shifts()
    gain = [gains[k : k + 1, :].astype(F32) for k in range(2)]
    shift = [shifts[k : k + 1, :].astype(F32) for k in range(2)]
    place = lax.axis_index("head") * part
    glu_b, glu_w = vector(glu_bias()), glu_w()
    gated(tokens, 0, place, lengths[0], gain, shift, glu_b, glu_w, first, joined, after_glu, second)
    for get in (conv_w, left_w, point_w):
        get()


def forward_kernel(
    lengths,
    other,
    mine,
    own_first,
    own_joined,
    own_after_glu,
    own_second,
    glu_w,
    conv_w,
    left_w,
    point_w,
    far,
    out_tokens,
    stream,
    first,
    joined,
    after_glu,
    second,
    left_pre,
    right_pre,
    depth_low,
    after_conv,
    fourth,
    packed,
    probs,
    context,
    after_attn,
    fifth,
    hidden,
    third,
    sides,
):
    part, width = other.shape
    seq = 2 * part
    ffn = left_pre.shape[1]
    half = right_pre.shape[1]
    side = lax.axis_index("head")
    length = lengths[0]
    own = pl.ds(pl.multiple_of(side * part, part), part)
    opposite = pl.multiple_of((1 - side) * part, part)
    (
        gains,
        shifts,
        glu_bias,
        conv_bias,
        left_bias,
        mid_gain,
        mid_bias,
        depth_w,
        point_bias,
        qkv_w,
        out_w,
        ffn_in_bias,
        ffn_in_w,
        ffn_out_bias,
        ffn_out_w,
    ) = far
    for whole, piece in (
        (stream, mine),
        (first, own_first),
        (joined, own_joined),
        (after_glu, own_after_glu),
        (second, own_second),
    ):
        whole[own, :] = piece[...]
    stream[pl.ds(opposite, part), :] = other[...]
    gains, shifts = gains(), shifts()
    gain = [gains[k : k + 1, :].astype(F32) for k in range(4)]
    shift = [shifts[k : k + 1, :].astype(F32) for k in range(4)]
    gated(
        other, opposite, opposite, length, gain, shift, vector(glu_bias()), glu_w, first, joined, after_glu, second
    )
    blank = jnp.zeros((8, half), F32)
    for k in range(2):
        sides[k, 0:8, :] = blank
        sides[k, 8 + seq : 16 + seq, :] = blank
    sides[0, 8 : 8 + seq, :] = mm(second[...], conv_w[0])
    sides[1, 8 : 8 + seq, :] = mm(second[...], conv_w[2])
    right_pre[...] = mm(second[...], conv_w[1]) + vector(conv_bias())
    right_pre[...] = right_pre[...] + sides[0, 7 : 7 + seq, :] + sides[1, 9 : 9 + seq, :]
    left_b = vector(left_bias())
    for n in range(ffn // TILE):
        left_pre[:, col(n)] = mm(second[...], left_w[:, col(n)]) + left_b[:, col(n)]
    mid_g, mid_b, depth_w = vector(mid_gain()), vector(mid_bias()), depth_w()
    chunks = ffn // LANES
    edge = jnp.zeros((8, LANES), F32)
    for k in range(chunks):
        third[k, 0:8, :] = edge
        third[k, 8 + seq : 16 + seq, :] = edge

    def mid_rows(r, c):
        rows = pl.ds(r, 16)
        vhat, _ = normalized(combine(left_pre[rows, :], right_pre[rows, :]))
        v = (vhat * mid_g + mid_b) * valid_rows(r, 16, length)
        for k in range(chunks):
            third[k, pl.ds(pl.multiple_of(8 + r, 8), 16), :] = v[:, col(k, LANES)]
        return c

    row_blocks(seq, 16, mid_rows, unroll=2)

    def depth_lanes(k, c):
        lanes = pl.ds(pl.multiple_of(k * LANES, LANES), LANES)
        taps = depth_w[:, lanes].astype(F32)
        total = third[k, 4 : 4 + seq, :] * taps[0:1, :]
        for j in range(1, 9):
            total = total + third[k, 4 + j : 4 + j + seq, :] * taps[j : j + 1, :]
        depth_low[:, lanes] = total.astype(BF16)
        return c

    lax.fori_loop(0, chunks, depth_lanes, 0)
    after_conv[:, :half] = (
        after_glu[:, :half] + mm(depth_low[...], point_w[...]) + vector(point_bias())
    )
    after_conv[:, half:] = after_glu[:, half:]

    def fourth_rows(r, c):
        rows = pl.ds(r, 64)
        vhat, _ = normalized(after_conv[rows, :])
        fourth[rows, :] = (vhat * gain[2] + shift[2]).astype(BF16)
        return c

    row_blocks(seq, 64, fourth_rows, unroll=2)
    qkv_w = qkv_w()
    for n in range(3 * width // TILE):
        packed[:, col(n)] = mm(fourth[...], qkv_w[:, col(n)]).astype(BF16)

    low_lanes = lax.broadcasted_iota(jnp.int32, (1, LANES), 1) < HEAD_DIM
    scale = HEAD_DIM ** (-0.5)

    def head_pair(p, c):
        lanes = pl.ds(pl.multiple_of(p * LANES, LANES), LANES)
        q = packed[:, lanes].astype(F32) * scale
        k = packed[:, pl.ds(pl.multiple_of(width + p * LANES, LANES), LANES)]
        v = packed[:, pl.ds(pl.multiple_of(2 * width + p * LANES, LANES), LANES)]
        open_keys = lax.broadcasted_iota(jnp.int32, (seq, 1), 0) < length
        results = []
        for e in range(2):
            q_one = jnp.where(low_lanes if e == 0 else ~low_lanes, q, 0.0).astype(BF16)
            s = jnp.where(open_keys, mm_nt(k, q_one), -1000000000.0)
            raised = jnp.exp(s - jnp.max(s, axis=0, keepdims=True))
            chance = raised * (1.0 / jnp.sum(raised, axis=0, keepdims=True))
            probs[2 * p + e] = chance
            results.append(mm_tn(v, chance.astype(BF16)))
        both = jnp.concatenate([results[0][:HEAD_DIM], results[1][HEAD_DIM:]], axis=0)
        context[:, lanes] = both.T.astype(BF16)
        return c

    lax.fori_loop(0, width // LANES, head_pair, 0)
    out_w = out_w()
    for n in range(width // TILE):
        after_attn[:, col(n)] = after_conv[:, col(n)] + mm(context[...], out_w[:, col(n)])

    def fifth_rows(r, c):
        rows = pl.ds(r, 64)
        vhat, _ = normalized(after_attn[rows, :])
        fifth[rows, :] = (vhat * gain[3] + shift[3]).astype(BF16)
        return c

    row_blocks(seq, 64, fifth_rows, unroll=2)
    ffn_in_b, ffn_in_w = vector(ffn_in_bias()), ffn_in_w()
    for n in range(ffn // TILE):
        pre = mm(fifth[...], ffn_in_w[:, col(n)]) + ffn_in_b[:, col(n)]
        hidden[:, col(n)] = jnp.where(pre > 0.0, pre, 0.0).astype(BF16)
    ffn_out_b, ffn_out_w = vector(ffn_out_bias()), ffn_out_w()
    for n in range(width // TILE):
        out_tokens[:, col(n)] = (
            after_attn[own, col(n)]
            + mm(hidden[own, :], ffn_out_w[:, col(n)])
            + ffn_out_b[:, col(n)]
        ).astype(BF16)


def ffn_back_kernel(
    cot_other,
    after_attn,
    fifth,
    hidden,
    ffn_in_w,
    ffn_out_w,
    far,
    d_after,
    small,
    keep,
    send,
    cot,
    d_hidden,
    d_fifth,
    grad,
):
    seq, width = fifth.shape
    part = seq // 2
    ffn = hidden.shape[1]
    side = lax.axis_index("head")
    cot_mine, gains = far
    own = pl.ds(pl.multiple_of(side * part, part), part)
    opposite = pl.ds(pl.multiple_of((1 - side) * part, part), part)
    cot[opposite, :] = cot_other[...]
    cot[own, :] = cot_mine()[...]
    for n in range(ffn // TILE):
        back = mm_nt(cot[...], ffn_out_w[col(n), :])
        back = jnp.where(hidden[:, col(n)].astype(F32) > 0.0, back, 0.0).astype(BF16)
        d_hidden[:, col(n)] = back
        small[0:1, col(n)] = sum_tokens(back.astype(F32))
    for n in range(width // TILE):
        d_fifth[:, col(n)] = mm_nt(d_hidden[...], ffn_in_w[col(n), :])

    cot_half = cot[:, pl.ds(pl.multiple_of(side * (width // 2), width // 2), width // 2)]
    per_row = ffn // GROUPS
    gain = gains()[3:4, :].astype(F32)
    sums = [jnp.zeros((8, width), F32)] * 3
    for p in range(GROUPS // 2):
        block = slice(p * seq // 8, (p + 1) * seq // 8)
        vhat, rate = normalized(after_attn[block, :])
        e = d_fifth[block, :]
        given = cot[block, :].astype(F32)
        d_after[block, :] = given + norm_back(vhat, rate, e * gain)
        sums = [total + part_sums(v) for total, v in zip(sums, (e * vhat, e, given))]
        count = GROUPS // 2 // len(send)
        for sent, out, place in ((0, keep, p), (1, send[p // count], p % count)):
            at = pl.multiple_of(slot_block(p, sent, FFN_BITS) * per_row, per_row)
            out[place, 0:per_row, :] = mm_tn(hidden[:, pl.ds(at, per_row)], cot_half).astype(BF16)
    for k in range(3):
        small[1:2, k * width : (k + 1) * width] = sum_tokens(sums[k])

    rows = width // GROUPS
    for j in range(ffn // 2 // TILE):
        at = pl.multiple_of(side * (ffn // 2) + j * TILE, TILE)
        grad[...] = mm_tn(fifth[...], d_hidden[:, pl.ds(at, TILE)])
        place_rows(grad, keep, send, FFN_BITS, per_row + j * rows, rows)


def combine(left_pre, right_pre):
    half = right_pre.shape[1]
    left = jnp.maximum(left_pre, 0.0)
    return jnp.concatenate([left[:, :half] + jnp.maximum(right_pre, 0.0), left[:, half:]], axis=1)


def attention_back_kernel(
    d_after,
    packed,
    probs,
    context,
    fourth,
    after_conv,
    depth_low,
    out_w,
    qkv_w,
    far,
    d_after_conv,
    small,
    keep,
    send,
    d_attn,
    d_context,
    d_packed,
    d_fourth,
    d_sep,
    grad,
):
    seq, width = d_after.shape
    side = lax.axis_index("head")
    (gains,) = far
    half = d_sep.shape[1]
    ffn = depth_low.shape[1]
    rows = width // GROUPS
    d_attn[...] = d_after[...].astype(BF16)
    for n in range(width // TILE):
        d_context[:, col(n)] = mm_nt(d_attn[...], out_w[col(n), :]).astype(BF16)
    low_lanes = lax.broadcasted_iota(jnp.int32, (1, LANES), 1) < HEAD_DIM
    scale = HEAD_DIM ** (-0.5)

    def head_pair(p, c):
        lanes = pl.ds(pl.multiple_of(p * LANES, LANES), LANES)
        k_lanes = pl.ds(pl.multiple_of(width + p * LANES, LANES), LANES)
        v_lanes = pl.ds(pl.multiple_of(2 * width + p * LANES, LANES), LANES)
        q = packed[:, lanes]
        k = packed[:, k_lanes]
        v = packed[:, v_lanes].astype(F32)
        given = d_context[:, lanes]
        dq, dk, dv = [], [], []
        for e in range(2):
            one = jnp.where(low_lanes if e == 0 else ~low_lanes, v, 0.0).astype(BF16)
            chance = probs[2 * p + e]
            d_probs = mm_nt(one, given)
            delta = jnp.sum(d_probs * chance, axis=0, keepdims=True)
            d_scores = (chance * (d_probs - delta)).astype(BF16)
            dv.append(mm(chance.astype(BF16), given))
            dk.append(mm(d_scores, q))
            dq.append(mm_tn(k, d_scores))
        both = jnp.concatenate([dq[0][:HEAD_DIM], dq[1][HEAD_DIM:]], axis=0)
        d_packed[:, lanes] = (both.T * scale).astype(BF16)
        d_packed[:, k_lanes] = (jnp.where(low_lanes, dk[0], dk[1]) * scale).astype(BF16)
        d_packed[:, v_lanes] = jnp.where(low_lanes, dv[0], dv[1]).astype(BF16)
        return c

    lax.fori_loop(0, width // LANES, head_pair, 0)
    for n in range(width // TILE):
        d_fourth[:, col(n)] = mm_nt(d_packed[...], qkv_w[col(n), :])
    gain = gains()[2:3, :].astype(F32)

    sums = [jnp.zeros((8, width), F32)] * 2
    g_point = jnp.zeros((8, half), F32)
    at = pl.multiple_of(side * (width // 2), width // 2)
    sides = [(context, d_attn, at)]
    for j in range(3 * width // 2 // TILE):
        sides.append((fourth, d_packed, pl.multiple_of(side * (3 * width // 2) + j * TILE, TILE)))
    for p in range(2 * len(sides)):
        block = slice(p * seq // 8, (p + 1) * seq // 8)
        vhat, rate = normalized(after_conv[block, :])
        e = d_fourth[block, :]
        total = d_after[block, :] + norm_back(vhat, rate, e * gain)
        d_after_conv[block, :] = total
        sep = total[:, :half].astype(BF16)
        d_sep[block, :] = sep
        sums = [total + part_sums(v) for total, v in zip(sums, (e * vhat, e))]
        g_point = g_point + part_sums(sep.astype(F32))
        values, incoming, at = sides[p // 2]
        part = slice(p % 2 * (width // 2), (p % 2 + 1) * (width // 2))
        grad[p // 2, part, :] = mm_tn(values[:, part], incoming[:, pl.ds(at, TILE)])
    small[0:1, 0:width] = sum_tokens(sums[0])
    small[0:1, width : 2 * width] = sum_tokens(sums[1])
    small[0:1, 2 * width : 2 * width + half] = sum_tokens(g_point)
    for j in range(len(sides)):
        place_rows(grad.at[j], keep, send, ATTN_BITS, j * rows, rows)
    sep_half = d_sep[:, pl.ds(pl.multiple_of(side * (half // 2), half // 2), half // 2)]
    per_row = ffn // GROUPS

    def point_slot(p, block, out):
        g = mm_tn(
            depth_low[:, pl.ds(pl.multiple_of(block * per_row, per_row), per_row)], sep_half
        ).astype(BF16)
        out[p, 4 * rows : 4 * rows + per_row // 2, 0:LANES] = g[: per_row // 2]
        out[p, 4 * rows : 4 * rows + per_row // 2, LANES : 2 * LANES] = g[per_row // 2 :]

    for_slots(keep, send, ATTN_BITS, point_slot)


def middle_back_kernel(
    lengths,
    d_after_conv,
    left_pre,
    right_pre,
    point_w,
    far,
    d_left,
    taps_right,
    small,
    vhat3,
    third,
    d_depth,
    d_third,
    rates,
    sums,
    d_right,
    mid_row,
):
    seq, width = d_after_conv.shape
    ffn = left_pre.shape[1]
    half = right_pre.shape[1]
    length = lengths[0]
    mid_gain, mid_bias, depth_w = far
    chunks = ffn // LANES
    edge = jnp.zeros((8, LANES), F32)
    for k in range(chunks):
        d_depth[k, 0:8, :] = edge
        d_depth[k, 8 + seq : 16 + seq, :] = edge
    d_sep = d_after_conv[:, :half].astype(BF16)
    for n in range(ffn // TILE):
        block = mm_nt(d_sep, point_w[col(n), :])
        for m in range(TILE // LANES):
            d_depth[n * (TILE // LANES) + m, 8 : 8 + seq, :] = block[:, col(m, LANES)]

    mid_g, mid_b, depth_w = vector(mid_gain()), vector(mid_bias()), depth_w()
    mid_row[...] = mid_g

    def mid_rows(r, c):
        rows = pl.ds(r, 16)
        vhat, rate = normalized(combine(left_pre[rows, :], right_pre[rows, :]))
        v = (vhat * mid_g + mid_b) * valid_rows(r, 16, length)
        rates[rows, :] = jnp.broadcast_to(rate, (16, LANES))
        for k in range(chunks):
            third[k, rows, :] = v[:, col(k, LANES)]
            vhat3[k, rows, :] = vhat[:, col(k, LANES)]
        return c

    row_blocks(seq, 16, mid_rows, unroll=2)
    sums[...] = jnp.zeros(sums.shape, F32)
    step = 64

    def depth_lanes(k, c):
        lanes = pl.ds(pl.multiple_of(k * LANES, LANES), LANES)
        taps = depth_w[:, lanes].astype(F32)
        mid_lanes = mid_row[0:1, lanes]
        totals = [jnp.zeros((8, LANES), F32)] * 11
        for r in range(0, seq, step):
            block = slice(r, r + step)
            here = third[k, block, :]
            total = None
            for j in range(9):
                moved = d_depth[k, 12 - j + r : 12 - j + r + step, :]
                totals[j] = totals[j] + part_sums(moved * here)
                term = moved * taps[j : j + 1, :]
                total = term if total is None else total + term
            total = total * valid_rows(r, step, length)
            vhat = vhat3[k, block, :]
            totals[9] = totals[9] + part_sums(total * vhat)
            totals[10] = totals[10] + part_sums(total)
            gained = total * mid_lanes
            d_third[k, block, :] = gained
            sums[0, block, :] = sums[0, block, :] + gained
            sums[1, block, :] = sums[1, block, :] + gained * vhat
        for j in range(11):
            small[j : j + 1, lanes] = sum_tokens(totals[j])
        return c

    lax.fori_loop(0, chunks, depth_lanes, 0)
    inverse = 1.0 / ffn
    sums[0] = jnp.broadcast_to(jnp.sum(sums[0], axis=-1, keepdims=True) * inverse, (seq, LANES))
    sums[1] = jnp.broadcast_to(jnp.sum(sums[1], axis=-1, keepdims=True) * inverse, (seq, LANES))

    def combined_lanes(k):
        return (d_third[k] - sums[0] - vhat3[k] * sums[1]) * rates[...]

    def left_lanes(k, c):
        lanes = pl.ds(pl.multiple_of(k * LANES, LANES), LANES)
        v = jnp.where(left_pre[:, lanes] > 0.0, combined_lanes(k), 0.0).astype(BF16)
        d_left[:, lanes] = v
        small[11:12, lanes] = sum_tokens(v.astype(F32))
        return c

    lax.fori_loop(0, chunks, left_lanes, 0)
    blank = jnp.zeros((8, half), F32)
    d_right[0:8, :] = blank
    d_right[8 + seq : 16 + seq, :] = blank
    for k in range(half // LANES):
        v = jnp.where(right_pre[:, col(k, LANES)] > 0.0, combined_lanes(k), 0.0).astype(BF16)
        v = v.astype(F32)
        d_right[8 : 8 + seq, col(k, LANES)] = v
        small[12:13, col(k, LANES)] = sum_tokens(v)
    taps_right[0] = d_right[9 : 9 + seq, :].astype(BF16)
    taps_right[1] = d_right[8 : 8 + seq, :].astype(BF16)
    taps_right[2] = d_right[7 : 7 + seq, :].astype(BF16)


def conv_back_kernel(
    lengths,
    d_left,
    taps_right,
    second,
    left_w,
    conv_w,
    far,
    d_second,
    keep,
    send,
    grad,
    grad_conv,
):
    seq, width = d_second.shape
    ffn = d_left.shape[1]
    half = taps_right.shape[2]
    side = lax.axis_index("head")
    valid = valid_rows(0, seq, lengths[0])
    rows = width // GROUPS
    for j in range(ffn // 2 // TILE):
        at = pl.multiple_of(side * (ffn // 2) + j * TILE, TILE)
        grad[...] = mm_tn(second[...], d_left[:, pl.ds(at, TILE)])
        place_rows(grad, keep, send, CONV_BITS, j * rows, rows)
    start = ffn // 2 // TILE * rows
    half_lanes = pl.ds(pl.multiple_of(side * (half // 2), half // 2), half // 2)
    for tap in range(3):
        grad_conv[tap] = mm_tn(second[...], taps_right[tap, :, half_lanes])

    def conv_slot(p, block, out):
        at = pl.multiple_of(block * rows, rows)
        middle = pl.multiple_of(block * rows + rows // 2, rows // 2)
        h = rows // 2
        out[p, start : start + rows, 0:LANES] = grad_conv[0, pl.ds(at, rows), :].astype(BF16)
        out[p, start + rows : start + rows + h, 0:LANES] = grad_conv[1, pl.ds(at, h), :].astype(BF16)
        out[p, start : start + h, LANES : 2 * LANES] = grad_conv[1, pl.ds(middle, h), :].astype(BF16)
        out[p, start + h : start + h + rows, LANES : 2 * LANES] = grad_conv[
            2, pl.ds(at, rows), :
        ].astype(BF16)

    for_slots(keep, send, CONV_BITS, conv_slot)
    for n in range(width // TILE):
        total = mm_nt(d_left[...], left_w[col(n), :])
        for tap in range(3):
            total = total + mm_nt(taps_right[tap], conv_w[tap, col(n), :])
        d_second[:, col(n)] = total * valid


def glu_back_kernel(
    d_second,
    d_after_conv,
    after_glu,
    joined,
    first,
    stream,
    small_ffn,
    small_attn,
    small_conv,
    glu_w,
    far,
    grad_tokens,
    keep,
    send,
    d_joined,
    d_after_glu,
    d_first,
    rolled,
    blocks,
    grad,
):
    seq, width = d_second.shape
    part = seq // 2
    side = lax.axis_index("head")
    gains = far[0]()
    gain = [gains[k : k + 1, :].astype(F32) for k in range(2)]

    def glu_rows(r, c):
        g_gain, g_shift, g_value, g_gate = c
        rows = pl.ds(r, 32)
        vhat, rate = normalized(after_glu[rows, :])
        e = d_second[rows, :]
        total = d_after_conv[rows, :] + norm_back(vhat, rate, e * gain[1])
        d_after_glu[rows, :] = total
        value = joined[rows, :width]
        gate = joined[rows, width:]
        d_value = (total * gate).astype(BF16)
        d_gate = (total * value * gate * (1.0 - gate)).astype(BF16)
        d_joined[rows, :width] = d_value
        d_joined[rows, width:] = d_gate
        return (
            g_gain + part_sums(e * vhat),
            g_shift + part_sums(e),
            g_value + part_sums(d_value.astype(F32)),
            g_gate + part_sums(d_gate.astype(F32)),
        )

    nothing = jnp.zeros((8, width), F32)
    sums = row_blocks(seq, 32, glu_rows, (nothing,) * 4, unroll=2)
    gain_one, shift_one, g_value, g_gate = (sum_tokens(v) for v in sums)
    for n in range(width // TILE):
        d_first[:, col(n)] = mm_nt(d_joined[...], glu_w[col(n), :])

    sums = [nothing] * 2
    rows = width // GROUPS
    columns = [pl.ds(pl.multiple_of(side * width + j * TILE, TILE), TILE) for j in range(width // TILE)]
    for p in range(8):
        block = slice(p * seq // 8, (p + 1) * seq // 8)
        vhat, rate = normalized(stream[block, :].astype(F32))
        e = d_first[block, :]
        d_after_glu[block, :] = d_after_glu[block, :] + norm_back(vhat, rate, e * gain[0])
        sums = [total + part_sums(v) for total, v in zip(sums, (e * vhat, e))]
        if p < 2 * len(columns):
            part_rows = slice(p % 2 * (width // 2), (p % 2 + 1) * (width // 2))
            grad[p // 2, part_rows, :] = mm_tn(first[:, part_rows], d_joined[:, columns[p // 2]])
    gain_zero, shift_zero = (sum_tokens(v) for v in sums)
    grad_tokens[...] = d_after_glu[pl.ds(pl.multiple_of(side * part, part), part), :]
    for j in range(len(columns)):
        place_rows(grad.at[j], keep, send, GLU_BITS, j * rows, rows)

    blocks[...] = jnp.zeros(blocks.shape, F32)
    rolled[...] = jnp.zeros(rolled.shape, F32)
    vectors = (
        (gain_zero, gain_one, small_attn[0:1, 0:width], small_ffn[1:2, 0:width]),
        (shift_zero, shift_one, small_attn[0:1, width : 2 * width], small_ffn[1:2, width : 2 * width]),
    )
    tiles = width // LANES
    lane = lax.broadcasted_iota(jnp.int32, (8, LANES), 1)
    quarter = LANES // tiles
    for kind, four in enumerate(vectors):
        for k, vector in enumerate(four):
            for t in range(tiles):
                rolled[kind, 8 * k + t : 8 * k + t + 1, :] = vector[:, col(t, LANES)]
        for q in range(tiles):
            total = jnp.zeros((8, LANES), F32)
            for k in range(4):
                moved = pltpu.roll(rolled[kind, 8 * k : 8 * k + 8, :], (quarter * (k - q)) % LANES, 1)
                total = jnp.where((lane >= quarter * k) & (lane < quarter * (k + 1)), moved, total)
            for t in range(tiles):
                blocks[tiles * t + q, 13 + kind : 14 + kind, 0:LANES] = total[t : t + 1, :]
    lane = lane[0:1, :]
    g_out = small_ffn[1:2, 2 * width : 3 * width]
    for s in range(GROUPS):
        source = g_value if s < GROUPS // 2 else g_gate
        place = (s % (GROUPS // 2)) * (2 * width // GROUPS)
        block = source[:, place // LANES * LANES : place // LANES * LANES + LANES]
        glu_part = block if place % LANES == 0 else pltpu.roll(block, LANES - place % LANES, 1)
        place = s * (width // GROUPS)
        block = g_out[:, place // LANES * LANES : place // LANES * LANES + LANES]
        moved = (LANES // 2 - place % LANES) % LANES
        out_part = block if moved == 0 else pltpu.roll(block, moved, 1)
        blocks[s, 15:16, 0:LANES] = jnp.where(
            lane < LANES // 2, glu_part, jnp.where(lane < LANES // 2 + quarter, out_part, 0.0)
        )
        blocks[s, 0:12, 0:LANES] = small_conv[0:12, col(s, LANES)]
        blocks[s, 12:13, 0:LANES] = small_ffn[0:1, col(s, LANES)]
        for k in range(2):
            blocks[s, k : k + 1, LANES : 2 * LANES] = small_conv[12:13, col(k, LANES)]
            blocks[s, 2 + k : 3 + k, LANES : 2 * LANES] = small_attn[
                0:1, 2 * width + k * LANES : 2 * width + (k + 1) * LANES
            ]
    start = width // TILE * rows

    def small_slot(p, block, out):
        out[p, start : start + 16, :] = blocks[block].astype(BF16)

    for_slots(keep, send, GLU_BITS, small_slot)


def add_kernel(keeps, gots, far, keep, send):
    at = 0
    for kept, got in zip(keeps, gots):
        rows = kept.shape[1]
        half = kept.shape[0] // 2
        count = kept.shape[0] // len(got)
        for i in range(kept.shape[0]):
            total = kept[i].astype(F32) + got[i // count][i % count].astype(F32)
            out = keep if i < half else send
            out[i % half, at : at + rows, :] = total.astype(BF16)
        at += rows


def finish_early_kernel(mine, other, far, ffn_out, ffn_in, out, qkv, point):
    side = lax.axis_index("head")
    per_row, width = ffn_out.shape
    rows = ffn_in.shape[0]
    for who, grads in ((side, mine), (1 - side, other)):
        count = ffn_in.shape[1] // 2 // TILE
        at = pl.ds(pl.multiple_of(who * TILE, TILE), TILE)
        start = per_row + count * rows
        ffn_out[:, at] = grads[0:per_row, :].astype(F32)
        out[:, at] = grads[start : start + rows, :].astype(F32)
        for j in range(count):
            at = pl.ds(pl.multiple_of((who * count + j) * TILE, TILE), TILE)
            ffn_in[:, at] = grads[per_row + j * rows : per_row + (j + 1) * rows, :].astype(F32)
        count = qkv.shape[1] // 2 // TILE
        for j in range(count):
            at = pl.ds(pl.multiple_of((who * count + j) * TILE, TILE), TILE)
            qkv[:, at] = grads[start + (1 + j) * rows : start + (2 + j) * rows, :].astype(F32)
        start = start + (1 + count) * rows
        at = pl.ds(pl.multiple_of(who * LANES, LANES), LANES)
        point[0 : per_row // 2, at] = grads[start : start + per_row // 2, 0:LANES].astype(F32)
        point[per_row // 2 :, at] = grads[start : start + per_row // 2, LANES : 2 * LANES].astype(F32)


def finish_late_kernel(
    mine,
    other,
    far,
    left,
    conv,
    glu,
    gains,
    shifts,
    depth,
    mid_gain,
    mid_bias,
    left_bias,
    ffn_in_bias,
    glu_bias,
    ffn_out_bias,
    conv_bias,
    point_bias,
):
    side = lax.axis_index("head")
    rows = glu.shape[0]
    h = rows // 2
    count = left.shape[1] // 2 // TILE
    behind = count * rows + 3 * h
    wide = glu.shape[1] // 2 // TILE
    for who, grads in ((side, mine), (1 - side, other)):
        for j in range(count):
            at = pl.ds(pl.multiple_of((who * count + j) * TILE, TILE), TILE)
            left[:, at] = grads[j * rows : (j + 1) * rows, :].astype(F32)
        start = count * rows
        at = pl.ds(pl.multiple_of(who * LANES, LANES), LANES)
        low = grads[start : start + 3 * h, 0:LANES].astype(F32)
        high = grads[start : start + 3 * h, LANES : 2 * LANES].astype(F32)
        conv[0, :, at] = low[0:rows]
        conv[1, 0:h, at] = low[rows:]
        conv[1, h:rows, at] = high[0:h]
        conv[2, :, at] = high[h:]
        for j in range(wide):
            at = pl.ds(pl.multiple_of((who * wide + j) * TILE, TILE), TILE)
            glu[:, at] = grads[behind + j * rows : behind + (j + 1) * rows, :].astype(F32)
    start = behind + wide * rows
    block = mine[start : start + 16, :].astype(F32)
    depth[...] = block[0:9, 0:LANES]
    for k in range(4):
        gains[k : k + 1, :] = block[13:14, k * rows : (k + 1) * rows]
        shifts[k : k + 1, :] = block[14:15, k * rows : (k + 1) * rows]
    mid_gain[...] = block[9, 0:LANES]
    mid_bias[...] = block[10, 0:LANES]
    left_bias[...] = block[11, 0:LANES]
    ffn_in_bias[...] = block[12, 0:LANES]
    glu_bias[...] = block[15, 0 : 2 * rows]
    ffn_out_bias[...] = block[15, 2 * rows : 3 * rows]
    for k in range(2):
        conv_bias[col(k, LANES)] = block[k, LANES : 2 * LANES]
        point_bias[col(k, LANES)] = block[2 + k, LANES : 2 * LANES]


def call(kernel, outs, scratch, near, far, micros=0, scalars=0, kept=()):
    smem = pl.BlockSpec(memory_space=pltpu.SMEM)
    vmem = pl.BlockSpec(memory_space=pltpu.VMEM)
    anywhere = pl.BlockSpec(memory_space=pltpu.HBM)

    near, inside = jax.tree.flatten(near)
    outs, outside = jax.tree.flatten(outs, is_leaf=lambda v: isinstance(v, tuple))
    own = len(outs)
    outs = outs + [(far[i].shape, far[i].dtype) for i in kept]

    def body(*refs):
        inputs = inside.unflatten(refs[: len(near)])
        sources = refs[len(near) : len(near) + len(far)]
        first = len(near) + len(far)
        results = outside.unflatten(refs[first : first + own])
        held = refs[first + own : first + len(outs)]
        rest = refs[first + len(outs) :]
        if not far:
            kernel(*inputs, (), *results, *rest)
            return
        *rest, done = rest
        fresh = iter(rest[len(scratch) :])
        buffers = [held[kept.index(i)] if i in kept else next(fresh) for i in range(len(far))]
        copies = [
            pltpu.make_async_copy(source, buffer, done.at[i])
            for i, (source, buffer) in enumerate(zip(sources, buffers))
        ]
        for copy in copies:
            copy.start()

        def fetched(copy, buffer):
            def get():
                copy.wait()
                return buffer

            return get

        kernel(*inputs, tuple(map(fetched, copies, buffers)), *results, *rest[: len(scratch)])

    temporaries = [pltpu.VMEM(shape, dtype) for shape, dtype in scratch]
    if far:
        temporaries += [pltpu.VMEM(v.shape, v.dtype) for i, v in enumerate(far) if i not in kept]
        temporaries.append(pltpu.SemaphoreType.DMA((len(far),)))
    results = pl.pallas_call(
        body,
        out_shape=tuple(jax.ShapeDtypeStruct(shape, dtype) for shape, dtype in outs),
        in_specs=[smem] * scalars + [vmem] * (len(near) - scalars) + [anywhere] * len(far),
        out_specs=(vmem,) * len(outs),
        scratch_shapes=temporaries,
        compiler_params=pltpu.CompilerParams(vmem_limit_bytes=VMEM_BYTES),
        cost_estimate=pl.CostEstimate(
            flops=micros * 10**9, transcendentals=0, bytes_accessed=micros * 3 * 10**6
        ),
        name=kernel.__name__,
    )(*near, *[pltpu.with_memory_space_constraint(v, pltpu.HBM) for v in far])
    return [*outside.unflatten(results[:own]), *results[own:]]


def per_device(
    tokens,
    lengths,
    cotangent,
    glu_weight,
    glu_bias,
    norm_gain,
    norm_bias,
    mid_gain,
    mid_bias,
    left_weight,
    left_bias,
    conv_weight,
    conv_bias,
    depth_weight,
    point_weight,
    point_bias,
    qkv_weight,
    out_weight,
    ffn_in_weight,
    ffn_in_bias,
    ffn_out_weight,
    ffn_out_bias,
):
    row_count, part, width = tokens.shape
    assert row_count == 1 and lax.axis_size("head") == 2
    seq = 2 * part
    shards = lax.axis_size("dp")
    below = shards // GROUPS
    assert below * GROUPS == shards
    heads = width // HEAD_DIM
    half = conv_weight.shape[2]
    ffn = left_weight.shape[1]
    swap = [(0, 1), (1, 0)]
    mine = tokens[0]
    cot_mine = cotangent[0]
    other = lax.ppermute(mine, "head", swap)
    cot_other = lax.ppermute(cot_mine, "head", swap)

    def slot_outs(rows, pieces=1):
        count = GROUPS // 2
        return [((count, rows, TILE), BF16), [((count // pieces, rows, TILE), BF16)] * pieces]

    rows = width // GROUPS
    per_row = ffn // GROUPS
    ffn_rows = per_row + ffn // 2 // TILE * rows
    own_first, own_joined, own_after_glu, own_second, mine, glu_w, conv_w, left_w, point_w = call(
        open_kernel,
        [
            ((part, width), BF16),
            ((part, 2 * width), F32),
            ((part, width), F32),
            ((part, width), BF16),
        ],
        [],
        [lengths],
        [mine, norm_gain, norm_bias, glu_bias, glu_weight, conv_weight, left_weight, point_weight],
        micros=1,
        scalars=1,
        kept=(0, 4, 5, 6, 7),
    )
    (
        out_tokens,
        stream,
        first_norm,
        joined,
        after_glu,
        second,
        left_pre,
        right_pre,
        depth_low,
        after_conv,
        fourth,
        packed,
        probs,
        context,
        after_attn,
        fifth,
        hidden,
        qkv_w,
        out_w,
        ffn_in_w,
        ffn_out_w,
    ) = call(
        forward_kernel,
        [
            ((part, width), BF16),
            ((seq, width), BF16),
            ((seq, width), BF16),
            ((seq, 2 * width), F32),
            ((seq, width), F32),
            ((seq, width), BF16),
            ((seq, ffn), F32),
            ((seq, half), F32),
            ((seq, ffn), BF16),
            ((seq, width), F32),
            ((seq, width), BF16),
            ((seq, 3 * width), BF16),
            ((heads, seq, seq), F32),
            ((seq, width), BF16),
            ((seq, width), F32),
            ((seq, width), BF16),
            ((seq, ffn), BF16),
        ],
        [
            ((ffn // LANES, seq + 16, LANES), F32),
            ((2, seq + 16, half), F32),
        ],
        [
            lengths,
            other,
            mine,
            own_first,
            own_joined,
            own_after_glu,
            own_second,
            glu_w,
            conv_w,
            left_w,
            point_w,
        ],
        [
            norm_gain,
            norm_bias,
            glu_bias,
            conv_bias,
            left_bias,
            mid_gain,
            mid_bias,
            depth_weight,
            point_bias,
            qkv_weight,
            out_weight,
            ffn_in_bias,
            ffn_in_weight,
            ffn_out_bias,
            ffn_out_weight,
        ],
        micros=14,
        scalars=1,
        kept=(9, 10, 12, 14),
    )
    d_after, small_ffn, keep_ffn, send_ffn = call(
        ffn_back_kernel,
        [((seq, width), F32), ((8, ffn), F32)] + slot_outs(ffn_rows),
        [
            ((seq, width), BF16),
            ((seq, ffn), BF16),
            ((seq, width), F32),
            ((width, TILE), F32),
        ],
        [cot_other, after_attn, fifth, hidden, ffn_in_w, ffn_out_w],
        [cot_mine, norm_gain],
        micros=5,
    )

    class Chunk:
        def __init__(self, keep, send, bits):
            self.keep, self.send, self.bits = keep, send, list(bits)

        def start(self):
            if not self.bits:
                self.got = [lax.ppermute(self.keep, "head", swap)]
                return
            step = below << self.bits.pop(0)
            pairs = [(i, i ^ step) for i in range(shards)]
            self.got = [lax.ppermute(v, "dp", pairs) for v in self.send]

    def last_sum(keep, got):
        total = (keep[0].astype(F32) + got[0].astype(F32)).astype(BF16)
        step = 1
        while step < below:
            total = total + lax.ppermute(total, "dp", [(i, i ^ step) for i in range(shards)])
            step *= 2
        return total

    def added(*chunks):
        keep = chunks[0].keep
        if keep.shape[0] == 1:
            return last_sum(keep, chunks[0].got[0]), None
        if len(chunks) == 1 and len(chunks[0].got) < 3:
            (c,) = chunks
            n = keep.shape[0] // 2
            got = c.got if len(c.got) == 2 else (c.got[0][:n], c.got[0][n:])
            return tuple(
                (keep[half * n : half * n + n].astype(F32) + got[half].astype(F32)).astype(BF16)
                for half in range(2)
            )
        shape = ((keep.shape[0] // 2, sum(c.keep.shape[1] for c in chunks), TILE), BF16)
        return call(
            add_kernel, [shape, shape], [], [[c.keep for c in chunks], [c.got for c in chunks]], []
        )

    def received(held, *chunks):
        held, gots = lax.optimization_barrier((held, [c.got for c in chunks]))
        for c, got in zip(chunks, gots):
            c.got = got
        return held

    def wave(held, *chunks, joined=False):
        held = received(held, *chunks)
        groups = [chunks] if joined else [(c,) for c in chunks]
        nexts = [Chunk(*added(*group), group[0].bits) for group in groups]
        held, keeps = lax.optimization_barrier((held, [(c.keep, c.send) for c in nexts]))
        for c, (keep, send) in zip(nexts, keeps):
            c.keep, c.send = keep, [send]
            c.start()
        return (held, *nexts)

    ffn_grads = Chunk(keep_ffn, send_ffn, (0, *FFN_BITS))
    ffn_grads.start()
    d_after_conv, small_attn, keep_attn, send_attn = call(
        attention_back_kernel,
        [((seq, width), F32), ((8, ffn), F32)] + slot_outs(4 * rows + per_row // 2),
        [
            ((seq, width), BF16),
            ((seq, width), BF16),
            ((seq, 3 * width), BF16),
            ((seq, width), F32),
            ((seq, half), BF16),
            ((4, width, TILE), F32),
        ],
        [d_after, packed, probs, context, fourth, after_conv, depth_low, out_w, qkv_w],
        [norm_gain],
        micros=10,
    )
    d_after_conv, ffn_grads = wave(d_after_conv, ffn_grads)
    attn_grads = Chunk(keep_attn, send_attn, (0, *ATTN_BITS))
    attn_grads.start()
    d_after_conv, attn_grads = wave(d_after_conv, attn_grads)
    d_left, taps_right, small_conv = call(
        middle_back_kernel,
        [((seq, ffn), BF16), ((3, seq, half), BF16), ((16, ffn), F32)],
        [
            ((ffn // LANES, seq, LANES), F32),
            ((ffn // LANES, seq, LANES), F32),
            ((ffn // LANES, seq + 16, LANES), F32),
            ((ffn // LANES, seq, LANES), F32),
            ((seq, LANES), F32),
            ((2, seq, LANES), F32),
            ((seq + 16, half), F32),
            ((1, ffn), F32),
        ],
        [lengths, d_after_conv, left_pre, right_pre, point_w],
        [mid_gain, mid_bias, depth_weight],
        micros=4,
        scalars=1,
    )
    d_left, ffn_grads, attn_grads = wave(d_left, ffn_grads, attn_grads)
    d_second, keep_conv, send_conv = call(
        conv_back_kernel,
        [((seq, width), F32)] + slot_outs(ffn // 2 // TILE * rows + 3 * rows // 2, 1),
        [((width, TILE), F32), ((3, width, LANES), F32)],
        [lengths, d_left, taps_right, second, left_w, conv_w],
        [],
        micros=5,
        scalars=1,
    )
    conv_grads = Chunk(keep_conv, send_conv, (0, *CONV_BITS))
    conv_grads.start()
    d_second, conv_grads = wave(d_second, conv_grads)
    grad_tokens, keep_glu, send_glu = call(
        glu_back_kernel,
        [((part, width), F32)] + slot_outs(width // TILE * rows + 16, 2),
        [
            ((seq, 2 * width), BF16),
            ((seq, width), F32),
            ((seq, width), F32),
            ((2, 32, LANES), F32),
            ((GROUPS, 16, 2 * LANES), F32),
            ((width // TILE, width, TILE), F32),
        ],
        [
            d_second,
            d_after_conv,
            after_glu,
            joined,
            first_norm,
            stream,
            small_ffn,
            small_attn,
            small_conv,
            glu_w,
        ],
        [norm_gain],
        micros=7,
    )
    glu_grads = Chunk(keep_glu, send_glu, (0, *GLU_BITS))
    glu_grads.start()
    held = received(grad_tokens, ffn_grads, attn_grads)
    held, glu_grads = wave(held, glu_grads)
    held, early = wave(held, ffn_grads, attn_grads, joined=True)
    held, conv_grads = wave(held, conv_grads)
    held, glu_grads = wave(held, glu_grads)
    held, late = wave(held, conv_grads, glu_grads, joined=True)
    held, early = wave(held, early)
    grad_tokens, late = wave(held, late)
    other = early.got[0]
    ffn_out, ffn_in, out, qkv, point = call(
        finish_early_kernel,
        [
            ((per_row, width), F32),
            ((rows, ffn), F32),
            ((rows, width), F32),
            ((rows, 3 * width), F32),
            ((per_row, half), F32),
        ],
        [],
        [early.keep, other],
        [],
    )
    (
        left,
        conv,
        glu,
        g_gains,
        g_shifts,
        g_depth,
        g_mid_gain,
        g_mid_bias,
        g_left_bias,
        g_ffn_in_bias,
        g_glu_bias,
        g_ffn_out_bias,
        g_conv_bias,
        g_point_bias,
    ) = call(
        finish_late_kernel,
        [
            ((rows, ffn), F32),
            ((3, rows, half), F32),
            ((rows, 2 * width), F32),
            ((4, rows), F32),
            ((4, rows), F32),
            ((9, LANES), F32),
            ((LANES,), F32),
            ((LANES,), F32),
            ((LANES,), F32),
            ((LANES,), F32),
            ((2 * rows,), F32),
            ((rows,), F32),
            ((half,), F32),
            ((half,), F32),
        ],
        [],
        [late.keep, late.got[0]],
        [],
    )
    results = (
        (glu, 0),
        (g_glu_bias, 0),
        (g_gains, 1),
        (g_shifts, 1),
        (g_mid_gain, 0),
        (g_mid_bias, 0),
        (left, 0),
        (g_left_bias, 0),
        (conv, 1),
        (g_conv_bias, None),
        (g_depth, 1),
        (point, 0),
        (g_point_bias, None),
        (qkv, 0),
        (out, 0),
        (ffn_in, 0),
        (g_ffn_in_bias, 0),
        (ffn_out, 0),
        (g_ffn_out_bias, 0),
    )
    final = []
    for value, axis in results:
        if axis is not None and below > 1:
            size = value.shape[axis] // below
            value = lax.dynamic_slice_in_dim(value, lax.axis_index("dp") % below * size, size, axis)
        final.append(value)
    return (out_tokens[None], grad_tokens[None], *final)


def solution(mesh):
    return jax.shard_map(
        per_device,
        mesh=mesh,
        in_specs=(P("dp", "head", None), P("dp"), P("dp", "head", None)) + (P(),) * 19,
        out_specs=(
            P("dp", "head", None),
            P("dp", "head", None),
            P("dp", None),
            P("dp"),
            P(None, "dp"),
            P(None, "dp"),
            P("dp"),
            P("dp"),
            P("dp", None),
            P("dp"),
            P(None, "dp", None),
            P(),
            P(None, "dp"),
            P("dp", None),
            P(),
            P("dp", None),
            P("dp", None),
            P("dp", None),
            P("dp"),
            P("dp", None),
            P("dp"),
        ),
        check_vma=False,
    )
```

```python
import functools

import jax
import jax.numpy as jnp
from jax import lax
from jax.experimental import pallas as pl
from jax.experimental.pallas import tpu as pltpu
from jax.sharding import PartitionSpec as P

HEAD_DIM = 64
EPSILON = 1e-06
LANES = 128
TILE = 256
GROUPS = 16
F32 = jnp.float32
BF16 = jnp.bfloat16
VMEM_BYTES = 28 * 1024 * 1024
FFN_BITS = (1, 2, 3)
ATTN_BITS = (2, 1, 3)
CONV_BITS = (1, 2, 3)
GLU_BITS = (2, 1, 3)


def mm(a, b):
    return lax.dot_general(a, b, (((1,), (0,)), ((), ())), preferred_element_type=F32)


def mm_nt(a, b):
    return lax.dot_general(a, b, (((1,), (1,)), ((), ())), preferred_element_type=F32)


def mm_tn(a, b):
    return lax.dot_general(a, b, (((0,), (0,)), ((), ())), preferred_element_type=F32)


def mean(v):
    return jnp.mean(v, axis=-1, keepdims=True)


def normalized(v):
    centred = v - mean(v)
    rate = lax.rsqrt(mean(centred * centred) + EPSILON)
    return centred * rate, rate


def norm_back(vhat, rate, gained):
    return (gained - mean(gained) - vhat * mean(gained * vhat)) * rate


def sum_tokens(v):
    return jnp.sum(v, axis=0, keepdims=True)


def part_sums(v):
    return jnp.sum(v.reshape(v.shape[0] // 8, 8, v.shape[1]), axis=0)


def row_blocks(total, step, body, carry=0, unroll=1):
    def visit(i, c):
        return body(pl.multiple_of(i * step, step), c)

    return lax.fori_loop(0, total // step, visit, carry, unroll=unroll)


def valid_rows(start, count, length):
    places = start + lax.broadcasted_iota(jnp.int32, (count, 1), 0)
    return (places < length).astype(F32)


def col(n, width=TILE):
    return slice(n * width, (n + 1) * width)


def vector(ref):
    return ref[...].astype(F32).reshape(1, ref.shape[0])


def slot_block(p, sent, bits):
    group = lax.axis_index("dp") // (lax.axis_size("dp") // GROUPS)
    wanted = ((p >> 2) & 1) << bits[0] | ((p >> 1) & 1) << bits[1] | (p & 1) << bits[2]
    return group ^ (wanted | sent)


def for_slots(keep, send, bits, body, unroll=1):
    count = GROUPS // 2 // len(send)
    for i, piece in enumerate(send):

        def visit(q, c, i=i, piece=piece):
            p = i * count + q
            body(p, slot_block(p, 0, bits), keep)
            body(q, slot_block(p, 1, bits), piece)
            return c

        lax.fori_loop(0, count, visit, 0, unroll=unroll)


def place_rows(grads, keep, send, bits, at, rows):
    def one(p, block, out):
        source = pl.ds(pl.multiple_of(block * rows, rows), rows)
        for j, grad in enumerate(grads):
            out[p, at + j * rows : at + (j + 1) * rows, :] = grad[source, :].astype(BF16)

    for_slots(keep, send, bits, one)


def gated(tokens, at, place, length, gain, shift, glu_b, glu_w, first, joined, after_glu, second):
    part, width = tokens.shape

    def first_rows(r, c):
        vhat, _ = normalized(tokens[pl.ds(r, 64), :].astype(F32))
        first[pl.ds(pl.multiple_of(at + r, 64), 64), :] = (vhat * gain[0] + shift[0]).astype(BF16)
        return c

    row_blocks(part, 64, first_rows, unroll=2)
    every = pl.ds(at, part)
    for n in range(2 * width // TILE):
        joined[every, col(n)] = mm(first[every, :], glu_w[:, col(n)]) + glu_b[:, col(n)]

    def glu_rows(r, c):
        rows = pl.ds(pl.multiple_of(at + r, 32), 32)
        gate = jax.nn.sigmoid(joined[rows, width:])
        joined[rows, width:] = gate
        v = tokens[pl.ds(r, 32), :].astype(F32) + joined[rows, :width] * gate
        after_glu[rows, :] = v
        vhat, _ = normalized(v)
        valid = valid_rows(place + r, 32, length)
        second[rows, :] = ((vhat * gain[1] + shift[1]) * valid).astype(BF16)
        return c

    row_blocks(part, 32, glu_rows, unroll=2)


def open_kernel(lengths, far, first, joined, after_glu, second):
    mine, gains, shifts, glu_bias, glu_w, conv_w, left_w, point_w = far
    part = first.shape[0]
    tokens, gains, shifts = mine(), gains(), shifts()
    gain = [gains[k : k + 1, :].astype(F32) for k in range(2)]
    shift = [shifts[k : k + 1, :].astype(F32) for k in range(2)]
    place = lax.axis_index("head") * part
    glu_b, glu_w = vector(glu_bias()), glu_w()
    gated(tokens, 0, place, lengths[0], gain, shift, glu_b, glu_w, first, joined, after_glu, second)
    for get in (conv_w, left_w, point_w):
        get()


def forward_kernel(
    lengths,
    other,
    mine,
    own_first,
    own_joined,
    own_after_glu,
    own_second,
    glu_w,
    conv_w,
    left_w,
    point_w,
    far,
    stream,
    first,
    joined,
    after_glu,
    second,
    left_pre,
    right_pre,
    depth_low,
    after_conv,
    fourth,
    packed,
    probs,
    context,
    after_attn,
    fifth,
    hidden,
    vhat,
    rates,
    third,
    sides,
    mid_row,
    mask,
):
    part, width = other.shape
    seq = 2 * part
    ffn = left_pre.shape[1]
    half = right_pre.shape[1]
    side = lax.axis_index("head")
    length = lengths[0]
    own = pl.ds(pl.multiple_of(side * part, part), part)
    opposite = pl.multiple_of((1 - side) * part, part)
    (
        gains,
        shifts,
        glu_bias,
        conv_bias,
        left_bias,
        mid_gain,
        mid_bias,
        depth_w,
        point_bias,
        qkv_w,
        out_w,
        ffn_in_bias,
        ffn_in_w,
        ffn_out_w,
    ) = far
    for whole, piece in (
        (stream, mine),
        (first, own_first),
        (joined, own_joined),
        (after_glu, own_after_glu),
        (second, own_second),
    ):
        whole[own, :] = piece[...]
    stream[pl.ds(opposite, part), :] = other[...]
    gains, shifts = gains(), shifts()
    gain = [gains[k : k + 1, :].astype(F32) for k in range(4)]
    shift = [shifts[k : k + 1, :].astype(F32) for k in range(4)]
    gated(
        other, opposite, opposite, length, gain, shift, vector(glu_bias()), glu_w, first, joined, after_glu, second
    )
    blank = jnp.zeros((8, half), F32)
    for k in range(2):
        sides[k, 0:8, :] = blank
        sides[k, 8 + seq : 16 + seq, :] = blank
    sides[0, 8 : 8 + seq, :] = mm(second[...], conv_w[0])
    sides[1, 8 : 8 + seq, :] = mm(second[...], conv_w[2])
    right_pre[...] = mm(second[...], conv_w[1]) + vector(conv_bias())
    right_pre[...] = right_pre[...] + sides[0, 7 : 7 + seq, :] + sides[1, 9 : 9 + seq, :]
    left_b = vector(left_bias())
    for n in range(ffn // TILE):
        left_pre[:, col(n)] = mm(second[...], left_w[:, col(n)]) + left_b[:, col(n)]
    mid_row[0:1, :], mid_row[1:2, :] = vector(mid_gain()), vector(mid_bias())
    depth_w = depth_w()
    chunks = ffn // LANES
    edge = jnp.zeros((8, LANES), F32)
    third[0:8, :] = edge
    third[8 + seq : 16 + seq, :] = edge
    mask[...] = (lax.broadcasted_iota(jnp.int32, (seq, LANES), 0) < length).astype(F32)

    def mid_rows(r, c):
        rows = pl.ds(r, 16)
        v, rate = normalized(combine(left_pre[rows, :], right_pre[rows, :]))
        rates[rows, :] = jnp.broadcast_to(rate, (16, LANES))
        for k in range(chunks):
            vhat[k, rows, :] = v[:, col(k, LANES)]
        return c

    row_blocks(seq, 16, mid_rows, unroll=2)

    def depth_lanes(k, c):
        lanes = pl.ds(pl.multiple_of(k * LANES, LANES), LANES)
        taps = depth_w[:, lanes].astype(F32)
        third[8 : 8 + seq, :] = (vhat[k] * mid_row[0:1, lanes] + mid_row[1:2, lanes]) * mask[...]
        total = third[4 : 4 + seq, :] * taps[0:1, :]
        for j in range(1, 9):
            total = total + third[4 + j : 4 + j + seq, :] * taps[j : j + 1, :]
        depth_low[:, lanes] = total.astype(BF16)
        return c

    lax.fori_loop(0, chunks, depth_lanes, 0)
    after_conv[:, :half] = (
        after_glu[:, :half] + mm(depth_low[...], point_w[...]) + vector(point_bias())
    )
    after_conv[:, half:] = after_glu[:, half:]

    def fourth_rows(r, c):
        rows = pl.ds(r, 64)
        vhat, _ = normalized(after_conv[rows, :])
        fourth[rows, :] = (vhat * gain[2] + shift[2]).astype(BF16)
        return c

    row_blocks(seq, 64, fourth_rows, unroll=2)
    qkv_w = qkv_w()
    for n in range(3 * width // TILE):
        packed[:, col(n)] = mm(fourth[...], qkv_w[:, col(n)]).astype(BF16)

    low_lanes = lax.broadcasted_iota(jnp.int32, (1, LANES), 1) < HEAD_DIM
    scale = HEAD_DIM ** (-0.5)

    def head_pair(p, c):
        lanes = pl.ds(pl.multiple_of(p * LANES, LANES), LANES)
        q = packed[:, lanes].astype(F32) * scale
        k = packed[:, pl.ds(pl.multiple_of(width + p * LANES, LANES), LANES)]
        v = packed[:, pl.ds(pl.multiple_of(2 * width + p * LANES, LANES), LANES)]
        open_keys = lax.broadcasted_iota(jnp.int32, (seq, 1), 0) < length
        results = []
        for e in range(2):
            q_one = jnp.where(low_lanes if e == 0 else ~low_lanes, q, 0.0).astype(BF16)
            s = jnp.where(open_keys, mm_nt(k, q_one), -1000000000.0)
            raised = jnp.exp(s - jnp.max(s, axis=0, keepdims=True))
            chance = raised * (1.0 / jnp.sum(raised, axis=0, keepdims=True))
            probs[2 * p + e] = chance
            results.append(mm_tn(v, chance.astype(BF16)))
        both = jnp.concatenate([results[0][:HEAD_DIM], results[1][HEAD_DIM:]], axis=0)
        context[:, lanes] = both.T.astype(BF16)
        return c

    lax.fori_loop(0, width // LANES, head_pair, 0)
    out_w = out_w()
    for n in range(width // TILE):
        after_attn[:, col(n)] = after_conv[:, col(n)] + mm(context[...], out_w[:, col(n)])

    def fifth_rows(r, c):
        rows = pl.ds(r, 64)
        vhat, _ = normalized(after_attn[rows, :])
        fifth[rows, :] = (vhat * gain[3] + shift[3]).astype(BF16)
        return c

    row_blocks(seq, 64, fifth_rows, unroll=2)
    ffn_in_b, ffn_in_w = vector(ffn_in_bias()), ffn_in_w()
    for n in range(ffn // TILE):
        pre = mm(fifth[...], ffn_in_w[:, col(n)]) + ffn_in_b[:, col(n)]
        hidden[:, col(n)] = jnp.where(pre > 0.0, pre, 0.0).astype(BF16)
    ffn_out_w()


def ffn_back_kernel(
    cot_other,
    after_attn,
    fifth,
    hidden,
    ffn_in_w,
    ffn_out_w,
    far,
    d_after,
    small,
    keep,
    send,
    cot,
    d_hidden,
    d_fifth,
    grad,
):
    seq, width = fifth.shape
    part = seq // 2
    ffn = hidden.shape[1]
    side = lax.axis_index("head")
    cot_mine, gains = far
    own = pl.ds(pl.multiple_of(side * part, part), part)
    opposite = pl.ds(pl.multiple_of((1 - side) * part, part), part)
    cot[opposite, :] = cot_other[...]
    cot[own, :] = cot_mine()[...]
    for n in range(ffn // TILE):
        back = mm_nt(cot[...], ffn_out_w[col(n), :])
        back = jnp.where(hidden[:, col(n)].astype(F32) > 0.0, back, 0.0).astype(BF16)
        d_hidden[:, col(n)] = back
        small[0:1, col(n)] = sum_tokens(back.astype(F32))
    for n in range(width // TILE):
        d_fifth[:, col(n)] = mm_nt(d_hidden[...], ffn_in_w[col(n), :])

    cot_half = cot[:, pl.ds(pl.multiple_of(side * (width // 2), width // 2), width // 2)]
    per_row = ffn // GROUPS
    gain = gains()[3:4, :].astype(F32)
    sums = [jnp.zeros((8, width), F32)] * 3
    for p in range(GROUPS // 2):
        block = slice(p * seq // 8, (p + 1) * seq // 8)
        vhat, rate = normalized(after_attn[block, :])
        e = d_fifth[block, :]
        given = cot[block, :].astype(F32)
        d_after[block, :] = given + norm_back(vhat, rate, e * gain)
        sums = [total + part_sums(v) for total, v in zip(sums, (e * vhat, e, given))]
        count = GROUPS // 2 // len(send)
        for sent, out, place in ((0, keep, p), (1, send[p // count], p % count)):
            at = pl.multiple_of(slot_block(p, sent, FFN_BITS) * per_row, per_row)
            out[place, 0:per_row, :] = mm_tn(hidden[:, pl.ds(at, per_row)], cot_half).astype(BF16)
    for k in range(3):
        small[1:2, k * width : (k + 1) * width] = sum_tokens(sums[k])

    rows = width // GROUPS
    for j in range(ffn // 2 // TILE):
        at = pl.multiple_of(side * (ffn // 2) + j * TILE, TILE)
        grad[j] = mm_tn(fifth[...], d_hidden[:, pl.ds(at, TILE)])
    count = ffn // 2 // TILE
    place_rows([grad.at[j] for j in range(count)], keep, send, FFN_BITS, per_row, rows)


def combine(left_pre, right_pre):
    half = right_pre.shape[1]
    left = jnp.maximum(left_pre, 0.0)
    return jnp.concatenate([left[:, :half] + jnp.maximum(right_pre, 0.0), left[:, half:]], axis=1)


def attention_back_kernel(
    d_after,
    packed,
    probs,
    context,
    fourth,
    after_conv,
    depth_low,
    out_w,
    qkv_w,
    far,
    d_after_conv,
    small,
    keep,
    send,
    d_attn,
    d_context,
    d_packed,
    d_fourth,
    d_sep,
    grad,
):
    seq, width = d_after.shape
    side = lax.axis_index("head")
    (gains,) = far
    half = d_sep.shape[1]
    ffn = depth_low.shape[1]
    rows = width // GROUPS
    d_attn[...] = d_after[...].astype(BF16)
    for n in range(width // TILE):
        d_context[:, col(n)] = mm_nt(d_attn[...], out_w[col(n), :]).astype(BF16)
    low_lanes = lax.broadcasted_iota(jnp.int32, (1, LANES), 1) < HEAD_DIM
    scale = HEAD_DIM ** (-0.5)

    def head_pair(p, c):
        lanes = pl.ds(pl.multiple_of(p * LANES, LANES), LANES)
        k_lanes = pl.ds(pl.multiple_of(width + p * LANES, LANES), LANES)
        v_lanes = pl.ds(pl.multiple_of(2 * width + p * LANES, LANES), LANES)
        q = packed[:, lanes]
        k = packed[:, k_lanes]
        v = packed[:, v_lanes].astype(F32)
        given = d_context[:, lanes]
        dq, dk, dv = [], [], []
        for e in range(2):
            one = jnp.where(low_lanes if e == 0 else ~low_lanes, v, 0.0).astype(BF16)
            chance = probs[2 * p + e]
            d_probs = mm_nt(one, given)
            delta = jnp.sum(d_probs * chance, axis=0, keepdims=True)
            d_scores = (chance * (d_probs - delta)).astype(BF16)
            dv.append(mm(chance.astype(BF16), given))
            dk.append(mm(d_scores, q))
            dq.append(mm_tn(k, d_scores))
        both = jnp.concatenate([dq[0][:HEAD_DIM], dq[1][HEAD_DIM:]], axis=0)
        d_packed[:, lanes] = (both.T * scale).astype(BF16)
        d_packed[:, k_lanes] = (jnp.where(low_lanes, dk[0], dk[1]) * scale).astype(BF16)
        d_packed[:, v_lanes] = jnp.where(low_lanes, dv[0], dv[1]).astype(BF16)
        return c

    lax.fori_loop(0, width // LANES, head_pair, 0)
    for n in range(width // TILE):
        d_fourth[:, col(n)] = mm_nt(d_packed[...], qkv_w[col(n), :])
    gain = gains()[2:3, :].astype(F32)

    sums = [jnp.zeros((8, width), F32)] * 2
    g_point = jnp.zeros((8, half), F32)
    at = pl.multiple_of(side * (width // 2), width // 2)
    sides = [(context, d_attn, at)]
    for j in range(3 * width // 2 // TILE):
        sides.append((fourth, d_packed, pl.multiple_of(side * (3 * width // 2) + j * TILE, TILE)))
    for p in range(2 * len(sides)):
        block = slice(p * seq // 8, (p + 1) * seq // 8)
        vhat, rate = normalized(after_conv[block, :])
        e = d_fourth[block, :]
        total = d_after[block, :] + norm_back(vhat, rate, e * gain)
        d_after_conv[block, :] = total
        sep = total[:, :half].astype(BF16)
        d_sep[block, :] = sep
        sums = [total + part_sums(v) for total, v in zip(sums, (e * vhat, e))]
        g_point = g_point + part_sums(sep.astype(F32))
        values, incoming, at = sides[p // 2]
        part = slice(p % 2 * (width // 2), (p % 2 + 1) * (width // 2))
        grad[p // 2, part, :] = mm_tn(values[:, part], incoming[:, pl.ds(at, TILE)])
    small[0:1, 0:width] = sum_tokens(sums[0])
    small[0:1, width : 2 * width] = sum_tokens(sums[1])
    small[0:1, 2 * width : 2 * width + half] = sum_tokens(g_point)
    place_rows([grad.at[j] for j in range(len(sides))], keep, send, ATTN_BITS, 0, rows)
    sep_half = d_sep[:, pl.ds(pl.multiple_of(side * (half // 2), half // 2), half // 2)]
    per_row = ffn // GROUPS

    def point_slot(p, block, out):
        g = mm_tn(
            depth_low[:, pl.ds(pl.multiple_of(block * per_row, per_row), per_row)], sep_half
        ).astype(BF16)
        out[p, 4 * rows : 4 * rows + per_row // 2, 0:LANES] = g[: per_row // 2]
        out[p, 4 * rows : 4 * rows + per_row // 2, LANES : 2 * LANES] = g[per_row // 2 :]

    for_slots(keep, send, ATTN_BITS, point_slot, unroll=4)


def middle_back_kernel(
    lengths,
    d_after_conv,
    left_pre,
    right_pre,
    vhat3,
    rates,
    point_w,
    far,
    d_left,
    taps_right,
    small,
    d_depth,
    d_third,
    sums,
    d_right,
    mid_row,
    mask,
):
    seq, width = d_after_conv.shape
    ffn = left_pre.shape[1]
    half = right_pre.shape[1]
    length = lengths[0]
    mid_gain, mid_bias, depth_w = far
    chunks = ffn // LANES
    edge = jnp.zeros((8, LANES), F32)
    for k in range(chunks):
        d_depth[k, 0:8, :] = edge
        d_depth[k, 8 + seq : 16 + seq, :] = edge
    d_sep = d_after_conv[:, :half].astype(BF16)
    for n in range(ffn // TILE):
        block = mm_nt(d_sep, point_w[col(n), :])
        for m in range(TILE // LANES):
            d_depth[n * (TILE // LANES) + m, 8 : 8 + seq, :] = block[:, col(m, LANES)]

    mid_row[0:1, :], mid_row[1:2, :] = vector(mid_gain()), vector(mid_bias())
    depth_w = depth_w()
    mask[...] = (lax.broadcasted_iota(jnp.int32, (seq, LANES), 0) < length).astype(F32)
    sums[...] = jnp.zeros(sums.shape, F32)
    step = 64

    def depth_lanes(k, c):
        lanes = pl.ds(pl.multiple_of(k * LANES, LANES), LANES)
        taps = depth_w[:, lanes].astype(F32)
        mid_lanes, low_lanes = mid_row[0:1, lanes], mid_row[1:2, lanes]
        totals = [jnp.zeros((8, LANES), F32)] * 11
        for r in range(0, seq, step):
            block = slice(r, r + step)
            vhat = vhat3[k, block, :]
            here = (vhat * mid_lanes + low_lanes) * mask[block, :]
            total = None
            for j in range(9):
                moved = d_depth[k, 12 - j + r : 12 - j + r + step, :]
                totals[j] = totals[j] + part_sums(moved * here)
                term = moved * taps[j : j + 1, :]
                total = term if total is None else total + term
            total = total * mask[block, :]
            totals[9] = totals[9] + part_sums(total * vhat)
            totals[10] = totals[10] + part_sums(total)
            gained = total * mid_lanes
            d_third[k, block, :] = gained
            sums[0, block, :] = sums[0, block, :] + gained
            sums[1, block, :] = sums[1, block, :] + gained * vhat
        for j in range(11):
            small[j : j + 1, lanes] = sum_tokens(totals[j])
        return c

    lax.fori_loop(0, chunks, depth_lanes, 0)
    inverse = 1.0 / ffn
    sums[0] = jnp.broadcast_to(jnp.sum(sums[0], axis=-1, keepdims=True) * inverse, (seq, LANES))
    sums[1] = jnp.broadcast_to(jnp.sum(sums[1], axis=-1, keepdims=True) * inverse, (seq, LANES))

    def combined_lanes(k):
        return (d_third[k] - sums[0] - vhat3[k] * sums[1]) * rates[...]

    def left_lanes(k, c):
        lanes = pl.ds(pl.multiple_of(k * LANES, LANES), LANES)
        v = jnp.where(left_pre[:, lanes] > 0.0, combined_lanes(k), 0.0).astype(BF16)
        d_left[:, lanes] = v
        small[11:12, lanes] = sum_tokens(v.astype(F32))
        return c

    lax.fori_loop(0, chunks, left_lanes, 0)
    blank = jnp.zeros((8, half), F32)
    d_right[0:8, :] = blank
    d_right[8 + seq : 16 + seq, :] = blank
    for k in range(half // LANES):
        v = jnp.where(right_pre[:, col(k, LANES)] > 0.0, combined_lanes(k), 0.0).astype(BF16)
        v = v.astype(F32)
        d_right[8 : 8 + seq, col(k, LANES)] = v
        small[12:13, col(k, LANES)] = sum_tokens(v)
    taps_right[0] = d_right[9 : 9 + seq, :].astype(BF16)
    taps_right[1] = d_right[8 : 8 + seq, :].astype(BF16)
    taps_right[2] = d_right[7 : 7 + seq, :].astype(BF16)


def conv_back_kernel(
    lengths,
    d_left,
    taps_right,
    second,
    left_w,
    conv_w,
    far,
    d_second,
    keep,
    send,
    grad,
    grad_conv,
):
    seq, width = d_second.shape
    ffn = d_left.shape[1]
    half = taps_right.shape[2]
    side = lax.axis_index("head")
    valid = valid_rows(0, seq, lengths[0])
    rows = width // GROUPS
    for j in range(ffn // 2 // TILE):
        at = pl.multiple_of(side * (ffn // 2) + j * TILE, TILE)
        grad[j] = mm_tn(second[...], d_left[:, pl.ds(at, TILE)])
    place_rows([grad.at[j] for j in range(ffn // 2 // TILE)], keep, send, CONV_BITS, 0, rows)
    start = ffn // 2 // TILE * rows
    half_lanes = pl.ds(pl.multiple_of(side * (half // 2), half // 2), half // 2)
    for tap in range(3):
        grad_conv[tap] = mm_tn(second[...], taps_right[tap, :, half_lanes])

    def conv_slot(p, block, out):
        at = pl.multiple_of(block * rows, rows)
        middle = pl.multiple_of(block * rows + rows // 2, rows // 2)
        h = rows // 2
        out[p, start : start + rows, 0:LANES] = grad_conv[0, pl.ds(at, rows), :].astype(BF16)
        out[p, start + rows : start + rows + h, 0:LANES] = grad_conv[1, pl.ds(at, h), :].astype(BF16)
        out[p, start : start + h, LANES : 2 * LANES] = grad_conv[1, pl.ds(middle, h), :].astype(BF16)
        out[p, start + h : start + h + rows, LANES : 2 * LANES] = grad_conv[
            2, pl.ds(at, rows), :
        ].astype(BF16)

    for_slots(keep, send, CONV_BITS, conv_slot)
    for n in range(width // TILE):
        total = mm_nt(d_left[...], left_w[col(n), :])
        for tap in range(3):
            total = total + mm_nt(taps_right[tap], conv_w[tap, col(n), :])
        d_second[:, col(n)] = total * valid


def glu_back_kernel(
    d_second,
    d_after_conv,
    after_glu,
    joined,
    first,
    stream,
    small_ffn,
    small_attn,
    small_conv,
    glu_w,
    far,
    d_after_glu,
    d_first,
    keep,
    send,
    d_joined,
    rolled,
    blocks,
    grad,
):
    seq, width = d_second.shape
    side = lax.axis_index("head")
    gains = far[0]()
    gain = [gains[k : k + 1, :].astype(F32) for k in range(2)]

    def glu_rows(r, c):
        g_gain, g_shift, g_value, g_gate = c
        rows = pl.ds(r, 32)
        vhat, rate = normalized(after_glu[rows, :])
        e = d_second[rows, :]
        total = d_after_conv[rows, :] + norm_back(vhat, rate, e * gain[1])
        d_after_glu[rows, :] = total
        value = joined[rows, :width]
        gate = joined[rows, width:]
        d_value = (total * gate).astype(BF16)
        d_gate = (total * value * gate * (1.0 - gate)).astype(BF16)
        d_joined[rows, :width] = d_value
        d_joined[rows, width:] = d_gate
        return (
            g_gain + part_sums(e * vhat),
            g_shift + part_sums(e),
            g_value + part_sums(d_value.astype(F32)),
            g_gate + part_sums(d_gate.astype(F32)),
        )

    nothing = jnp.zeros((8, width), F32)
    sums = row_blocks(seq, 32, glu_rows, (nothing,) * 4, unroll=2)
    gain_one, shift_one, g_value, g_gate = (sum_tokens(v) for v in sums)
    for n in range(width // TILE):
        d_first[:, col(n)] = mm_nt(d_joined[...], glu_w[col(n), :])

    sums = [nothing] * 2
    rows = width // GROUPS
    columns = [pl.ds(pl.multiple_of(side * width + j * TILE, TILE), TILE) for j in range(width // TILE)]
    for p in range(8):
        block = slice(p * seq // 8, (p + 1) * seq // 8)
        vhat, _ = normalized(stream[block, :].astype(F32))
        e = d_first[block, :]
        sums = [total + part_sums(v) for total, v in zip(sums, (e * vhat, e))]
        if p < 2 * len(columns):
            part_rows = slice(p % 2 * (width // 2), (p % 2 + 1) * (width // 2))
            grad[p // 2, part_rows, :] = mm_tn(first[:, part_rows], d_joined[:, columns[p // 2]])
    gain_zero, shift_zero = (sum_tokens(v) for v in sums)
    place_rows([grad.at[j] for j in range(len(columns))], keep, send, GLU_BITS, 0, rows)

    blocks[...] = jnp.zeros(blocks.shape, F32)
    rolled[...] = jnp.zeros(rolled.shape, F32)
    vectors = (
        (gain_zero, gain_one, small_attn[0:1, 0:width], small_ffn[1:2, 0:width]),
        (shift_zero, shift_one, small_attn[0:1, width : 2 * width], small_ffn[1:2, width : 2 * width]),
    )
    tiles = width // LANES
    lane = lax.broadcasted_iota(jnp.int32, (8, LANES), 1)
    quarter = LANES // tiles
    for kind, four in enumerate(vectors):
        for k, vector in enumerate(four):
            for t in range(tiles):
                rolled[kind, 8 * k + t : 8 * k + t + 1, :] = vector[:, col(t, LANES)]
        for q in range(tiles):
            total = jnp.zeros((8, LANES), F32)
            for k in range(4):
                moved = pltpu.roll(rolled[kind, 8 * k : 8 * k + 8, :], (quarter * (k - q)) % LANES, 1)
                total = jnp.where((lane >= quarter * k) & (lane < quarter * (k + 1)), moved, total)
            for t in range(tiles):
                blocks[tiles * t + q, 13 + kind : 14 + kind, 0:LANES] = total[t : t + 1, :]
    lane = lane[0:1, :]
    g_out = small_ffn[1:2, 2 * width : 3 * width]
    for s in range(GROUPS):
        source = g_value if s < GROUPS // 2 else g_gate
        place = (s % (GROUPS // 2)) * (2 * width // GROUPS)
        block = source[:, place // LANES * LANES : place // LANES * LANES + LANES]
        glu_part = block if place % LANES == 0 else pltpu.roll(block, LANES - place % LANES, 1)
        place = s * (width // GROUPS)
        block = g_out[:, place // LANES * LANES : place // LANES * LANES + LANES]
        moved = (LANES // 2 - place % LANES) % LANES
        out_part = block if moved == 0 else pltpu.roll(block, moved, 1)
        blocks[s, 15:16, 0:LANES] = jnp.where(
            lane < LANES // 2, glu_part, jnp.where(lane < LANES // 2 + quarter, out_part, 0.0)
        )
        blocks[s, 0:12, 0:LANES] = small_conv[0:12, col(s, LANES)]
        blocks[s, 12:13, 0:LANES] = small_ffn[0:1, col(s, LANES)]
        for k in range(2):
            blocks[s, k : k + 1, LANES : 2 * LANES] = small_conv[12:13, col(k, LANES)]
            blocks[s, 2 + k : 3 + k, LANES : 2 * LANES] = small_attn[
                0:1, 2 * width + k * LANES : 2 * width + (k + 1) * LANES
            ]
    start = width // TILE * rows

    def small_slot(p, block, out):
        out[p, start : start + 16, :] = blocks[block].astype(BF16)

    for_slots(keep, send, GLU_BITS, small_slot)


def tokens_kernel(after_attn, hidden, ffn_out_w, d_after_glu, d_first, stream, far, out_tokens, grad_tokens):
    part, width = out_tokens.shape
    gains, ffn_out_bias = far
    at = pl.multiple_of(lax.axis_index("head") * part, part)
    own = pl.ds(at, part)
    gain, bias = gains()[0:1, :].astype(F32), vector(ffn_out_bias())
    for n in range(width // TILE):
        out_tokens[:, col(n)] = (
            after_attn[own, col(n)] + mm(hidden[own, :], ffn_out_w[:, col(n)]) + bias[:, col(n)]
        ).astype(BF16)

    def rows(r, c):
        block = pl.ds(pl.multiple_of(at + r, 32), 32)
        vhat, rate = normalized(stream[block, :].astype(F32))
        grad_tokens[pl.ds(r, 32), :] = d_after_glu[block, :] + norm_back(vhat, rate, d_first[block, :] * gain)
        return c

    row_blocks(part, 32, rows, unroll=2)


def add_kernel(keeps, gots, far, keep, send):
    at = 0
    for kept, got in zip(keeps, gots):
        rows = kept.shape[1]
        half = kept.shape[0] // 2
        count = kept.shape[0] // len(got)
        for i in range(kept.shape[0]):
            total = kept[i].astype(F32) + got[i // count][i % count].astype(F32)
            out = keep if i < half else send
            out[i % half, at : at + rows, :] = total.astype(BF16)
        at += rows


def finish_early_kernel(mine, other, far, ffn_out, ffn_in, out, qkv, point):
    side = lax.axis_index("head")
    per_row, width = ffn_out.shape
    rows = ffn_in.shape[0]
    for who, grads in ((side, mine), (1 - side, other)):
        count = ffn_in.shape[1] // 2 // TILE
        at = pl.ds(pl.multiple_of(who * TILE, TILE), TILE)
        start = per_row + count * rows
        ffn_out[:, at] = grads[0:per_row, :].astype(F32)
        out[:, at] = grads[start : start + rows, :].astype(F32)
        for j in range(count):
            at = pl.ds(pl.multiple_of((who * count + j) * TILE, TILE), TILE)
            ffn_in[:, at] = grads[per_row + j * rows : per_row + (j + 1) * rows, :].astype(F32)
        count = qkv.shape[1] // 2 // TILE
        for j in range(count):
            at = pl.ds(pl.multiple_of((who * count + j) * TILE, TILE), TILE)
            qkv[:, at] = grads[start + (1 + j) * rows : start + (2 + j) * rows, :].astype(F32)
        start = start + (1 + count) * rows
        at = pl.ds(pl.multiple_of(who * LANES, LANES), LANES)
        point[0 : per_row // 2, at] = grads[start : start + per_row // 2, 0:LANES].astype(F32)
        point[per_row // 2 :, at] = grads[start : start + per_row // 2, LANES : 2 * LANES].astype(F32)


def finish_late_kernel(
    mine,
    other,
    far,
    left,
    conv,
    glu,
    gains,
    shifts,
    depth,
    mid_gain,
    mid_bias,
    left_bias,
    ffn_in_bias,
    glu_bias,
    ffn_out_bias,
    conv_bias,
    point_bias,
):
    side = lax.axis_index("head")
    rows = glu.shape[0]
    h = rows // 2
    count = left.shape[1] // 2 // TILE
    behind = count * rows + 3 * h
    wide = glu.shape[1] // 2 // TILE
    for who, grads in ((side, mine), (1 - side, other)):
        for j in range(count):
            at = pl.ds(pl.multiple_of((who * count + j) * TILE, TILE), TILE)
            left[:, at] = grads[j * rows : (j + 1) * rows, :].astype(F32)
        start = count * rows
        at = pl.ds(pl.multiple_of(who * LANES, LANES), LANES)
        low = grads[start : start + 3 * h, 0:LANES].astype(F32)
        high = grads[start : start + 3 * h, LANES : 2 * LANES].astype(F32)
        conv[0, :, at] = low[0:rows]
        conv[1, 0:h, at] = low[rows:]
        conv[1, h:rows, at] = high[0:h]
        conv[2, :, at] = high[h:]
        for j in range(wide):
            at = pl.ds(pl.multiple_of((who * wide + j) * TILE, TILE), TILE)
            glu[:, at] = grads[behind + j * rows : behind + (j + 1) * rows, :].astype(F32)
    start = behind + wide * rows
    block = mine[start : start + 16, :].astype(F32)
    depth[...] = block[0:9, 0:LANES]
    for k in range(4):
        gains[k : k + 1, :] = block[13:14, k * rows : (k + 1) * rows]
        shifts[k : k + 1, :] = block[14:15, k * rows : (k + 1) * rows]
    mid_gain[...] = block[9, 0:LANES]
    mid_bias[...] = block[10, 0:LANES]
    left_bias[...] = block[11, 0:LANES]
    ffn_in_bias[...] = block[12, 0:LANES]
    glu_bias[...] = block[15, 0 : 2 * rows]
    ffn_out_bias[...] = block[15, 2 * rows : 3 * rows]
    for k in range(2):
        conv_bias[col(k, LANES)] = block[k, LANES : 2 * LANES]
        point_bias[col(k, LANES)] = block[2 + k, LANES : 2 * LANES]


def call(kernel, outs, scratch, near, far, micros=0, scalars=0, kept=()):
    smem = pl.BlockSpec(memory_space=pltpu.SMEM)
    vmem = pl.BlockSpec(memory_space=pltpu.VMEM)
    anywhere = pl.BlockSpec(memory_space=pltpu.HBM)

    near, inside = jax.tree.flatten(near)
    outs, outside = jax.tree.flatten(outs, is_leaf=lambda v: isinstance(v, tuple))
    own = len(outs)
    outs = outs + [(far[i].shape, far[i].dtype) for i in kept]

    def body(*refs):
        inputs = inside.unflatten(refs[: len(near)])
        sources = refs[len(near) : len(near) + len(far)]
        first = len(near) + len(far)
        results = outside.unflatten(refs[first : first + own])
        held = refs[first + own : first + len(outs)]
        rest = refs[first + len(outs) :]
        if not far:
            kernel(*inputs, (), *results, *rest)
            return
        *rest, done = rest
        fresh = iter(rest[len(scratch) :])
        buffers = [held[kept.index(i)] if i in kept else next(fresh) for i in range(len(far))]
        copies = [
            pltpu.make_async_copy(source, buffer, done.at[i])
            for i, (source, buffer) in enumerate(zip(sources, buffers))
        ]
        for copy in copies:
            copy.start()

        def fetched(copy, buffer):
            def get():
                copy.wait()
                return buffer

            return get

        kernel(*inputs, tuple(map(fetched, copies, buffers)), *results, *rest[: len(scratch)])

    temporaries = [pltpu.VMEM(shape, dtype) for shape, dtype in scratch]
    if far:
        temporaries += [pltpu.VMEM(v.shape, v.dtype) for i, v in enumerate(far) if i not in kept]
        temporaries.append(pltpu.SemaphoreType.DMA((len(far),)))
    results = pl.pallas_call(
        body,
        out_shape=tuple(jax.ShapeDtypeStruct(shape, dtype) for shape, dtype in outs),
        in_specs=[smem] * scalars + [vmem] * (len(near) - scalars) + [anywhere] * len(far),
        out_specs=(vmem,) * len(outs),
        scratch_shapes=temporaries,
        compiler_params=pltpu.CompilerParams(vmem_limit_bytes=VMEM_BYTES),
        cost_estimate=pl.CostEstimate(
            flops=micros * 10**9, transcendentals=0, bytes_accessed=micros * 3 * 10**6
        ),
        name=kernel.__name__,
    )(*near, *[pltpu.with_memory_space_constraint(v, pltpu.HBM) for v in far])
    return [*outside.unflatten(results[:own]), *results[own:]]


def per_device(
    tokens,
    lengths,
    cotangent,
    glu_weight,
    glu_bias,
    norm_gain,
    norm_bias,
    mid_gain,
    mid_bias,
    left_weight,
    left_bias,
    conv_weight,
    conv_bias,
    depth_weight,
    point_weight,
    point_bias,
    qkv_weight,
    out_weight,
    ffn_in_weight,
    ffn_in_bias,
    ffn_out_weight,
    ffn_out_bias,
):
    row_count, part, width = tokens.shape
    assert row_count == 1 and lax.axis_size("head") == 2
    seq = 2 * part
    shards = lax.axis_size("dp")
    below = shards // GROUPS
    assert below * GROUPS == shards
    heads = width // HEAD_DIM
    half = conv_weight.shape[2]
    ffn = left_weight.shape[1]
    swap = [(0, 1), (1, 0)]
    mine = tokens[0]
    cot_mine = cotangent[0]
    other = lax.ppermute(mine, "head", swap)
    cot_other = lax.ppermute(cot_mine, "head", swap)

    def slot_outs(rows, pieces=1):
        count = GROUPS // 2
        return [((count, rows, TILE), BF16), [((count // pieces, rows, TILE), BF16)] * pieces]

    rows = width // GROUPS
    per_row = ffn // GROUPS
    ffn_rows = per_row + ffn // 2 // TILE * rows
    own_first, own_joined, own_after_glu, own_second, mine, glu_w, conv_w, left_w, point_w = call(
        open_kernel,
        [
            ((part, width), BF16),
            ((part, 2 * width), F32),
            ((part, width), F32),
            ((part, width), BF16),
        ],
        [],
        [lengths],
        [mine, norm_gain, norm_bias, glu_bias, glu_weight, conv_weight, left_weight, point_weight],
        micros=1,
        scalars=1,
        kept=(0, 4, 5, 6, 7),
    )
    (
        stream,
        first_norm,
        joined,
        after_glu,
        second,
        left_pre,
        right_pre,
        depth_low,
        after_conv,
        fourth,
        packed,
        probs,
        context,
        after_attn,
        fifth,
        hidden,
        vhat,
        rates,
        qkv_w,
        out_w,
        ffn_in_w,
        ffn_out_w,
    ) = call(
        forward_kernel,
        [
            ((seq, width), BF16),
            ((seq, width), BF16),
            ((seq, 2 * width), F32),
            ((seq, width), F32),
            ((seq, width), BF16),
            ((seq, ffn), F32),
            ((seq, half), F32),
            ((seq, ffn), BF16),
            ((seq, width), F32),
            ((seq, width), BF16),
            ((seq, 3 * width), BF16),
            ((heads, seq, seq), F32),
            ((seq, width), BF16),
            ((seq, width), F32),
            ((seq, width), BF16),
            ((seq, ffn), BF16),
            ((ffn // LANES, seq, LANES), F32),
            ((seq, LANES), F32),
        ],
        [
            ((seq + 16, LANES), F32),
            ((2, seq + 16, half), F32),
            ((2, ffn), F32),
            ((seq, LANES), F32),
        ],
        [
            lengths,
            other,
            mine,
            own_first,
            own_joined,
            own_after_glu,
            own_second,
            glu_w,
            conv_w,
            left_w,
            point_w,
        ],
        [
            norm_gain,
            norm_bias,
            glu_bias,
            conv_bias,
            left_bias,
            mid_gain,
            mid_bias,
            depth_weight,
            point_bias,
            qkv_weight,
            out_weight,
            ffn_in_bias,
            ffn_in_weight,
            ffn_out_weight,
        ],
        micros=14,
        scalars=1,
        kept=(9, 10, 12, 13),
    )
    d_after, small_ffn, keep_ffn, send_ffn = call(
        ffn_back_kernel,
        [((seq, width), F32), ((8, ffn), F32)] + slot_outs(ffn_rows),
        [
            ((seq, width), BF16),
            ((seq, ffn), BF16),
            ((seq, width), F32),
            ((ffn // 2 // TILE, width, TILE), F32),
        ],
        [cot_other, after_attn, fifth, hidden, ffn_in_w, ffn_out_w],
        [cot_mine, norm_gain],
        micros=5,
    )

    class Chunk:
        def __init__(self, keep, send, bits):
            self.keep, self.send, self.bits = keep, send, list(bits)

        def start(self):
            if not self.bits:
                self.got = [lax.ppermute(self.keep, "head", swap)]
                return
            step = below << self.bits.pop(0)
            pairs = [(i, i ^ step) for i in range(shards)]
            self.got = [lax.ppermute(v, "dp", pairs) for v in self.send]

    def last_sum(keep, got):
        total = (keep[0].astype(F32) + got[0].astype(F32)).astype(BF16)
        step = 1
        while step < below:
            total = total + lax.ppermute(total, "dp", [(i, i ^ step) for i in range(shards)])
            step *= 2
        return total

    def added(*chunks, whole=False):
        keep = chunks[0].keep
        if keep.shape[0] == 1:
            return last_sum(keep, chunks[0].got[0]), None
        if len(chunks) == 1 and len(chunks[0].got) < 3 and not whole:
            (c,) = chunks
            n = keep.shape[0] // 2
            got = c.got if len(c.got) == 2 else (c.got[0][:n], c.got[0][n:])
            return tuple(
                (keep[half * n : half * n + n].astype(F32) + got[half].astype(F32)).astype(BF16)
                for half in range(2)
            )
        shape = ((keep.shape[0] // 2, sum(c.keep.shape[1] for c in chunks), TILE), BF16)
        return call(
            add_kernel, [shape, shape], [], [[c.keep for c in chunks], [c.got for c in chunks]], []
        )

    def received(held, *chunks):
        held, gots = lax.optimization_barrier((held, [c.got for c in chunks]))
        for c, got in zip(chunks, gots):
            c.got = got
        return held

    def wave(held, *chunks, joined=False, whole=True):
        held = received(held, *chunks)
        groups = [chunks] if joined else [(c,) for c in chunks]
        nexts = [Chunk(*added(*group, whole=whole), group[0].bits) for group in groups]
        held, keeps = lax.optimization_barrier((held, [(c.keep, c.send) for c in nexts]))
        for c, (keep, send) in zip(nexts, keeps):
            c.keep, c.send = keep, [send]
            c.start()
        return (held, *nexts)

    ffn_grads = Chunk(keep_ffn, send_ffn, (0, *FFN_BITS))
    ffn_grads.start()
    d_after_conv, small_attn, keep_attn, send_attn = call(
        attention_back_kernel,
        [((seq, width), F32), ((8, ffn), F32)] + slot_outs(4 * rows + per_row // 2),
        [
            ((seq, width), BF16),
            ((seq, width), BF16),
            ((seq, 3 * width), BF16),
            ((seq, width), F32),
            ((seq, half), BF16),
            ((4, width, TILE), F32),
        ],
        [d_after, packed, probs, context, fourth, after_conv, depth_low, out_w, qkv_w],
        [norm_gain],
        micros=10,
    )
    d_after_conv, ffn_grads = wave(d_after_conv, ffn_grads, whole=False)
    attn_grads = Chunk(keep_attn, send_attn, (0, *ATTN_BITS))
    attn_grads.start()
    d_after_conv, attn_grads = wave(d_after_conv, attn_grads, whole=True)
    d_left, taps_right, small_conv = call(
        middle_back_kernel,
        [((seq, ffn), BF16), ((3, seq, half), BF16), ((16, ffn), F32)],
        [
            ((ffn // LANES, seq + 16, LANES), F32),
            ((ffn // LANES, seq, LANES), F32),
            ((2, seq, LANES), F32),
            ((seq + 16, half), F32),
            ((2, ffn), F32),
            ((seq, LANES), F32),
        ],
        [lengths, d_after_conv, left_pre, right_pre, vhat, rates, point_w],
        [mid_gain, mid_bias, depth_weight],
        micros=0,
        scalars=1,
    )
    d_second, keep_conv, send_conv = call(
        conv_back_kernel,
        [((seq, width), F32)] + slot_outs(ffn // 2 // TILE * rows + 3 * rows // 2, 1),
        [((ffn // 2 // TILE, width, TILE), F32), ((3, width, LANES), F32)],
        [lengths, d_left, taps_right, second, left_w, conv_w],
        [],
        micros=0,
        scalars=1,
    )
    conv_grads = Chunk(keep_conv, send_conv, (0, *CONV_BITS))
    conv_grads.start()
    d_second, ffn_grads, attn_grads = wave(d_second, ffn_grads, attn_grads, whole=False)
    d_second, conv_grads = wave(d_second, conv_grads)
    d_after_glu, d_first, keep_glu, send_glu = call(
        glu_back_kernel,
        [((seq, width), F32)] * 2 + slot_outs(width // TILE * rows + 16, 2),
        [
            ((seq, 2 * width), BF16),
            ((2, 32, LANES), F32),
            ((GROUPS, 16, 2 * LANES), F32),
            ((width // TILE, width, TILE), F32),
        ],
        [
            d_second,
            d_after_conv,
            after_glu,
            joined,
            first_norm,
            stream,
            small_ffn,
            small_attn,
            small_conv,
            glu_w,
        ],
        [norm_gain],
        micros=7,
    )
    glu_grads = Chunk(keep_glu, send_glu, (0, *GLU_BITS))
    glu_grads.start()
    held = received(d_after_glu, ffn_grads, attn_grads)
    held, glu_grads = wave(held, glu_grads)
    held, early = wave(held, ffn_grads, attn_grads, joined=True)
    held, conv_grads = wave(held, conv_grads)
    out_tokens, grad_tokens = call(
        tokens_kernel,
        [((part, width), BF16), ((part, width), F32)],
        [],
        [after_attn, hidden, ffn_out_w, held, d_first, stream],
        [norm_gain, ffn_out_bias],
    )
    grad_tokens, glu_grads = wave(grad_tokens, glu_grads)
    held, late = wave(grad_tokens, conv_grads, glu_grads, joined=True)
    held, early = wave(held, early)
    grad_tokens, late = wave(held, late)
    other = early.got[0]
    ffn_out, ffn_in, out, qkv, point = call(
        finish_early_kernel,
        [
            ((per_row, width), F32),
            ((rows, ffn), F32),
            ((rows, width), F32),
            ((rows, 3 * width), F32),
            ((per_row, half), F32),
        ],
        [],
        [early.keep, other],
        [],
    )
    (
        left,
        conv,
        glu,
        g_gains,
        g_shifts,
        g_depth,
        g_mid_gain,
        g_mid_bias,
        g_left_bias,
        g_ffn_in_bias,
        g_glu_bias,
        g_ffn_out_bias,
        g_conv_bias,
        g_point_bias,
    ) = call(
        finish_late_kernel,
        [
            ((rows, ffn), F32),
            ((3, rows, half), F32),
            ((rows, 2 * width), F32),
            ((4, rows), F32),
            ((4, rows), F32),
            ((9, LANES), F32),
            ((LANES,), F32),
            ((LANES,), F32),
            ((LANES,), F32),
            ((LANES,), F32),
            ((2 * rows,), F32),
            ((rows,), F32),
            ((half,), F32),
            ((half,), F32),
        ],
        [],
        [late.keep, late.got[0]],
        [],
    )
    results = (
        (glu, 0),
        (g_glu_bias, 0),
        (g_gains, 1),
        (g_shifts, 1),
        (g_mid_gain, 0),
        (g_mid_bias, 0),
        (left, 0),
        (g_left_bias, 0),
        (conv, 1),
        (g_conv_bias, None),
        (g_depth, 1),
        (point, 0),
        (g_point_bias, None),
        (qkv, 0),
        (out, 0),
        (ffn_in, 0),
        (g_ffn_in_bias, 0),
        (ffn_out, 0),
        (g_ffn_out_bias, 0),
    )
    final = []
    for value, axis in results:
        if axis is not None and below > 1:
            size = value.shape[axis] // below
            value = lax.dynamic_slice_in_dim(value, lax.axis_index("dp") % below * size, size, axis)
        final.append(value)
    return (out_tokens[None], grad_tokens[None], *final)


def solution(mesh):
    return jax.shard_map(
        per_device,
        mesh=mesh,
        in_specs=(P("dp", "head", None), P("dp"), P("dp", "head", None)) + (P(),) * 19,
        out_specs=(
            P("dp", "head", None),
            P("dp", "head", None),
            P("dp", None),
            P("dp"),
            P(None, "dp"),
            P(None, "dp"),
            P("dp"),
            P("dp"),
            P("dp", None),
            P("dp"),
            P(None, "dp", None),
            P(),
            P(None, "dp"),
            P("dp", None),
            P(),
            P("dp", None),
            P("dp", None),
            P("dp", None),
            P("dp"),
            P("dp", None),
            P("dp"),
        ),
        check_vma=False,
    )
```

```python
import functools

import jax
import jax.numpy as jnp
from jax import lax
from jax.experimental import pallas as pl
from jax.experimental.pallas import tpu as pltpu
from jax.sharding import PartitionSpec as P

HEAD_DIM = 64
EPSILON = 1e-06
LANES = 128
TILE = 256
GROUPS = 16
F32 = jnp.float32
BF16 = jnp.bfloat16
VMEM_BYTES = 28 * 1024 * 1024
FFN_BITS = (1, 2, 3)
ATTN_BITS = (2, 1, 3)
CONV_BITS = (1, 2, 3)
GLU_BITS = (2, 1, 3)


def mm(a, b):
    return lax.dot_general(a, b, (((1,), (0,)), ((), ())), preferred_element_type=F32)


def mm_nt(a, b):
    return lax.dot_general(a, b, (((1,), (1,)), ((), ())), preferred_element_type=F32)


def mm_tn(a, b):
    return lax.dot_general(a, b, (((0,), (0,)), ((), ())), preferred_element_type=F32)


def mean(v):
    return jnp.mean(v, axis=-1, keepdims=True)


def normalized(v):
    centred = v - mean(v)
    rate = lax.rsqrt(mean(centred * centred) + EPSILON)
    return centred * rate, rate


def norm_back(vhat, rate, gained):
    return (gained - mean(gained) - vhat * mean(gained * vhat)) * rate


def sum_tokens(v):
    return jnp.sum(v, axis=0, keepdims=True)


def part_sums(v):
    return jnp.sum(v.reshape(v.shape[0] // 8, 8, v.shape[1]), axis=0)


def row_blocks(total, step, body, carry=0, unroll=1):
    def visit(i, c):
        return body(pl.multiple_of(i * step, step), c)

    return lax.fori_loop(0, total // step, visit, carry, unroll=unroll)


def valid_rows(start, count, length):
    places = start + lax.broadcasted_iota(jnp.int32, (count, 1), 0)
    return (places < length).astype(F32)


def col(n, width=TILE):
    return slice(n * width, (n + 1) * width)


def vector(ref):
    return ref[...].astype(F32).reshape(1, ref.shape[0])


def slot_block(p, sent, bits):
    group = lax.axis_index("dp") // (lax.axis_size("dp") // GROUPS)
    wanted = ((p >> 2) & 1) << bits[0] | ((p >> 1) & 1) << bits[1] | (p & 1) << bits[2]
    return group ^ (wanted | sent)


def for_slots(keep, send, bits, body, unroll=1):
    count = GROUPS // 2 // len(send)
    for i, piece in enumerate(send):

        def visit(q, c, i=i, piece=piece):
            p = i * count + q
            body(p, slot_block(p, 0, bits), keep)
            body(q, slot_block(p, 1, bits), piece)
            return c

        lax.fori_loop(0, count, visit, 0, unroll=unroll)


def place_rows(grads, keep, send, bits, at, rows):
    def one(p, block, out):
        source = pl.ds(pl.multiple_of(block * rows, rows), rows)
        for j, grad in enumerate(grads):
            out[p, at + j * rows : at + (j + 1) * rows, :] = grad[source, :].astype(BF16)

    for_slots(keep, send, bits, one)


def gated(tokens, at, place, length, gain, shift, glu_b, glu_w, first, joined, after_glu, second):
    part, width = tokens.shape

    def first_rows(r, c):
        vhat, _ = normalized(tokens[pl.ds(r, 64), :].astype(F32))
        first[pl.ds(pl.multiple_of(at + r, 64), 64), :] = (vhat * gain[0] + shift[0]).astype(BF16)
        return c

    row_blocks(part, 64, first_rows, unroll=2)
    every = pl.ds(at, part)
    for n in range(2 * width // TILE):
        joined[every, col(n)] = mm(first[every, :], glu_w[:, col(n)]) + glu_b[:, col(n)]

    def glu_rows(r, c):
        rows = pl.ds(pl.multiple_of(at + r, 32), 32)
        gate = jax.nn.sigmoid(joined[rows, width:])
        joined[rows, width:] = gate
        v = tokens[pl.ds(r, 32), :].astype(F32) + joined[rows, :width] * gate
        after_glu[rows, :] = v
        vhat, _ = normalized(v)
        valid = valid_rows(place + r, 32, length)
        second[rows, :] = ((vhat * gain[1] + shift[1]) * valid).astype(BF16)
        return c

    row_blocks(part, 32, glu_rows, unroll=4)


def open_kernel(lengths, far, first, joined, after_glu, second):
    mine, gains, shifts, glu_bias, glu_w, conv_w, left_w, point_w = far
    part = first.shape[0]
    tokens, gains, shifts = mine(), gains(), shifts()
    gain = [gains[k : k + 1, :].astype(F32) for k in range(2)]
    shift = [shifts[k : k + 1, :].astype(F32) for k in range(2)]
    place = lax.axis_index("head") * part
    glu_b, glu_w = vector(glu_bias()), glu_w()
    gated(tokens, 0, place, lengths[0], gain, shift, glu_b, glu_w, first, joined, after_glu, second)
    for get in (conv_w, left_w, point_w):
        get()


def forward_kernel(
    lengths,
    other,
    mine,
    own_first,
    own_joined,
    own_after_glu,
    own_second,
    glu_w,
    conv_w,
    left_w,
    point_w,
    far,
    stream,
    first,
    joined,
    after_glu,
    second,
    left_pre,
    right_pre,
    depth_low,
    after_conv,
    fourth,
    packed,
    probs,
    context,
    after_attn,
    fifth,
    hidden,
    vhat,
    rates,
    third,
    sides,
    mid_row,
    mask,
):
    part, width = other.shape
    seq = 2 * part
    ffn = left_pre.shape[1]
    half = right_pre.shape[1]
    side = lax.axis_index("head")
    length = lengths[0]
    own = pl.ds(pl.multiple_of(side * part, part), part)
    opposite = pl.multiple_of((1 - side) * part, part)
    (
        gains,
        shifts,
        glu_bias,
        conv_bias,
        left_bias,
        mid_gain,
        mid_bias,
        depth_w,
        point_bias,
        qkv_w,
        out_w,
        ffn_in_bias,
        ffn_in_w,
        ffn_out_w,
    ) = far
    for whole, piece in (
        (stream, mine),
        (first, own_first),
        (joined, own_joined),
        (after_glu, own_after_glu),
        (second, own_second),
    ):
        whole[own, :] = piece[...]
    stream[pl.ds(opposite, part), :] = other[...]
    gains, shifts = gains(), shifts()
    gain = [gains[k : k + 1, :].astype(F32) for k in range(4)]
    shift = [shifts[k : k + 1, :].astype(F32) for k in range(4)]
    gated(
        other, opposite, opposite, length, gain, shift, vector(glu_bias()), glu_w, first, joined, after_glu, second
    )
    blank = jnp.zeros((8, half), F32)
    for k in range(2):
        sides[k, 0:8, :] = blank
        sides[k, 8 + seq : 16 + seq, :] = blank
    sides[0, 8 : 8 + seq, :] = mm(second[...], conv_w[0])
    sides[1, 8 : 8 + seq, :] = mm(second[...], conv_w[2])
    right_pre[...] = mm(second[...], conv_w[1]) + vector(conv_bias())
    right_pre[...] = right_pre[...] + sides[0, 7 : 7 + seq, :] + sides[1, 9 : 9 + seq, :]
    left_b = vector(left_bias())
    for n in range(ffn // TILE):
        left_pre[:, col(n)] = mm(second[...], left_w[:, col(n)]) + left_b[:, col(n)]
    mid_row[0:1, :], mid_row[1:2, :] = vector(mid_gain()), vector(mid_bias())
    depth_w = depth_w()
    chunks = ffn // LANES
    edge = jnp.zeros((8, LANES), F32)
    third[0:8, :] = edge
    third[8 + seq : 16 + seq, :] = edge
    mask[...] = (lax.broadcasted_iota(jnp.int32, (seq, LANES), 0) < length).astype(F32)

    def mid_rows(r, c):
        rows = pl.ds(r, 16)
        v, rate = normalized(combine(left_pre[rows, :], right_pre[rows, :]))
        rates[rows, :] = jnp.broadcast_to(rate, (16, LANES))
        for k in range(chunks):
            vhat[k, rows, :] = v[:, col(k, LANES)]
        return c

    row_blocks(seq, 16, mid_rows, unroll=8)

    def depth_lanes(k, c):
        lanes = pl.ds(pl.multiple_of(k * LANES, LANES), LANES)
        taps = depth_w[:, lanes].astype(F32)
        mid_gains, mid_shifts = mid_row[0:1, lanes], mid_row[1:2, lanes]
        step = 64
        for r in range(0, seq, step):
            block = slice(r, r + step)
            third[8 + r : 8 + r + step, :] = (vhat[k, block, :] * mid_gains + mid_shifts) * mask[block, :]
        for r in range(0, seq, step):
            total = third[4 + r : 4 + r + step, :] * taps[0:1, :]
            for j in range(1, 9):
                total = total + third[4 + j + r : 4 + j + r + step, :] * taps[j : j + 1, :]
            depth_low[r : r + step, lanes] = total.astype(BF16)
        return c

    lax.fori_loop(0, chunks, depth_lanes, 0, unroll=2)
    after_conv[:, :half] = (
        after_glu[:, :half] + mm(depth_low[...], point_w[...]) + vector(point_bias())
    )
    after_conv[:, half:] = after_glu[:, half:]

    def fourth_rows(r, c):
        rows = pl.ds(r, 64)
        vhat, _ = normalized(after_conv[rows, :])
        fourth[rows, :] = (vhat * gain[2] + shift[2]).astype(BF16)
        return c

    row_blocks(seq, 64, fourth_rows, unroll=4)
    qkv_w = qkv_w()
    for n in range(3 * width // TILE):
        packed[:, col(n)] = mm(fourth[...], qkv_w[:, col(n)]).astype(BF16)

    low_lanes = lax.broadcasted_iota(jnp.int32, (1, LANES), 1) < HEAD_DIM
    scale = HEAD_DIM ** (-0.5)

    def head_pair(p, c):
        lanes = pl.ds(pl.multiple_of(p * LANES, LANES), LANES)
        q = packed[:, lanes].astype(F32) * scale
        k = packed[:, pl.ds(pl.multiple_of(width + p * LANES, LANES), LANES)]
        v = packed[:, pl.ds(pl.multiple_of(2 * width + p * LANES, LANES), LANES)]
        open_keys = lax.broadcasted_iota(jnp.int32, (seq, 1), 0) < length
        results = []
        for e in range(2):
            q_one = jnp.where(low_lanes if e == 0 else ~low_lanes, q, 0.0).astype(BF16)
            s = jnp.where(open_keys, mm_nt(k, q_one), -1000000000.0)
            raised = jnp.exp(s - jnp.max(s, axis=0, keepdims=True))
            chance = raised * (1.0 / jnp.sum(raised, axis=0, keepdims=True))
            probs[2 * p + e] = chance
            results.append(mm_tn(v, chance.astype(BF16)))
        both = jnp.concatenate([results[0][:HEAD_DIM], results[1][HEAD_DIM:]], axis=0)
        context[:, lanes] = both.T.astype(BF16)
        return c

    lax.fori_loop(0, width // LANES, head_pair, 0, unroll=4)
    out_w = out_w()
    for n in range(width // TILE):
        after_attn[:, col(n)] = after_conv[:, col(n)] + mm(context[...], out_w[:, col(n)])

    def fifth_rows(r, c):
        rows = pl.ds(r, 64)
        vhat, _ = normalized(after_attn[rows, :])
        fifth[rows, :] = (vhat * gain[3] + shift[3]).astype(BF16)
        return c

    row_blocks(seq, 64, fifth_rows, unroll=4)
    ffn_in_b, ffn_in_w = vector(ffn_in_bias()), ffn_in_w()
    for n in range(ffn // TILE):
        pre = mm(fifth[...], ffn_in_w[:, col(n)]) + ffn_in_b[:, col(n)]
        hidden[:, col(n)] = jnp.where(pre > 0.0, pre, 0.0).astype(BF16)
    ffn_out_w()


def ffn_back_kernel(
    cot_other,
    after_attn,
    fifth,
    hidden,
    ffn_in_w,
    ffn_out_w,
    far,
    d_after,
    small,
    keep,
    send,
    cot,
    d_hidden,
    d_fifth,
    grad,
):
    seq, width = fifth.shape
    part = seq // 2
    ffn = hidden.shape[1]
    side = lax.axis_index("head")
    cot_mine, gains = far
    own = pl.ds(pl.multiple_of(side * part, part), part)
    opposite = pl.ds(pl.multiple_of((1 - side) * part, part), part)
    cot[opposite, :] = cot_other[...]
    cot[own, :] = cot_mine()[...]
    for n in range(ffn // TILE):
        back = mm_nt(cot[...], ffn_out_w[col(n), :])
        back = jnp.where(hidden[:, col(n)].astype(F32) > 0.0, back, 0.0).astype(BF16)
        d_hidden[:, col(n)] = back
        small[0:1, col(n)] = sum_tokens(back.astype(F32))
    for n in range(width // TILE):
        d_fifth[:, col(n)] = mm_nt(d_hidden[...], ffn_in_w[col(n), :])

    cot_half = cot[:, pl.ds(pl.multiple_of(side * (width // 2), width // 2), width // 2)]
    per_row = ffn // GROUPS
    gain = gains()[3:4, :].astype(F32)
    sums = [jnp.zeros((8, width), F32)] * 3
    for p in range(GROUPS // 2):
        block = slice(p * seq // 8, (p + 1) * seq // 8)
        vhat, rate = normalized(after_attn[block, :])
        e = d_fifth[block, :]
        given = cot[block, :].astype(F32)
        d_after[block, :] = given + norm_back(vhat, rate, e * gain)
        sums = [total + part_sums(v) for total, v in zip(sums, (e * vhat, e, given))]
        count = GROUPS // 2 // len(send)
        for sent, out, place in ((0, keep, p), (1, send[p // count], p % count)):
            at = pl.multiple_of(slot_block(p, sent, FFN_BITS) * per_row, per_row)
            out[place, 0:per_row, :] = mm_tn(hidden[:, pl.ds(at, per_row)], cot_half).astype(BF16)
    for k in range(3):
        small[1:2, k * width : (k + 1) * width] = sum_tokens(sums[k])

    rows = width // GROUPS
    for j in range(ffn // 2 // TILE):
        at = pl.multiple_of(side * (ffn // 2) + j * TILE, TILE)
        grad[j] = mm_tn(fifth[...], d_hidden[:, pl.ds(at, TILE)])
    count = ffn // 2 // TILE
    place_rows([grad.at[j] for j in range(count)], keep, send, FFN_BITS, per_row, rows)


def combine(left_pre, right_pre):
    half = right_pre.shape[1]
    left = jnp.maximum(left_pre, 0.0)
    return jnp.concatenate([left[:, :half] + jnp.maximum(right_pre, 0.0), left[:, half:]], axis=1)


def attention_back_kernel(
    d_after,
    packed,
    probs,
    context,
    fourth,
    after_conv,
    depth_low,
    out_w,
    qkv_w,
    far,
    d_after_conv,
    small,
    keep,
    send,
    d_attn,
    d_context,
    d_packed,
    d_fourth,
    d_sep,
    grad,
):
    seq, width = d_after.shape
    side = lax.axis_index("head")
    (gains,) = far
    half = d_sep.shape[1]
    ffn = depth_low.shape[1]
    rows = width // GROUPS
    d_attn[...] = d_after[...].astype(BF16)
    for n in range(width // TILE):
        d_context[:, col(n)] = mm_nt(d_attn[...], out_w[col(n), :]).astype(BF16)
    low_lanes = lax.broadcasted_iota(jnp.int32, (1, LANES), 1) < HEAD_DIM
    scale = HEAD_DIM ** (-0.5)

    def head_pair(p, c):
        lanes = pl.ds(pl.multiple_of(p * LANES, LANES), LANES)
        k_lanes = pl.ds(pl.multiple_of(width + p * LANES, LANES), LANES)
        v_lanes = pl.ds(pl.multiple_of(2 * width + p * LANES, LANES), LANES)
        q = packed[:, lanes]
        k = packed[:, k_lanes]
        v = packed[:, v_lanes].astype(F32)
        given = d_context[:, lanes]
        dq, dk, dv = [], [], []
        for e in range(2):
            one = jnp.where(low_lanes if e == 0 else ~low_lanes, v, 0.0).astype(BF16)
            chance = probs[2 * p + e]
            d_probs = mm_nt(one, given)
            delta = jnp.sum(d_probs * chance, axis=0, keepdims=True)
            d_scores = (chance * (d_probs - delta)).astype(BF16)
            dv.append(mm(chance.astype(BF16), given))
            dk.append(mm(d_scores, q))
            dq.append(mm_tn(k, d_scores))
        both = jnp.concatenate([dq[0][:HEAD_DIM], dq[1][HEAD_DIM:]], axis=0)
        d_packed[:, lanes] = (both.T * scale).astype(BF16)
        d_packed[:, k_lanes] = (jnp.where(low_lanes, dk[0], dk[1]) * scale).astype(BF16)
        d_packed[:, v_lanes] = jnp.where(low_lanes, dv[0], dv[1]).astype(BF16)
        return c

    lax.fori_loop(0, width // LANES, head_pair, 0, unroll=4)
    for n in range(width // TILE):
        d_fourth[:, col(n)] = mm_nt(d_packed[...], qkv_w[col(n), :])
    gain = gains()[2:3, :].astype(F32)

    sums = [jnp.zeros((8, width), F32)] * 2
    g_point = jnp.zeros((8, half), F32)
    at = pl.multiple_of(side * (width // 2), width // 2)
    sides = [(context, d_attn, at)]
    for j in range(3 * width // 2 // TILE):
        sides.append((fourth, d_packed, pl.multiple_of(side * (3 * width // 2) + j * TILE, TILE)))
    for p in range(2 * len(sides)):
        block = slice(p * seq // 8, (p + 1) * seq // 8)
        vhat, rate = normalized(after_conv[block, :])
        e = d_fourth[block, :]
        total = d_after[block, :] + norm_back(vhat, rate, e * gain)
        d_after_conv[block, :] = total
        sep = total[:, :half].astype(BF16)
        d_sep[block, :] = sep
        sums = [total + part_sums(v) for total, v in zip(sums, (e * vhat, e))]
        g_point = g_point + part_sums(sep.astype(F32))
        values, incoming, at = sides[p // 2]
        part = slice(p % 2 * (width // 2), (p % 2 + 1) * (width // 2))
        grad[p // 2, part, :] = mm_tn(values[:, part], incoming[:, pl.ds(at, TILE)])
    small[0:1, 0:width] = sum_tokens(sums[0])
    small[0:1, width : 2 * width] = sum_tokens(sums[1])
    small[0:1, 2 * width : 2 * width + half] = sum_tokens(g_point)
    place_rows([grad.at[j] for j in range(len(sides))], keep, send, ATTN_BITS, 0, rows)
    sep_half = d_sep[:, pl.ds(pl.multiple_of(side * (half // 2), half // 2), half // 2)]
    per_row = ffn // GROUPS

    def point_slot(p, block, out):
        g = mm_tn(
            depth_low[:, pl.ds(pl.multiple_of(block * per_row, per_row), per_row)], sep_half
        ).astype(BF16)
        out[p, 4 * rows : 4 * rows + per_row // 2, 0:LANES] = g[: per_row // 2]
        out[p, 4 * rows : 4 * rows + per_row // 2, LANES : 2 * LANES] = g[per_row // 2 :]

    for_slots(keep, send, ATTN_BITS, point_slot, unroll=4)


def middle_back_kernel(
    lengths,
    d_after_conv,
    left_pre,
    right_pre,
    vhat3,
    rates,
    point_w,
    far,
    d_left,
    taps_right,
    small,
    d_depth,
    d_third,
    sums,
    d_right,
    mid_row,
    mask,
    left_sums,
):
    seq, width = d_after_conv.shape
    ffn = left_pre.shape[1]
    half = right_pre.shape[1]
    length = lengths[0]
    mid_gain, mid_bias, depth_w = far
    chunks = ffn // LANES
    edge = jnp.zeros((8, LANES), F32)
    for k in range(chunks):
        d_depth[k, 0:8, :] = edge
        d_depth[k, 8 + seq : 16 + seq, :] = edge
    d_sep = d_after_conv[:, :half].astype(BF16)
    for n in range(ffn // TILE):
        block = mm_nt(d_sep, point_w[col(n), :])
        for m in range(TILE // LANES):
            d_depth[n * (TILE // LANES) + m, 8 : 8 + seq, :] = block[:, col(m, LANES)]

    mid_row[0:1, :], mid_row[1:2, :] = vector(mid_gain()), vector(mid_bias())
    depth_w = depth_w()
    mask[...] = (lax.broadcasted_iota(jnp.int32, (seq, LANES), 0) < length).astype(F32)
    sums[...] = jnp.zeros(sums.shape, F32)
    step = 64

    def depth_lanes(k, c):
        lanes = pl.ds(pl.multiple_of(k * LANES, LANES), LANES)
        taps = depth_w[:, lanes].astype(F32)
        mid_lanes, low_lanes = mid_row[0:1, lanes], mid_row[1:2, lanes]
        totals = [jnp.zeros((8, LANES), F32)] * 11
        for r in range(0, seq, step):
            block = slice(r, r + step)
            vhat = vhat3[k, block, :]
            here = (vhat * mid_lanes + low_lanes) * mask[block, :]
            total = None
            for j in range(9):
                moved = d_depth[k, 12 - j + r : 12 - j + r + step, :]
                totals[j] = totals[j] + part_sums(moved * here)
                term = moved * taps[j : j + 1, :]
                total = term if total is None else total + term
            total = total * mask[block, :]
            totals[9] = totals[9] + part_sums(total * vhat)
            totals[10] = totals[10] + part_sums(total)
            gained = total * mid_lanes
            d_third[k, block, :] = gained
            sums[0, block, :] = sums[0, block, :] + gained
            sums[1, block, :] = sums[1, block, :] + gained * vhat
        for j in range(11):
            small[j : j + 1, lanes] = sum_tokens(totals[j])
        return c

    lax.fori_loop(0, chunks, depth_lanes, 0, unroll=2)
    inverse = 1.0 / ffn
    sums[0] = jnp.broadcast_to(jnp.sum(sums[0], axis=-1, keepdims=True) * inverse, (seq, LANES))
    sums[1] = jnp.broadcast_to(jnp.sum(sums[1], axis=-1, keepdims=True) * inverse, (seq, LANES))

    def combined_lanes(k):
        return (d_third[k] - sums[0] - vhat3[k] * sums[1]) * rates[...]

    left_sums[...] = jnp.zeros(left_sums.shape, F32)
    for r in range(0, seq, step):
        block = slice(r, r + step)
        first, second, rate = sums[0, block, :], sums[1, block, :], rates[block, :]

        def left_lanes(k, c, block=block, first=first, second=second, rate=rate):
            lanes = pl.ds(pl.multiple_of(k * LANES, LANES), LANES)
            v = (d_third[k, block, :] - first - vhat3[k, block, :] * second) * rate
            v = jnp.where(left_pre[block, lanes] > 0.0, v, 0.0).astype(BF16)
            d_left[block, lanes] = v
            left_sums[k] = left_sums[k] + part_sums(v.astype(F32))
            return c

        lax.fori_loop(0, chunks, left_lanes, 0, unroll=2)
    for k in range(chunks):
        small[11:12, col(k, LANES)] = sum_tokens(left_sums[k])
    blank = jnp.zeros((8, half), F32)
    d_right[0:8, :] = blank
    d_right[8 + seq : 16 + seq, :] = blank
    for k in range(half // LANES):
        v = jnp.where(right_pre[:, col(k, LANES)] > 0.0, combined_lanes(k), 0.0).astype(BF16)
        v = v.astype(F32)
        d_right[8 : 8 + seq, col(k, LANES)] = v
        small[12:13, col(k, LANES)] = sum_tokens(v)
    taps_right[0] = d_right[9 : 9 + seq, :].astype(BF16)
    taps_right[1] = d_right[8 : 8 + seq, :].astype(BF16)
    taps_right[2] = d_right[7 : 7 + seq, :].astype(BF16)


def conv_back_kernel(
    lengths,
    d_left,
    taps_right,
    second,
    left_w,
    conv_w,
    far,
    d_second,
    keep,
    send,
    grad,
    grad_conv,
):
    seq, width = d_second.shape
    ffn = d_left.shape[1]
    half = taps_right.shape[2]
    side = lax.axis_index("head")
    valid = valid_rows(0, seq, lengths[0])
    rows = width // GROUPS
    for j in range(ffn // 2 // TILE):
        at = pl.multiple_of(side * (ffn // 2) + j * TILE, TILE)
        grad[j] = mm_tn(second[...], d_left[:, pl.ds(at, TILE)])
    place_rows([grad.at[j] for j in range(ffn // 2 // TILE)], keep, send, CONV_BITS, 0, rows)
    start = ffn // 2 // TILE * rows
    half_lanes = pl.ds(pl.multiple_of(side * (half // 2), half // 2), half // 2)
    for tap in range(3):
        grad_conv[tap] = mm_tn(second[...], taps_right[tap, :, half_lanes])

    def conv_slot(p, block, out):
        at = pl.multiple_of(block * rows, rows)
        middle = pl.multiple_of(block * rows + rows // 2, rows // 2)
        h = rows // 2
        out[p, start : start + rows, 0:LANES] = grad_conv[0, pl.ds(at, rows), :].astype(BF16)
        out[p, start + rows : start + rows + h, 0:LANES] = grad_conv[1, pl.ds(at, h), :].astype(BF16)
        out[p, start : start + h, LANES : 2 * LANES] = grad_conv[1, pl.ds(middle, h), :].astype(BF16)
        out[p, start + h : start + h + rows, LANES : 2 * LANES] = grad_conv[
            2, pl.ds(at, rows), :
        ].astype(BF16)

    for_slots(keep, send, CONV_BITS, conv_slot)
    for n in range(width // TILE):
        total = mm_nt(d_left[...], left_w[col(n), :])
        for tap in range(3):
            total = total + mm_nt(taps_right[tap], conv_w[tap, col(n), :])
        d_second[:, col(n)] = total * valid


def glu_back_kernel(
    d_second,
    d_after_conv,
    after_glu,
    joined,
    first,
    stream,
    small_ffn,
    small_attn,
    small_conv,
    glu_w,
    far,
    d_after_glu,
    d_first,
    keep,
    send,
    d_joined,
    rolled,
    blocks,
    grad,
):
    seq, width = d_second.shape
    side = lax.axis_index("head")
    gains = far[0]()
    gain = [gains[k : k + 1, :].astype(F32) for k in range(2)]

    def glu_rows(r, c):
        g_gain, g_shift, g_value, g_gate = c
        rows = pl.ds(r, 32)
        vhat, rate = normalized(after_glu[rows, :])
        e = d_second[rows, :]
        total = d_after_conv[rows, :] + norm_back(vhat, rate, e * gain[1])
        d_after_glu[rows, :] = total
        value = joined[rows, :width]
        gate = joined[rows, width:]
        d_value = (total * gate).astype(BF16)
        d_gate = (total * value * gate * (1.0 - gate)).astype(BF16)
        d_joined[rows, :width] = d_value
        d_joined[rows, width:] = d_gate
        return (
            g_gain + part_sums(e * vhat),
            g_shift + part_sums(e),
            g_value + part_sums(d_value.astype(F32)),
            g_gate + part_sums(d_gate.astype(F32)),
        )

    nothing = jnp.zeros((8, width), F32)
    sums = row_blocks(seq, 32, glu_rows, (nothing,) * 4, unroll=8)
    gain_one, shift_one, g_value, g_gate = (sum_tokens(v) for v in sums)
    for n in range(width // TILE):
        d_first[:, col(n)] = mm_nt(d_joined[...], glu_w[col(n), :])

    sums = [nothing] * 2
    rows = width // GROUPS
    columns = [pl.ds(pl.multiple_of(side * width + j * TILE, TILE), TILE) for j in range(width // TILE)]
    for p in range(8):
        block = slice(p * seq // 8, (p + 1) * seq // 8)
        vhat, _ = normalized(stream[block, :].astype(F32))
        e = d_first[block, :]
        sums = [total + part_sums(v) for total, v in zip(sums, (e * vhat, e))]
        if p < 2 * len(columns):
            part_rows = slice(p % 2 * (width // 2), (p % 2 + 1) * (width // 2))
            grad[p // 2, part_rows, :] = mm_tn(first[:, part_rows], d_joined[:, columns[p // 2]])
    gain_zero, shift_zero = (sum_tokens(v) for v in sums)
    place_rows([grad.at[j] for j in range(len(columns))], keep, send, GLU_BITS, 0, rows)

    blocks[...] = jnp.zeros(blocks.shape, F32)
    rolled[...] = jnp.zeros(rolled.shape, F32)
    vectors = (
        (gain_zero, gain_one, small_attn[0:1, 0:width], small_ffn[1:2, 0:width]),
        (shift_zero, shift_one, small_attn[0:1, width : 2 * width], small_ffn[1:2, width : 2 * width]),
    )
    tiles = width // LANES
    lane = lax.broadcasted_iota(jnp.int32, (8, LANES), 1)
    quarter = LANES // tiles
    for kind, four in enumerate(vectors):
        for k, vector in enumerate(four):
            for t in range(tiles):
                rolled[kind, 8 * k + t : 8 * k + t + 1, :] = vector[:, col(t, LANES)]
        for q in range(tiles):
            total = jnp.zeros((8, LANES), F32)
            for k in range(4):
                moved = pltpu.roll(rolled[kind, 8 * k : 8 * k + 8, :], (quarter * (k - q)) % LANES, 1)
                total = jnp.where((lane >= quarter * k) & (lane < quarter * (k + 1)), moved, total)
            for t in range(tiles):
                blocks[tiles * t + q, 13 + kind : 14 + kind, 0:LANES] = total[t : t + 1, :]
    lane = lane[0:1, :]
    g_out = small_ffn[1:2, 2 * width : 3 * width]
    for s in range(GROUPS):
        source = g_value if s < GROUPS // 2 else g_gate
        place = (s % (GROUPS // 2)) * (2 * width // GROUPS)
        block = source[:, place // LANES * LANES : place // LANES * LANES + LANES]
        glu_part = block if place % LANES == 0 else pltpu.roll(block, LANES - place % LANES, 1)
        place = s * (width // GROUPS)
        block = g_out[:, place // LANES * LANES : place // LANES * LANES + LANES]
        moved = (LANES // 2 - place % LANES) % LANES
        out_part = block if moved == 0 else pltpu.roll(block, moved, 1)
        blocks[s, 15:16, 0:LANES] = jnp.where(
            lane < LANES // 2, glu_part, jnp.where(lane < LANES // 2 + quarter, out_part, 0.0)
        )
        blocks[s, 0:12, 0:LANES] = small_conv[0:12, col(s, LANES)]
        blocks[s, 12:13, 0:LANES] = small_ffn[0:1, col(s, LANES)]
        for k in range(2):
            blocks[s, k : k + 1, LANES : 2 * LANES] = small_conv[12:13, col(k, LANES)]
            blocks[s, 2 + k : 3 + k, LANES : 2 * LANES] = small_attn[
                0:1, 2 * width + k * LANES : 2 * width + (k + 1) * LANES
            ]
    start = width // TILE * rows

    def small_slot(p, block, out):
        out[p, start : start + 16, :] = blocks[block].astype(BF16)

    for_slots(keep, send, GLU_BITS, small_slot)


def tokens_kernel(after_attn, hidden, ffn_out_w, d_after_glu, d_first, stream, far, out_tokens, grad_tokens):
    part, width = out_tokens.shape
    gains, ffn_out_bias = far
    at = pl.multiple_of(lax.axis_index("head") * part, part)
    own = pl.ds(at, part)
    gain, bias = gains()[0:1, :].astype(F32), vector(ffn_out_bias())
    for n in range(width // TILE):
        out_tokens[:, col(n)] = (
            after_attn[own, col(n)] + mm(hidden[own, :], ffn_out_w[:, col(n)]) + bias[:, col(n)]
        ).astype(BF16)

    def rows(r, c):
        block = pl.ds(pl.multiple_of(at + r, 32), 32)
        vhat, rate = normalized(stream[block, :].astype(F32))
        grad_tokens[pl.ds(r, 32), :] = d_after_glu[block, :] + norm_back(vhat, rate, d_first[block, :] * gain)
        return c

    row_blocks(part, 32, rows, unroll=2)


def add_kernel(keeps, gots, far, keep, send):
    at = 0
    for kept, got in zip(keeps, gots):
        rows = kept.shape[1]
        half = kept.shape[0] // 2
        count = kept.shape[0] // len(got)
        for i in range(kept.shape[0]):
            total = kept[i].astype(F32) + got[i // count][i % count].astype(F32)
            out = keep if i < half else send
            out[i % half, at : at + rows, :] = total.astype(BF16)
        at += rows


def finish_early_kernel(mine, other, far, ffn_out, ffn_in, out, qkv, point):
    side = lax.axis_index("head")
    per_row, width = ffn_out.shape
    rows = ffn_in.shape[0]
    for who, grads in ((side, mine), (1 - side, other)):
        count = ffn_in.shape[1] // 2 // TILE
        at = pl.ds(pl.multiple_of(who * TILE, TILE), TILE)
        start = per_row + count * rows
        ffn_out[:, at] = grads[0:per_row, :].astype(F32)
        out[:, at] = grads[start : start + rows, :].astype(F32)
        for j in range(count):
            at = pl.ds(pl.multiple_of((who * count + j) * TILE, TILE), TILE)
            ffn_in[:, at] = grads[per_row + j * rows : per_row + (j + 1) * rows, :].astype(F32)
        count = qkv.shape[1] // 2 // TILE
        for j in range(count):
            at = pl.ds(pl.multiple_of((who * count + j) * TILE, TILE), TILE)
            qkv[:, at] = grads[start + (1 + j) * rows : start + (2 + j) * rows, :].astype(F32)
        start = start + (1 + count) * rows
        at = pl.ds(pl.multiple_of(who * LANES, LANES), LANES)
        point[0 : per_row // 2, at] = grads[start : start + per_row // 2, 0:LANES].astype(F32)
        point[per_row // 2 :, at] = grads[start : start + per_row // 2, LANES : 2 * LANES].astype(F32)


def finish_late_kernel(
    mine,
    other,
    far,
    left,
    conv,
    glu,
    gains,
    shifts,
    depth,
    mid_gain,
    mid_bias,
    left_bias,
    ffn_in_bias,
    glu_bias,
    ffn_out_bias,
    conv_bias,
    point_bias,
):
    side = lax.axis_index("head")
    rows = glu.shape[0]
    h = rows // 2
    count = left.shape[1] // 2 // TILE
    behind = count * rows + 3 * h
    wide = glu.shape[1] // 2 // TILE
    for who, grads in ((side, mine), (1 - side, other)):
        for j in range(count):
            at = pl.ds(pl.multiple_of((who * count + j) * TILE, TILE), TILE)
            left[:, at] = grads[j * rows : (j + 1) * rows, :].astype(F32)
        start = count * rows
        at = pl.ds(pl.multiple_of(who * LANES, LANES), LANES)
        low = grads[start : start + 3 * h, 0:LANES].astype(F32)
        high = grads[start : start + 3 * h, LANES : 2 * LANES].astype(F32)
        conv[0, :, at] = low[0:rows]
        conv[1, 0:h, at] = low[rows:]
        conv[1, h:rows, at] = high[0:h]
        conv[2, :, at] = high[h:]
        for j in range(wide):
            at = pl.ds(pl.multiple_of((who * wide + j) * TILE, TILE), TILE)
            glu[:, at] = grads[behind + j * rows : behind + (j + 1) * rows, :].astype(F32)
    start = behind + wide * rows
    block = mine[start : start + 16, :].astype(F32)
    depth[...] = block[0:9, 0:LANES]
    for k in range(4):
        gains[k : k + 1, :] = block[13:14, k * rows : (k + 1) * rows]
        shifts[k : k + 1, :] = block[14:15, k * rows : (k + 1) * rows]
    mid_gain[...] = block[9, 0:LANES]
    mid_bias[...] = block[10, 0:LANES]
    left_bias[...] = block[11, 0:LANES]
    ffn_in_bias[...] = block[12, 0:LANES]
    glu_bias[...] = block[15, 0 : 2 * rows]
    ffn_out_bias[...] = block[15, 2 * rows : 3 * rows]
    for k in range(2):
        conv_bias[col(k, LANES)] = block[k, LANES : 2 * LANES]
        point_bias[col(k, LANES)] = block[2 + k, LANES : 2 * LANES]


def call(kernel, outs, scratch, near, far, micros=0, scalars=0, kept=()):
    smem = pl.BlockSpec(memory_space=pltpu.SMEM)
    vmem = pl.BlockSpec(memory_space=pltpu.VMEM)
    anywhere = pl.BlockSpec(memory_space=pltpu.HBM)

    near, inside = jax.tree.flatten(near)
    outs, outside = jax.tree.flatten(outs, is_leaf=lambda v: isinstance(v, tuple))
    own = len(outs)
    outs = outs + [(far[i].shape, far[i].dtype) for i in kept]

    def body(*refs):
        inputs = inside.unflatten(refs[: len(near)])
        sources = refs[len(near) : len(near) + len(far)]
        first = len(near) + len(far)
        results = outside.unflatten(refs[first : first + own])
        held = refs[first + own : first + len(outs)]
        rest = refs[first + len(outs) :]
        if not far:
            kernel(*inputs, (), *results, *rest)
            return
        *rest, done = rest
        fresh = iter(rest[len(scratch) :])
        buffers = [held[kept.index(i)] if i in kept else next(fresh) for i in range(len(far))]
        copies = [
            pltpu.make_async_copy(source, buffer, done.at[i])
            for i, (source, buffer) in enumerate(zip(sources, buffers))
        ]
        for copy in copies:
            copy.start()

        def fetched(copy, buffer):
            def get():
                copy.wait()
                return buffer

            return get

        kernel(*inputs, tuple(map(fetched, copies, buffers)), *results, *rest[: len(scratch)])

    temporaries = [pltpu.VMEM(shape, dtype) for shape, dtype in scratch]
    if far:
        temporaries += [pltpu.VMEM(v.shape, v.dtype) for i, v in enumerate(far) if i not in kept]
        temporaries.append(pltpu.SemaphoreType.DMA((len(far),)))
    results = pl.pallas_call(
        body,
        out_shape=tuple(jax.ShapeDtypeStruct(shape, dtype) for shape, dtype in outs),
        in_specs=[smem] * scalars + [vmem] * (len(near) - scalars) + [anywhere] * len(far),
        out_specs=(vmem,) * len(outs),
        scratch_shapes=temporaries,
        compiler_params=pltpu.CompilerParams(vmem_limit_bytes=VMEM_BYTES),
        cost_estimate=pl.CostEstimate(
            flops=micros * 10**9, transcendentals=0, bytes_accessed=micros * 3 * 10**6
        ),
        name=kernel.__name__,
    )(*near, *[pltpu.with_memory_space_constraint(v, pltpu.HBM) for v in far])
    return [*outside.unflatten(results[:own]), *results[own:]]


def per_device(
    tokens,
    lengths,
    cotangent,
    glu_weight,
    glu_bias,
    norm_gain,
    norm_bias,
    mid_gain,
    mid_bias,
    left_weight,
    left_bias,
    conv_weight,
    conv_bias,
    depth_weight,
    point_weight,
    point_bias,
    qkv_weight,
    out_weight,
    ffn_in_weight,
    ffn_in_bias,
    ffn_out_weight,
    ffn_out_bias,
):
    row_count, part, width = tokens.shape
    assert row_count == 1 and lax.axis_size("head") == 2
    seq = 2 * part
    shards = lax.axis_size("dp")
    below = shards // GROUPS
    assert below * GROUPS == shards
    heads = width // HEAD_DIM
    half = conv_weight.shape[2]
    ffn = left_weight.shape[1]
    swap = [(0, 1), (1, 0)]
    mine = tokens[0]
    cot_mine = cotangent[0]
    other = lax.ppermute(mine, "head", swap)
    cot_other = lax.ppermute(cot_mine, "head", swap)

    def slot_outs(rows, pieces=1):
        count = GROUPS // 2
        return [((count, rows, TILE), BF16), [((count // pieces, rows, TILE), BF16)] * pieces]

    rows = width // GROUPS
    per_row = ffn // GROUPS
    ffn_rows = per_row + ffn // 2 // TILE * rows
    own_first, own_joined, own_after_glu, own_second, mine, glu_w, conv_w, left_w, point_w = call(
        open_kernel,
        [
            ((part, width), BF16),
            ((part, 2 * width), F32),
            ((part, width), F32),
            ((part, width), BF16),
        ],
        [],
        [lengths],
        [mine, norm_gain, norm_bias, glu_bias, glu_weight, conv_weight, left_weight, point_weight],
        micros=1,
        scalars=1,
        kept=(0, 4, 5, 6, 7),
    )
    (
        stream,
        first_norm,
        joined,
        after_glu,
        second,
        left_pre,
        right_pre,
        depth_low,
        after_conv,
        fourth,
        packed,
        probs,
        context,
        after_attn,
        fifth,
        hidden,
        vhat,
        rates,
        qkv_w,
        out_w,
        ffn_in_w,
        ffn_out_w,
    ) = call(
        forward_kernel,
        [
            ((seq, width), BF16),
            ((seq, width), BF16),
            ((seq, 2 * width), F32),
            ((seq, width), F32),
            ((seq, width), BF16),
            ((seq, ffn), F32),
            ((seq, half), F32),
            ((seq, ffn), BF16),
            ((seq, width), F32),
            ((seq, width), BF16),
            ((seq, 3 * width), BF16),
            ((heads, seq, seq), F32),
            ((seq, width), BF16),
            ((seq, width), F32),
            ((seq, width), BF16),
            ((seq, ffn), BF16),
            ((ffn // LANES, seq, LANES), F32),
            ((seq, LANES), F32),
        ],
        [
            ((seq + 16, LANES), F32),
            ((2, seq + 16, half), F32),
            ((2, ffn), F32),
            ((seq, LANES), F32),
        ],
        [
            lengths,
            other,
            mine,
            own_first,
            own_joined,
            own_after_glu,
            own_second,
            glu_w,
            conv_w,
            left_w,
            point_w,
        ],
        [
            norm_gain,
            norm_bias,
            glu_bias,
            conv_bias,
            left_bias,
            mid_gain,
            mid_bias,
            depth_weight,
            point_bias,
            qkv_weight,
            out_weight,
            ffn_in_bias,
            ffn_in_weight,
            ffn_out_weight,
        ],
        micros=14,
        scalars=1,
        kept=(9, 10, 12, 13),
    )
    d_after, small_ffn, keep_ffn, send_ffn = call(
        ffn_back_kernel,
        [((seq, width), F32), ((8, ffn), F32)] + slot_outs(ffn_rows),
        [
            ((seq, width), BF16),
            ((seq, ffn), BF16),
            ((seq, width), F32),
            ((ffn // 2 // TILE, width, TILE), F32),
        ],
        [cot_other, after_attn, fifth, hidden, ffn_in_w, ffn_out_w],
        [cot_mine, norm_gain],
        micros=5,
    )

    class Chunk:
        def __init__(self, keep, send, bits):
            self.keep, self.send, self.bits = keep, send, list(bits)

        def start(self):
            if not self.bits:
                self.got = [lax.ppermute(self.keep, "head", swap)]
                return
            step = below << self.bits.pop(0)
            pairs = [(i, i ^ step) for i in range(shards)]
            self.got = [lax.ppermute(v, "dp", pairs) for v in self.send]

    def last_sum(keep, got):
        total = (keep[0].astype(F32) + got[0].astype(F32)).astype(BF16)
        step = 1
        while step < below:
            total = total + lax.ppermute(total, "dp", [(i, i ^ step) for i in range(shards)])
            step *= 2
        return total

    def added(*chunks, whole=False):
        keep = chunks[0].keep
        if keep.shape[0] == 1:
            return last_sum(keep, chunks[0].got[0]), None
        if len(chunks) == 1 and len(chunks[0].got) < 3 and not whole:
            (c,) = chunks
            n = keep.shape[0] // 2
            got = c.got if len(c.got) == 2 else (c.got[0][:n], c.got[0][n:])
            return tuple(
                (keep[half * n : half * n + n].astype(F32) + got[half].astype(F32)).astype(BF16)
                for half in range(2)
            )
        shape = ((keep.shape[0] // 2, sum(c.keep.shape[1] for c in chunks), TILE), BF16)
        return call(
            add_kernel, [shape, shape], [], [[c.keep for c in chunks], [c.got for c in chunks]], []
        )

    def received(held, *chunks):
        held, gots = lax.optimization_barrier((held, [c.got for c in chunks]))
        for c, got in zip(chunks, gots):
            c.got = got
        return held

    def wave(held, *chunks, joined=False, whole=True):
        held = received(held, *chunks)
        groups = [chunks] if joined else [(c,) for c in chunks]
        nexts = [Chunk(*added(*group, whole=whole), group[0].bits) for group in groups]
        held, keeps = lax.optimization_barrier((held, [(c.keep, c.send) for c in nexts]))
        for c, (keep, send) in zip(nexts, keeps):
            c.keep, c.send = keep, [send]
            c.start()
        return (held, *nexts)

    ffn_grads = Chunk(keep_ffn, send_ffn, (0, *FFN_BITS))
    ffn_grads.start()
    d_after_conv, small_attn, keep_attn, send_attn = call(
        attention_back_kernel,
        [((seq, width), F32), ((8, ffn), F32)] + slot_outs(4 * rows + per_row // 2),
        [
            ((seq, width), BF16),
            ((seq, width), BF16),
            ((seq, 3 * width), BF16),
            ((seq, width), F32),
            ((seq, half), BF16),
            ((4, width, TILE), F32),
        ],
        [d_after, packed, probs, context, fourth, after_conv, depth_low, out_w, qkv_w],
        [norm_gain],
        micros=10,
    )
    d_after_conv, ffn_grads = wave(d_after_conv, ffn_grads, whole=False)
    attn_grads = Chunk(keep_attn, send_attn, (0, *ATTN_BITS))
    attn_grads.start()
    d_after_conv, attn_grads = wave(d_after_conv, attn_grads, whole=True)
    d_left, taps_right, small_conv = call(
        middle_back_kernel,
        [((seq, ffn), BF16), ((3, seq, half), BF16), ((16, ffn), F32)],
        [
            ((ffn // LANES, seq + 16, LANES), F32),
            ((ffn // LANES, seq, LANES), F32),
            ((2, seq, LANES), F32),
            ((seq + 16, half), F32),
            ((2, ffn), F32),
            ((seq, LANES), F32),
            ((ffn // LANES, 8, LANES), F32),
        ],
        [lengths, d_after_conv, left_pre, right_pre, vhat, rates, point_w],
        [mid_gain, mid_bias, depth_weight],
        micros=0,
        scalars=1,
    )
    d_second, keep_conv, send_conv = call(
        conv_back_kernel,
        [((seq, width), F32)] + slot_outs(ffn // 2 // TILE * rows + 3 * rows // 2, 1),
        [((ffn // 2 // TILE, width, TILE), F32), ((3, width, LANES), F32)],
        [lengths, d_left, taps_right, second, left_w, conv_w],
        [],
        micros=0,
        scalars=1,
    )
    conv_grads = Chunk(keep_conv, send_conv, (0, *CONV_BITS))
    conv_grads.start()
    d_second, ffn_grads, attn_grads = wave(d_second, ffn_grads, attn_grads, whole=False)
    d_second, conv_grads = wave(d_second, conv_grads)
    d_after_glu, d_first, keep_glu, send_glu = call(
        glu_back_kernel,
        [((seq, width), F32)] * 2 + slot_outs(width // TILE * rows + 16, 2),
        [
            ((seq, 2 * width), BF16),
            ((2, 32, LANES), F32),
            ((GROUPS, 16, 2 * LANES), F32),
            ((width // TILE, width, TILE), F32),
        ],
        [
            d_second,
            d_after_conv,
            after_glu,
            joined,
            first_norm,
            stream,
            small_ffn,
            small_attn,
            small_conv,
            glu_w,
        ],
        [norm_gain],
        micros=7,
    )
    glu_grads = Chunk(keep_glu, send_glu, (0, *GLU_BITS))
    glu_grads.start()
    held = received(d_after_glu, ffn_grads, attn_grads)
    held, glu_grads = wave(held, glu_grads)
    held, early = wave(held, ffn_grads, attn_grads, joined=True)
    held, conv_grads = wave(held, conv_grads)
    out_tokens, grad_tokens = call(
        tokens_kernel,
        [((part, width), BF16), ((part, width), F32)],
        [],
        [after_attn, hidden, ffn_out_w, held, d_first, stream],
        [norm_gain, ffn_out_bias],
    )
    grad_tokens, glu_grads = wave(grad_tokens, glu_grads)
    held, late = wave(grad_tokens, conv_grads, glu_grads, joined=True)
    held, early = wave(held, early)
    grad_tokens, late = wave(held, late)
    other = early.got[0]
    ffn_out, ffn_in, out, qkv, point = call(
        finish_early_kernel,
        [
            ((per_row, width), F32),
            ((rows, ffn), F32),
            ((rows, width), F32),
            ((rows, 3 * width), F32),
            ((per_row, half), F32),
        ],
        [],
        [early.keep, other],
        [],
    )
    (
        left,
        conv,
        glu,
        g_gains,
        g_shifts,
        g_depth,
        g_mid_gain,
        g_mid_bias,
        g_left_bias,
        g_ffn_in_bias,
        g_glu_bias,
        g_ffn_out_bias,
        g_conv_bias,
        g_point_bias,
    ) = call(
        finish_late_kernel,
        [
            ((rows, ffn), F32),
            ((3, rows, half), F32),
            ((rows, 2 * width), F32),
            ((4, rows), F32),
            ((4, rows), F32),
            ((9, LANES), F32),
            ((LANES,), F32),
            ((LANES,), F32),
            ((LANES,), F32),
            ((LANES,), F32),
            ((2 * rows,), F32),
            ((rows,), F32),
            ((half,), F32),
            ((half,), F32),
        ],
        [],
        [late.keep, late.got[0]],
        [],
    )
    results = (
        (glu, 0),
        (g_glu_bias, 0),
        (g_gains, 1),
        (g_shifts, 1),
        (g_mid_gain, 0),
        (g_mid_bias, 0),
        (left, 0),
        (g_left_bias, 0),
        (conv, 1),
        (g_conv_bias, None),
        (g_depth, 1),
        (point, 0),
        (g_point_bias, None),
        (qkv, 0),
        (out, 0),
        (ffn_in, 0),
        (g_ffn_in_bias, 0),
        (ffn_out, 0),
        (g_ffn_out_bias, 0),
    )
    final = []
    for value, axis in results:
        if axis is not None and below > 1:
            size = value.shape[axis] // below
            value = lax.dynamic_slice_in_dim(value, lax.axis_index("dp") % below * size, size, axis)
        final.append(value)
    return (out_tokens[None], grad_tokens[None], *final)


def solution(mesh):
    return jax.shard_map(
        per_device,
        mesh=mesh,
        in_specs=(P("dp", "head", None), P("dp"), P("dp", "head", None)) + (P(),) * 19,
        out_specs=(
            P("dp", "head", None),
            P("dp", "head", None),
            P("dp", None),
            P("dp"),
            P(None, "dp"),
            P(None, "dp"),
            P("dp"),
            P("dp"),
            P("dp", None),
            P("dp"),
            P(None, "dp", None),
            P(),
            P(None, "dp"),
            P("dp", None),
            P(),
            P("dp", None),
            P("dp", None),
            P("dp", None),
            P("dp"),
            P("dp", None),
            P("dp"),
        ),
        check_vma=False,
    )
```

```python
import functools

import jax
import jax.numpy as jnp
from jax import lax
from jax.experimental import pallas as pl
from jax.experimental.pallas import tpu as pltpu
from jax.sharding import PartitionSpec as P

HEAD_DIM = 64
EPSILON = 1e-06
LANES = 128
TILE = 256
GROUPS = 16
F32 = jnp.float32
BF16 = jnp.bfloat16
VMEM_BYTES = 28 * 1024 * 1024
FFN_BITS = (1, 2, 3)
ATTN_BITS = (2, 1, 3)
CONV_BITS = (1, 2, 3)
GLU_BITS = (2, 1, 3)


def mm(a, b):
    return lax.dot_general(a, b, (((1,), (0,)), ((), ())), preferred_element_type=F32)


def mm_nt(a, b):
    return lax.dot_general(a, b, (((1,), (1,)), ((), ())), preferred_element_type=F32)


def mm_tn(a, b):
    return lax.dot_general(a, b, (((0,), (0,)), ((), ())), preferred_element_type=F32)


def mean(v):
    return jnp.mean(v, axis=-1, keepdims=True)


def normalized(v):
    centred = v - mean(v)
    rate = lax.rsqrt(mean(centred * centred) + EPSILON)
    return centred * rate, rate


def norm_back(vhat, rate, gained):
    return (gained - mean(gained) - vhat * mean(gained * vhat)) * rate


def sum_tokens(v):
    return jnp.sum(v, axis=0, keepdims=True)


def part_sums(v):
    return jnp.sum(v.reshape(v.shape[0] // 8, 8, v.shape[1]), axis=0)


def row_blocks(total, step, body, carry=0, unroll=1):
    def visit(i, c):
        return body(pl.multiple_of(i * step, step), c)

    return lax.fori_loop(0, total // step, visit, carry, unroll=unroll)


def valid_rows(start, count, length):
    places = start + lax.broadcasted_iota(jnp.int32, (count, 1), 0)
    return (places < length).astype(F32)


def col(n, width=TILE):
    return slice(n * width, (n + 1) * width)


def vector(ref):
    return ref[...].astype(F32).reshape(1, ref.shape[0])


def slot_block(p, sent, bits):
    group = lax.axis_index("dp") // (lax.axis_size("dp") // GROUPS)
    wanted = ((p >> 2) & 1) << bits[0] | ((p >> 1) & 1) << bits[1] | (p & 1) << bits[2]
    return group ^ (wanted | sent)


def for_slots(keep, send, bits, body, unroll=1):
    count = GROUPS // 2 // len(send)
    for i, piece in enumerate(send):

        def visit(q, c, i=i, piece=piece):
            p = i * count + q
            body(p, slot_block(p, 0, bits), keep)
            body(q, slot_block(p, 1, bits), piece)
            return c

        lax.fori_loop(0, count, visit, 0, unroll=unroll)


def place_rows(grads, keep, send, bits, at, rows):
    def one(p, block, out):
        source = pl.ds(pl.multiple_of(block * rows, rows), rows)
        for j, grad in enumerate(grads):
            out[p, at + j * rows : at + (j + 1) * rows, :] = grad[source, :].astype(BF16)

    for_slots(keep, send, bits, one)


def gated(tokens, at, place, length, gain, shift, glu_b, glu_w, first, joined, after_glu, second):
    part, width = tokens.shape

    def first_rows(r, c):
        vhat, _ = normalized(tokens[pl.ds(r, 64), :].astype(F32))
        first[pl.ds(pl.multiple_of(at + r, 64), 64), :] = (vhat * gain[0] + shift[0]).astype(BF16)
        return c

    row_blocks(part, 64, first_rows, unroll=2)
    every = pl.ds(at, part)
    for n in range(2 * width // TILE):
        joined[every, col(n)] = mm(first[every, :], glu_w[:, col(n)]) + glu_b[:, col(n)]

    def glu_rows(r, c):
        rows = pl.ds(pl.multiple_of(at + r, 32), 32)
        gate = jax.nn.sigmoid(joined[rows, width:])
        joined[rows, width:] = gate
        v = tokens[pl.ds(r, 32), :].astype(F32) + joined[rows, :width] * gate
        after_glu[rows, :] = v
        vhat, _ = normalized(v)
        valid = valid_rows(place + r, 32, length)
        second[rows, :] = ((vhat * gain[1] + shift[1]) * valid).astype(BF16)
        return c

    row_blocks(part, 32, glu_rows, unroll=4)


def open_kernel(lengths, far, first, joined, after_glu, second):
    mine, gains, shifts, glu_bias, glu_w, conv_w = far
    part = first.shape[0]
    tokens, gains, shifts = mine(), gains(), shifts()
    gain = [gains[k : k + 1, :].astype(F32) for k in range(2)]
    shift = [shifts[k : k + 1, :].astype(F32) for k in range(2)]
    place = lax.axis_index("head") * part
    glu_b, glu_w = vector(glu_bias()), glu_w()
    gated(tokens, 0, place, lengths[0], gain, shift, glu_b, glu_w, first, joined, after_glu, second)
    conv_w()


def forward_kernel(
    lengths,
    other,
    mine,
    own_first,
    own_joined,
    own_after_glu,
    own_second,
    glu_w,
    conv_w,
    far,
    stream,
    first,
    joined,
    after_glu,
    second,
    left_pre,
    right_pre,
    depth_low,
    after_conv,
    fourth,
    packed,
    probs,
    context,
    after_attn,
    fifth,
    hidden,
    vhat,
    rates,
    third,
    sides,
    mid_row,
    mask,
):
    part, width = other.shape
    seq = 2 * part
    ffn = left_pre.shape[1]
    half = right_pre.shape[1]
    side = lax.axis_index("head")
    length = lengths[0]
    own = pl.ds(pl.multiple_of(side * part, part), part)
    opposite = pl.multiple_of((1 - side) * part, part)
    (
        gains,
        shifts,
        glu_bias,
        conv_bias,
        left_bias,
        left_w,
        mid_gain,
        mid_bias,
        depth_w,
        point_bias,
        point_w,
        qkv_w,
        out_w,
        ffn_in_bias,
        ffn_in_w,
        ffn_out_w,
    ) = far
    for whole, piece in (
        (stream, mine),
        (first, own_first),
        (joined, own_joined),
        (after_glu, own_after_glu),
        (second, own_second),
    ):
        whole[own, :] = piece[...]
    stream[pl.ds(opposite, part), :] = other[...]
    gains, shifts = gains(), shifts()
    gain = [gains[k : k + 1, :].astype(F32) for k in range(4)]
    shift = [shifts[k : k + 1, :].astype(F32) for k in range(4)]
    gated(
        other, opposite, opposite, length, gain, shift, vector(glu_bias()), glu_w, first, joined, after_glu, second
    )
    blank = jnp.zeros((8, half), F32)
    for k in range(2):
        sides[k, 0:8, :] = blank
        sides[k, 8 + seq : 16 + seq, :] = blank
    sides[0, 8 : 8 + seq, :] = mm(second[...], conv_w[0])
    sides[1, 8 : 8 + seq, :] = mm(second[...], conv_w[2])
    right_pre[...] = mm(second[...], conv_w[1]) + vector(conv_bias())
    right_pre[...] = right_pre[...] + sides[0, 7 : 7 + seq, :] + sides[1, 9 : 9 + seq, :]
    left_b, left_w = vector(left_bias()), left_w()
    for n in range(ffn // TILE):
        left_pre[:, col(n)] = mm(second[...], left_w[:, col(n)]) + left_b[:, col(n)]
    mid_row[0:1, :], mid_row[1:2, :] = vector(mid_gain()), vector(mid_bias())
    depth_w = depth_w()
    chunks = ffn // LANES
    edge = jnp.zeros((8, LANES), F32)
    third[0:8, :] = edge
    third[8 + seq : 16 + seq, :] = edge
    mask[...] = (lax.broadcasted_iota(jnp.int32, (seq, LANES), 0) < length).astype(F32)

    def mid_rows(r, c):
        rows = pl.ds(r, 16)
        v, rate = normalized(combine(left_pre[rows, :], right_pre[rows, :]))
        rates[rows, :] = jnp.broadcast_to(rate, (16, LANES))
        for k in range(chunks):
            vhat[k, rows, :] = v[:, col(k, LANES)]
        return c

    row_blocks(seq, 16, mid_rows, unroll=8)

    def depth_lanes(k, c):
        lanes = pl.ds(pl.multiple_of(k * LANES, LANES), LANES)
        taps = depth_w[:, lanes].astype(F32)
        mid_gains, mid_shifts = mid_row[0:1, lanes], mid_row[1:2, lanes]
        step = 64
        for r in range(0, seq, step):
            block = slice(r, r + step)
            third[8 + r : 8 + r + step, :] = (vhat[k, block, :] * mid_gains + mid_shifts) * mask[block, :]
        for r in range(0, seq, step):
            total = third[4 + r : 4 + r + step, :] * taps[0:1, :]
            for j in range(1, 9):
                total = total + third[4 + j + r : 4 + j + r + step, :] * taps[j : j + 1, :]
            depth_low[r : r + step, lanes] = total.astype(BF16)
        return c

    lax.fori_loop(0, chunks, depth_lanes, 0, unroll=2)
    after_conv[:, :half] = (
        after_glu[:, :half] + mm(depth_low[...], point_w()[...]) + vector(point_bias())
    )
    after_conv[:, half:] = after_glu[:, half:]

    def fourth_rows(r, c):
        rows = pl.ds(r, 64)
        vhat, _ = normalized(after_conv[rows, :])
        fourth[rows, :] = (vhat * gain[2] + shift[2]).astype(BF16)
        return c

    row_blocks(seq, 64, fourth_rows, unroll=4)
    qkv_w = qkv_w()
    for n in range(3 * width // TILE):
        packed[:, col(n)] = mm(fourth[...], qkv_w[:, col(n)]).astype(BF16)

    low_lanes = lax.broadcasted_iota(jnp.int32, (1, LANES), 1) < HEAD_DIM
    scale = HEAD_DIM ** (-0.5)

    def head_pair(p, c):
        lanes = pl.ds(pl.multiple_of(p * LANES, LANES), LANES)
        q = packed[:, lanes].astype(F32) * scale
        k = packed[:, pl.ds(pl.multiple_of(width + p * LANES, LANES), LANES)]
        v = packed[:, pl.ds(pl.multiple_of(2 * width + p * LANES, LANES), LANES)]
        open_keys = lax.broadcasted_iota(jnp.int32, (seq, 1), 0) < length
        results = []
        for e in range(2):
            q_one = jnp.where(low_lanes if e == 0 else ~low_lanes, q, 0.0).astype(BF16)
            s = jnp.where(open_keys, mm_nt(k, q_one), -1000000000.0)
            raised = jnp.exp(s - jnp.max(s, axis=0, keepdims=True))
            chance = raised * (1.0 / jnp.sum(raised, axis=0, keepdims=True))
            probs[2 * p + e] = chance
            results.append(mm_tn(v, chance.astype(BF16)))
        both = jnp.concatenate([results[0][:HEAD_DIM], results[1][HEAD_DIM:]], axis=0)
        context[:, lanes] = both.T.astype(BF16)
        return c

    lax.fori_loop(0, width // LANES, head_pair, 0, unroll=4)
    out_w = out_w()
    for n in range(width // TILE):
        after_attn[:, col(n)] = after_conv[:, col(n)] + mm(context[...], out_w[:, col(n)])

    def fifth_rows(r, c):
        rows = pl.ds(r, 64)
        vhat, _ = normalized(after_attn[rows, :])
        fifth[rows, :] = (vhat * gain[3] + shift[3]).astype(BF16)
        return c

    row_blocks(seq, 64, fifth_rows, unroll=4)
    ffn_in_b, ffn_in_w = vector(ffn_in_bias()), ffn_in_w()
    for n in range(ffn // TILE):
        pre = mm(fifth[...], ffn_in_w[:, col(n)]) + ffn_in_b[:, col(n)]
        hidden[:, col(n)] = jnp.where(pre > 0.0, pre, 0.0).astype(BF16)
    ffn_out_w()


def ffn_back_kernel(
    cot_other,
    after_attn,
    fifth,
    hidden,
    ffn_in_w,
    ffn_out_w,
    far,
    d_after,
    small,
    keep,
    send,
    cot,
    d_hidden,
    d_fifth,
    grad,
):
    seq, width = fifth.shape
    part = seq // 2
    ffn = hidden.shape[1]
    side = lax.axis_index("head")
    cot_mine, gains = far
    own = pl.ds(pl.multiple_of(side * part, part), part)
    opposite = pl.ds(pl.multiple_of((1 - side) * part, part), part)
    cot[opposite, :] = cot_other[...]
    cot[own, :] = cot_mine()[...]
    for n in range(ffn // TILE):
        back = mm_nt(cot[...], ffn_out_w[col(n), :])
        back = jnp.where(hidden[:, col(n)].astype(F32) > 0.0, back, 0.0).astype(BF16)
        d_hidden[:, col(n)] = back
        small[0:1, col(n)] = sum_tokens(back.astype(F32))
    for n in range(width // TILE):
        d_fifth[:, col(n)] = mm_nt(d_hidden[...], ffn_in_w[col(n), :])

    cot_half = cot[:, pl.ds(pl.multiple_of(side * (width // 2), width // 2), width // 2)]
    per_row = ffn // GROUPS
    gain = gains()[3:4, :].astype(F32)
    sums = [jnp.zeros((8, width), F32)] * 3
    for p in range(GROUPS // 2):
        block = slice(p * seq // 8, (p + 1) * seq // 8)
        vhat, rate = normalized(after_attn[block, :])
        e = d_fifth[block, :]
        given = cot[block, :].astype(F32)
        d_after[block, :] = given + norm_back(vhat, rate, e * gain)
        sums = [total + part_sums(v) for total, v in zip(sums, (e * vhat, e, given))]
        count = GROUPS // 2 // len(send)
        for sent, out, place in ((0, keep, p), (1, send[p // count], p % count)):
            at = pl.multiple_of(slot_block(p, sent, FFN_BITS) * per_row, per_row)
            out[place, 0:per_row, :] = mm_tn(hidden[:, pl.ds(at, per_row)], cot_half).astype(BF16)
    for k in range(3):
        small[1:2, k * width : (k + 1) * width] = sum_tokens(sums[k])

    rows = width // GROUPS
    for j in range(ffn // 2 // TILE):
        at = pl.multiple_of(side * (ffn // 2) + j * TILE, TILE)
        grad[j] = mm_tn(fifth[...], d_hidden[:, pl.ds(at, TILE)])
    count = ffn // 2 // TILE
    place_rows([grad.at[j] for j in range(count)], keep, send, FFN_BITS, per_row, rows)


def combine(left_pre, right_pre):
    half = right_pre.shape[1]
    left = jnp.maximum(left_pre, 0.0)
    return jnp.concatenate([left[:, :half] + jnp.maximum(right_pre, 0.0), left[:, half:]], axis=1)


def attention_back_kernel(
    d_after,
    packed,
    probs,
    context,
    fourth,
    after_conv,
    depth_low,
    out_w,
    qkv_w,
    far,
    d_after_conv,
    small,
    keep,
    send,
    d_attn,
    d_context,
    d_packed,
    d_fourth,
    d_sep,
    grad,
):
    seq, width = d_after.shape
    side = lax.axis_index("head")
    (gains,) = far
    half = d_sep.shape[1]
    ffn = depth_low.shape[1]
    rows = width // GROUPS
    d_attn[...] = d_after[...].astype(BF16)
    for n in range(width // TILE):
        d_context[:, col(n)] = mm_nt(d_attn[...], out_w[col(n), :]).astype(BF16)
    low_lanes = lax.broadcasted_iota(jnp.int32, (1, LANES), 1) < HEAD_DIM
    scale = HEAD_DIM ** (-0.5)

    def head_pair(p, c):
        lanes = pl.ds(pl.multiple_of(p * LANES, LANES), LANES)
        k_lanes = pl.ds(pl.multiple_of(width + p * LANES, LANES), LANES)
        v_lanes = pl.ds(pl.multiple_of(2 * width + p * LANES, LANES), LANES)
        q = packed[:, lanes]
        k = packed[:, k_lanes]
        v = packed[:, v_lanes].astype(F32)
        given = d_context[:, lanes]
        dq, dk, dv = [], [], []
        for e in range(2):
            one = jnp.where(low_lanes if e == 0 else ~low_lanes, v, 0.0).astype(BF16)
            chance = probs[2 * p + e]
            d_probs = mm_nt(one, given)
            delta = jnp.sum(d_probs * chance, axis=0, keepdims=True)
            d_scores = (chance * (d_probs - delta)).astype(BF16)
            dv.append(mm(chance.astype(BF16), given))
            dk.append(mm(d_scores, q))
            dq.append(mm_tn(k, d_scores))
        both = jnp.concatenate([dq[0][:HEAD_DIM], dq[1][HEAD_DIM:]], axis=0)
        d_packed[:, lanes] = (both.T * scale).astype(BF16)
        d_packed[:, k_lanes] = (jnp.where(low_lanes, dk[0], dk[1]) * scale).astype(BF16)
        d_packed[:, v_lanes] = jnp.where(low_lanes, dv[0], dv[1]).astype(BF16)
        return c

    lax.fori_loop(0, width // LANES, head_pair, 0, unroll=4)
    for n in range(width // TILE):
        d_fourth[:, col(n)] = mm_nt(d_packed[...], qkv_w[col(n), :])
    gain = gains()[2:3, :].astype(F32)

    sums = [jnp.zeros((8, width), F32)] * 2
    g_point = jnp.zeros((8, half), F32)
    at = pl.multiple_of(side * (width // 2), width // 2)
    sides = [(context, d_attn, at)]
    for j in range(3 * width // 2 // TILE):
        sides.append((fourth, d_packed, pl.multiple_of(side * (3 * width // 2) + j * TILE, TILE)))
    for p in range(2 * len(sides)):
        block = slice(p * seq // 8, (p + 1) * seq // 8)
        vhat, rate = normalized(after_conv[block, :])
        e = d_fourth[block, :]
        total = d_after[block, :] + norm_back(vhat, rate, e * gain)
        d_after_conv[block, :] = total
        sep = total[:, :half].astype(BF16)
        d_sep[block, :] = sep
        sums = [total + part_sums(v) for total, v in zip(sums, (e * vhat, e))]
        g_point = g_point + part_sums(sep.astype(F32))
        values, incoming, at = sides[p // 2]
        part = slice(p % 2 * (width // 2), (p % 2 + 1) * (width // 2))
        grad[p // 2, part, :] = mm_tn(values[:, part], incoming[:, pl.ds(at, TILE)])
    small[0:1, 0:width] = sum_tokens(sums[0])
    small[0:1, width : 2 * width] = sum_tokens(sums[1])
    small[0:1, 2 * width : 2 * width + half] = sum_tokens(g_point)
    place_rows([grad.at[j] for j in range(len(sides))], keep, send, ATTN_BITS, 0, rows)
    sep_half = d_sep[:, pl.ds(pl.multiple_of(side * (half // 2), half // 2), half // 2)]
    per_row = ffn // GROUPS

    def point_slot(p, block, out):
        g = mm_tn(
            depth_low[:, pl.ds(pl.multiple_of(block * per_row, per_row), per_row)], sep_half
        ).astype(BF16)
        out[p, 4 * rows : 4 * rows + per_row // 2, 0:LANES] = g[: per_row // 2]
        out[p, 4 * rows : 4 * rows + per_row // 2, LANES : 2 * LANES] = g[per_row // 2 :]

    for_slots(keep, send, ATTN_BITS, point_slot, unroll=8)


def depth_back_kernel(d_after_conv, point_w, far, d_depth):
    seq = d_after_conv.shape[0]
    ffn, half = point_w.shape
    chunks = ffn // LANES
    edge = jnp.zeros((8, LANES), F32)
    for k in range(chunks):
        d_depth[k, 0:8, :] = edge
        d_depth[k, 8 + seq : 16 + seq, :] = edge
    d_sep = d_after_conv[:, :half].astype(BF16)
    for n in range(ffn // TILE):
        block = mm_nt(d_sep, point_w[col(n), :])
        for m in range(TILE // LANES):
            d_depth[n * (TILE // LANES) + m, 8 : 8 + seq, :] = block[:, col(m, LANES)]


def middle_back_kernel(
    lengths,
    d_depth,
    left_pre,
    right_pre,
    vhat3,
    rates,
    far,
    d_left,
    taps_right,
    small,
    d_third,
    sums,
    d_right,
    mid_row,
    mask,
    left_sums,
):
    seq = left_pre.shape[0]
    ffn = left_pre.shape[1]
    half = right_pre.shape[1]
    length = lengths[0]
    mid_gain, mid_bias, depth_w = far
    chunks = ffn // LANES
    mid_row[0:1, :], mid_row[1:2, :] = vector(mid_gain()), vector(mid_bias())
    depth_w = depth_w()
    mask[...] = (lax.broadcasted_iota(jnp.int32, (seq, LANES), 0) < length).astype(F32)
    sums[...] = jnp.zeros(sums.shape, F32)
    step = 64

    def depth_lanes(k, c):
        lanes = pl.ds(pl.multiple_of(k * LANES, LANES), LANES)
        taps = depth_w[:, lanes].astype(F32)
        mid_lanes, low_lanes = mid_row[0:1, lanes], mid_row[1:2, lanes]
        totals = [jnp.zeros((8, LANES), F32)] * 11
        for r in range(0, seq, step):
            block = slice(r, r + step)
            vhat = vhat3[k, block, :]
            here = (vhat * mid_lanes + low_lanes) * mask[block, :]
            total = None
            for j in range(9):
                moved = d_depth[k, 12 - j + r : 12 - j + r + step, :]
                totals[j] = totals[j] + part_sums(moved * here)
                term = moved * taps[j : j + 1, :]
                total = term if total is None else total + term
            total = total * mask[block, :]
            totals[9] = totals[9] + part_sums(total * vhat)
            totals[10] = totals[10] + part_sums(total)
            gained = total * mid_lanes
            d_third[k, block, :] = gained
            sums[0, block, :] = sums[0, block, :] + gained
            sums[1, block, :] = sums[1, block, :] + gained * vhat
        for j in range(11):
            small[j : j + 1, lanes] = sum_tokens(totals[j])
        return c

    lax.fori_loop(0, chunks, depth_lanes, 0, unroll=2)
    inverse = 1.0 / ffn
    sums[0] = jnp.broadcast_to(jnp.sum(sums[0], axis=-1, keepdims=True) * inverse, (seq, LANES))
    sums[1] = jnp.broadcast_to(jnp.sum(sums[1], axis=-1, keepdims=True) * inverse, (seq, LANES))

    def combined_lanes(k):
        return (d_third[k] - sums[0] - vhat3[k] * sums[1]) * rates[...]

    left_sums[...] = jnp.zeros(left_sums.shape, F32)
    for r in range(0, seq, step):
        block = slice(r, r + step)
        first, second, rate = sums[0, block, :], sums[1, block, :], rates[block, :]

        def left_lanes(k, c, block=block, first=first, second=second, rate=rate):
            lanes = pl.ds(pl.multiple_of(k * LANES, LANES), LANES)
            v = (d_third[k, block, :] - first - vhat3[k, block, :] * second) * rate
            v = jnp.where(left_pre[block, lanes] > 0.0, v, 0.0).astype(BF16)
            d_left[block, lanes] = v
            left_sums[k] = left_sums[k] + part_sums(v.astype(F32))
            return c

        lax.fori_loop(0, chunks, left_lanes, 0, unroll=2)
    for k in range(chunks):
        small[11:12, col(k, LANES)] = sum_tokens(left_sums[k])
    blank = jnp.zeros((8, half), F32)
    d_right[0:8, :] = blank
    d_right[8 + seq : 16 + seq, :] = blank
    for k in range(half // LANES):
        v = jnp.where(right_pre[:, col(k, LANES)] > 0.0, combined_lanes(k), 0.0).astype(BF16)
        v = v.astype(F32)
        d_right[8 : 8 + seq, col(k, LANES)] = v
        small[12:13, col(k, LANES)] = sum_tokens(v)
    taps_right[0] = d_right[9 : 9 + seq, :].astype(BF16)
    taps_right[1] = d_right[8 : 8 + seq, :].astype(BF16)
    taps_right[2] = d_right[7 : 7 + seq, :].astype(BF16)


def conv_back_kernel(
    lengths,
    d_left,
    taps_right,
    second,
    left_w,
    conv_w,
    far,
    d_second,
    keep,
    send,
    grad,
    grad_conv,
):
    seq, width = d_second.shape
    ffn = d_left.shape[1]
    half = taps_right.shape[2]
    side = lax.axis_index("head")
    valid = valid_rows(0, seq, lengths[0])
    rows = width // GROUPS
    for j in range(ffn // 2 // TILE):
        at = pl.multiple_of(side * (ffn // 2) + j * TILE, TILE)
        grad[j] = mm_tn(second[...], d_left[:, pl.ds(at, TILE)])
    place_rows([grad.at[j] for j in range(ffn // 2 // TILE)], keep, send, CONV_BITS, 0, rows)
    start = ffn // 2 // TILE * rows
    half_lanes = pl.ds(pl.multiple_of(side * (half // 2), half // 2), half // 2)
    for tap in range(3):
        grad_conv[tap] = mm_tn(second[...], taps_right[tap, :, half_lanes])

    def conv_slot(p, block, out):
        at = pl.multiple_of(block * rows, rows)
        middle = pl.multiple_of(block * rows + rows // 2, rows // 2)
        h = rows // 2
        out[p, start : start + rows, 0:LANES] = grad_conv[0, pl.ds(at, rows), :].astype(BF16)
        out[p, start + rows : start + rows + h, 0:LANES] = grad_conv[1, pl.ds(at, h), :].astype(BF16)
        out[p, start : start + h, LANES : 2 * LANES] = grad_conv[1, pl.ds(middle, h), :].astype(BF16)
        out[p, start + h : start + h + rows, LANES : 2 * LANES] = grad_conv[
            2, pl.ds(at, rows), :
        ].astype(BF16)

    for_slots(keep, send, CONV_BITS, conv_slot)
    for n in range(width // TILE):
        total = mm_nt(d_left[...], left_w[col(n), :])
        for tap in range(3):
            total = total + mm_nt(taps_right[tap], conv_w[tap, col(n), :])
        d_second[:, col(n)] = total * valid


def glu_back_kernel(
    d_second,
    d_after_conv,
    after_glu,
    joined,
    first,
    stream,
    small_ffn,
    small_attn,
    small_conv,
    glu_w,
    far,
    d_after_glu,
    d_first,
    keep,
    send,
    d_joined,
    rolled,
    blocks,
    grad,
):
    seq, width = d_second.shape
    side = lax.axis_index("head")
    gains = far[0]()
    gain = [gains[k : k + 1, :].astype(F32) for k in range(2)]

    def glu_rows(r, c):
        g_gain, g_shift, g_value, g_gate = c
        rows = pl.ds(r, 32)
        vhat, rate = normalized(after_glu[rows, :])
        e = d_second[rows, :]
        total = d_after_conv[rows, :] + norm_back(vhat, rate, e * gain[1])
        d_after_glu[rows, :] = total
        value = joined[rows, :width]
        gate = joined[rows, width:]
        d_value = (total * gate).astype(BF16)
        d_gate = (total * value * gate * (1.0 - gate)).astype(BF16)
        d_joined[rows, :width] = d_value
        d_joined[rows, width:] = d_gate
        return (
            g_gain + part_sums(e * vhat),
            g_shift + part_sums(e),
            g_value + part_sums(d_value.astype(F32)),
            g_gate + part_sums(d_gate.astype(F32)),
        )

    nothing = jnp.zeros((8, width), F32)
    sums = row_blocks(seq, 32, glu_rows, (nothing,) * 4, unroll=8)
    gain_one, shift_one, g_value, g_gate = (sum_tokens(v) for v in sums)
    for n in range(width // TILE):
        d_first[:, col(n)] = mm_nt(d_joined[...], glu_w[col(n), :])

    sums = [nothing] * 2
    rows = width // GROUPS
    columns = [pl.ds(pl.multiple_of(side * width + j * TILE, TILE), TILE) for j in range(width // TILE)]
    for p in range(8):
        block = slice(p * seq // 8, (p + 1) * seq // 8)
        vhat, _ = normalized(stream[block, :].astype(F32))
        e = d_first[block, :]
        sums = [total + part_sums(v) for total, v in zip(sums, (e * vhat, e))]
        if p < 2 * len(columns):
            part_rows = slice(p % 2 * (width // 2), (p % 2 + 1) * (width // 2))
            grad[p // 2, part_rows, :] = mm_tn(first[:, part_rows], d_joined[:, columns[p // 2]])
    gain_zero, shift_zero = (sum_tokens(v) for v in sums)
    place_rows([grad.at[j] for j in range(len(columns))], keep, send, GLU_BITS, 0, rows)

    blocks[...] = jnp.zeros(blocks.shape, F32)
    rolled[...] = jnp.zeros(rolled.shape, F32)
    vectors = (
        (gain_zero, gain_one, small_attn[0:1, 0:width], small_ffn[1:2, 0:width]),
        (shift_zero, shift_one, small_attn[0:1, width : 2 * width], small_ffn[1:2, width : 2 * width]),
    )
    tiles = width // LANES
    lane = lax.broadcasted_iota(jnp.int32, (8, LANES), 1)
    quarter = LANES // tiles
    for kind, four in enumerate(vectors):
        for k, vector in enumerate(four):
            for t in range(tiles):
                rolled[kind, 8 * k + t : 8 * k + t + 1, :] = vector[:, col(t, LANES)]
        for q in range(tiles):
            total = jnp.zeros((8, LANES), F32)
            for k in range(4):
                moved = pltpu.roll(rolled[kind, 8 * k : 8 * k + 8, :], (quarter * (k - q)) % LANES, 1)
                total = jnp.where((lane >= quarter * k) & (lane < quarter * (k + 1)), moved, total)
            for t in range(tiles):
                blocks[tiles * t + q, 13 + kind : 14 + kind, 0:LANES] = total[t : t + 1, :]
    lane = lane[0:1, :]
    g_out = small_ffn[1:2, 2 * width : 3 * width]
    for s in range(GROUPS):
        source = g_value if s < GROUPS // 2 else g_gate
        place = (s % (GROUPS // 2)) * (2 * width // GROUPS)
        block = source[:, place // LANES * LANES : place // LANES * LANES + LANES]
        glu_part = block if place % LANES == 0 else pltpu.roll(block, LANES - place % LANES, 1)
        place = s * (width // GROUPS)
        block = g_out[:, place // LANES * LANES : place // LANES * LANES + LANES]
        moved = (LANES // 2 - place % LANES) % LANES
        out_part = block if moved == 0 else pltpu.roll(block, moved, 1)
        blocks[s, 15:16, 0:LANES] = jnp.where(
            lane < LANES // 2, glu_part, jnp.where(lane < LANES // 2 + quarter, out_part, 0.0)
        )
        blocks[s, 0:12, 0:LANES] = small_conv[0:12, col(s, LANES)]
        blocks[s, 12:13, 0:LANES] = small_ffn[0:1, col(s, LANES)]
        for k in range(2):
            blocks[s, k : k + 1, LANES : 2 * LANES] = small_conv[12:13, col(k, LANES)]
            blocks[s, 2 + k : 3 + k, LANES : 2 * LANES] = small_attn[
                0:1, 2 * width + k * LANES : 2 * width + (k + 1) * LANES
            ]
    start = width // TILE * rows

    def small_slot(p, block, out):
        out[p, start : start + 16, :] = blocks[block].astype(BF16)

    for_slots(keep, send, GLU_BITS, small_slot)


def tokens_kernel(after_attn, hidden, ffn_out_w, d_after_glu, d_first, stream, far, out_tokens, grad_tokens):
    part, width = out_tokens.shape
    gains, ffn_out_bias = far
    at = pl.multiple_of(lax.axis_index("head") * part, part)
    own = pl.ds(at, part)
    gain, bias = gains()[0:1, :].astype(F32), vector(ffn_out_bias())
    for n in range(width // TILE):
        out_tokens[:, col(n)] = (
            after_attn[own, col(n)] + mm(hidden[own, :], ffn_out_w[:, col(n)]) + bias[:, col(n)]
        ).astype(BF16)

    def rows(r, c):
        block = pl.ds(pl.multiple_of(at + r, 32), 32)
        vhat, rate = normalized(stream[block, :].astype(F32))
        grad_tokens[pl.ds(r, 32), :] = d_after_glu[block, :] + norm_back(vhat, rate, d_first[block, :] * gain)
        return c

    row_blocks(part, 32, rows, unroll=2)


def add_kernel(keeps, gots, far, keep, send):
    at = 0
    for kept, got in zip(keeps, gots):
        rows = kept.shape[1]
        half = kept.shape[0] // 2
        count = kept.shape[0] // len(got)
        for i in range(kept.shape[0]):
            total = kept[i].astype(F32) + got[i // count][i % count].astype(F32)
            out = keep if i < half else send
            out[i % half, at : at + rows, :] = total.astype(BF16)
        at += rows


def finish_early_kernel(mine, other, far, ffn_out, ffn_in, out, qkv, point):
    side = lax.axis_index("head")
    per_row, width = ffn_out.shape
    rows = ffn_in.shape[0]
    for who, grads in ((side, mine), (1 - side, other)):
        count = ffn_in.shape[1] // 2 // TILE
        at = pl.ds(pl.multiple_of(who * TILE, TILE), TILE)
        start = per_row + count * rows
        ffn_out[:, at] = grads[0:per_row, :].astype(F32)
        out[:, at] = grads[start : start + rows, :].astype(F32)
        for j in range(count):
            at = pl.ds(pl.multiple_of((who * count + j) * TILE, TILE), TILE)
            ffn_in[:, at] = grads[per_row + j * rows : per_row + (j + 1) * rows, :].astype(F32)
        count = qkv.shape[1] // 2 // TILE
        for j in range(count):
            at = pl.ds(pl.multiple_of((who * count + j) * TILE, TILE), TILE)
            qkv[:, at] = grads[start + (1 + j) * rows : start + (2 + j) * rows, :].astype(F32)
        start = start + (1 + count) * rows
        at = pl.ds(pl.multiple_of(who * LANES, LANES), LANES)
        point[0 : per_row // 2, at] = grads[start : start + per_row // 2, 0:LANES].astype(F32)
        point[per_row // 2 :, at] = grads[start : start + per_row // 2, LANES : 2 * LANES].astype(F32)


def finish_late_kernel(
    mine,
    other,
    far,
    left,
    conv,
    glu,
    gains,
    shifts,
    depth,
    mid_gain,
    mid_bias,
    left_bias,
    ffn_in_bias,
    glu_bias,
    ffn_out_bias,
    conv_bias,
    point_bias,
):
    side = lax.axis_index("head")
    rows = glu.shape[0]
    h = rows // 2
    count = left.shape[1] // 2 // TILE
    behind = count * rows + 3 * h
    wide = glu.shape[1] // 2 // TILE
    for who, grads in ((side, mine), (1 - side, other)):
        for j in range(count):
            at = pl.ds(pl.multiple_of((who * count + j) * TILE, TILE), TILE)
            left[:, at] = grads[j * rows : (j + 1) * rows, :].astype(F32)
        start = count * rows
        at = pl.ds(pl.multiple_of(who * LANES, LANES), LANES)
        low = grads[start : start + 3 * h, 0:LANES].astype(F32)
        high = grads[start : start + 3 * h, LANES : 2 * LANES].astype(F32)
        conv[0, :, at] = low[0:rows]
        conv[1, 0:h, at] = low[rows:]
        conv[1, h:rows, at] = high[0:h]
        conv[2, :, at] = high[h:]
        for j in range(wide):
            at = pl.ds(pl.multiple_of((who * wide + j) * TILE, TILE), TILE)
            glu[:, at] = grads[behind + j * rows : behind + (j + 1) * rows, :].astype(F32)
    start = behind + wide * rows
    block = mine[start : start + 16, :].astype(F32)
    depth[...] = block[0:9, 0:LANES]
    for k in range(4):
        gains[k : k + 1, :] = block[13:14, k * rows : (k + 1) * rows]
        shifts[k : k + 1, :] = block[14:15, k * rows : (k + 1) * rows]
    mid_gain[...] = block[9, 0:LANES]
    mid_bias[...] = block[10, 0:LANES]
    left_bias[...] = block[11, 0:LANES]
    ffn_in_bias[...] = block[12, 0:LANES]
    glu_bias[...] = block[15, 0 : 2 * rows]
    ffn_out_bias[...] = block[15, 2 * rows : 3 * rows]
    for k in range(2):
        conv_bias[col(k, LANES)] = block[k, LANES : 2 * LANES]
        point_bias[col(k, LANES)] = block[2 + k, LANES : 2 * LANES]


def call(kernel, outs, scratch, near, far, micros=0, scalars=0, kept=()):
    smem = pl.BlockSpec(memory_space=pltpu.SMEM)
    vmem = pl.BlockSpec(memory_space=pltpu.VMEM)
    anywhere = pl.BlockSpec(memory_space=pltpu.HBM)

    near, inside = jax.tree.flatten(near)
    outs, outside = jax.tree.flatten(outs, is_leaf=lambda v: isinstance(v, tuple))
    own = len(outs)
    outs = outs + [(far[i].shape, far[i].dtype) for i in kept]

    def body(*refs):
        inputs = inside.unflatten(refs[: len(near)])
        sources = refs[len(near) : len(near) + len(far)]
        first = len(near) + len(far)
        results = outside.unflatten(refs[first : first + own])
        held = refs[first + own : first + len(outs)]
        rest = refs[first + len(outs) :]
        if not far:
            kernel(*inputs, (), *results, *rest)
            return
        *rest, done = rest
        fresh = iter(rest[len(scratch) :])
        buffers = [held[kept.index(i)] if i in kept else next(fresh) for i in range(len(far))]
        copies = [
            pltpu.make_async_copy(source, buffer, done.at[i])
            for i, (source, buffer) in enumerate(zip(sources, buffers))
        ]
        for copy in copies:
            copy.start()

        def fetched(copy, buffer):
            def get():
                copy.wait()
                return buffer

            return get

        kernel(*inputs, tuple(map(fetched, copies, buffers)), *results, *rest[: len(scratch)])

    temporaries = [pltpu.VMEM(shape, dtype) for shape, dtype in scratch]
    if far:
        temporaries += [pltpu.VMEM(v.shape, v.dtype) for i, v in enumerate(far) if i not in kept]
        temporaries.append(pltpu.SemaphoreType.DMA((len(far),)))
    results = pl.pallas_call(
        body,
        out_shape=tuple(jax.ShapeDtypeStruct(shape, dtype) for shape, dtype in outs),
        in_specs=[smem] * scalars + [vmem] * (len(near) - scalars) + [anywhere] * len(far),
        out_specs=(vmem,) * len(outs),
        scratch_shapes=temporaries,
        compiler_params=pltpu.CompilerParams(vmem_limit_bytes=VMEM_BYTES),
        cost_estimate=pl.CostEstimate(
            flops=micros * 10**9, transcendentals=0, bytes_accessed=micros * 3 * 10**6
        ),
        name=kernel.__name__,
    )(*near, *[pltpu.with_memory_space_constraint(v, pltpu.HBM) for v in far])
    return [*outside.unflatten(results[:own]), *results[own:]]


def per_device(
    tokens,
    lengths,
    cotangent,
    glu_weight,
    glu_bias,
    norm_gain,
    norm_bias,
    mid_gain,
    mid_bias,
    left_weight,
    left_bias,
    conv_weight,
    conv_bias,
    depth_weight,
    point_weight,
    point_bias,
    qkv_weight,
    out_weight,
    ffn_in_weight,
    ffn_in_bias,
    ffn_out_weight,
    ffn_out_bias,
):
    row_count, part, width = tokens.shape
    assert row_count == 1 and lax.axis_size("head") == 2
    seq = 2 * part
    shards = lax.axis_size("dp")
    below = shards // GROUPS
    assert below * GROUPS == shards
    heads = width // HEAD_DIM
    half = conv_weight.shape[2]
    ffn = left_weight.shape[1]
    swap = [(0, 1), (1, 0)]
    mine = tokens[0]
    cot_mine = cotangent[0]
    other = lax.ppermute(mine, "head", swap)
    cot_other = lax.ppermute(cot_mine, "head", swap)

    def slot_outs(rows, pieces=1):
        count = GROUPS // 2
        return [((count, rows, TILE), BF16), [((count // pieces, rows, TILE), BF16)] * pieces]

    rows = width // GROUPS
    per_row = ffn // GROUPS
    ffn_rows = per_row + ffn // 2 // TILE * rows
    own_first, own_joined, own_after_glu, own_second, mine, glu_w, conv_w = call(
        open_kernel,
        [
            ((part, width), BF16),
            ((part, 2 * width), F32),
            ((part, width), F32),
            ((part, width), BF16),
        ],
        [],
        [lengths],
        [mine, norm_gain, norm_bias, glu_bias, glu_weight, conv_weight],
        micros=1,
        scalars=1,
        kept=(0, 4, 5),
    )
    (
        stream,
        first_norm,
        joined,
        after_glu,
        second,
        left_pre,
        right_pre,
        depth_low,
        after_conv,
        fourth,
        packed,
        probs,
        context,
        after_attn,
        fifth,
        hidden,
        vhat,
        rates,
        left_w,
        point_w,
        qkv_w,
        out_w,
        ffn_in_w,
        ffn_out_w,
    ) = call(
        forward_kernel,
        [
            ((seq, width), BF16),
            ((seq, width), BF16),
            ((seq, 2 * width), F32),
            ((seq, width), F32),
            ((seq, width), BF16),
            ((seq, ffn), F32),
            ((seq, half), F32),
            ((seq, ffn), BF16),
            ((seq, width), F32),
            ((seq, width), BF16),
            ((seq, 3 * width), BF16),
            ((heads, seq, seq), F32),
            ((seq, width), BF16),
            ((seq, width), F32),
            ((seq, width), BF16),
            ((seq, ffn), BF16),
            ((ffn // LANES, seq, LANES), F32),
            ((seq, LANES), F32),
        ],
        [
            ((seq + 16, LANES), F32),
            ((2, seq + 16, half), F32),
            ((2, ffn), F32),
            ((seq, LANES), F32),
        ],
        [
            lengths,
            other,
            mine,
            own_first,
            own_joined,
            own_after_glu,
            own_second,
            glu_w,
            conv_w,
        ],
        [
            norm_gain,
            norm_bias,
            glu_bias,
            conv_bias,
            left_bias,
            left_weight,
            mid_gain,
            mid_bias,
            depth_weight,
            point_bias,
            point_weight,
            qkv_weight,
            out_weight,
            ffn_in_bias,
            ffn_in_weight,
            ffn_out_weight,
        ],
        micros=14,
        scalars=1,
        kept=(5, 10, 11, 12, 14, 15),
    )
    d_after, small_ffn, keep_ffn, send_ffn = call(
        ffn_back_kernel,
        [((seq, width), F32), ((8, ffn), F32)] + slot_outs(ffn_rows),
        [
            ((seq, width), BF16),
            ((seq, ffn), BF16),
            ((seq, width), F32),
            ((ffn // 2 // TILE, width, TILE), F32),
        ],
        [cot_other, after_attn, fifth, hidden, ffn_in_w, ffn_out_w],
        [cot_mine, norm_gain],
        micros=5,
    )

    class Chunk:
        def __init__(self, keep, send, bits):
            self.keep, self.send, self.bits = keep, send, list(bits)

        def start(self):
            if not self.bits:
                self.got = [lax.ppermute(self.keep, "head", swap)]
                return
            step = below << self.bits.pop(0)
            pairs = [(i, i ^ step) for i in range(shards)]
            self.got = [lax.ppermute(v, "dp", pairs) for v in self.send]

    def last_sum(keep, got):
        total = (keep[0].astype(F32) + got[0].astype(F32)).astype(BF16)
        step = 1
        while step < below:
            total = total + lax.ppermute(total, "dp", [(i, i ^ step) for i in range(shards)])
            step *= 2
        return total

    def added(*chunks, whole=False):
        keep = chunks[0].keep
        if keep.shape[0] == 1:
            return last_sum(keep, chunks[0].got[0]), None
        if len(chunks) == 1 and len(chunks[0].got) < 3 and not whole:
            (c,) = chunks
            n = keep.shape[0] // 2
            got = c.got if len(c.got) == 2 else (c.got[0][:n], c.got[0][n:])
            return tuple(
                (keep[half * n : half * n + n].astype(F32) + got[half].astype(F32)).astype(BF16)
                for half in range(2)
            )
        shape = ((keep.shape[0] // 2, sum(c.keep.shape[1] for c in chunks), TILE), BF16)
        return call(
            add_kernel, [shape, shape], [], [[c.keep for c in chunks], [c.got for c in chunks]], []
        )

    def received(held, *chunks):
        held, gots = lax.optimization_barrier((held, [c.got for c in chunks]))
        for c, got in zip(chunks, gots):
            c.got = got
        return held

    def wave(held, *chunks, joined=False, whole=True):
        held = received(held, *chunks)
        groups = [chunks] if joined else [(c,) for c in chunks]
        nexts = [Chunk(*added(*group, whole=whole), group[0].bits) for group in groups]
        held, keeps = lax.optimization_barrier((held, [(c.keep, c.send) for c in nexts]))
        for c, (keep, send) in zip(nexts, keeps):
            c.keep, c.send = keep, [send]
            c.start()
        return (held, *nexts)

    ffn_grads = Chunk(keep_ffn, send_ffn, (0, *FFN_BITS))
    ffn_grads.start()
    d_after_conv, small_attn, keep_attn, send_attn = call(
        attention_back_kernel,
        [((seq, width), F32), ((8, ffn), F32)] + slot_outs(4 * rows + per_row // 2),
        [
            ((seq, width), BF16),
            ((seq, width), BF16),
            ((seq, 3 * width), BF16),
            ((seq, width), F32),
            ((seq, half), BF16),
            ((4, width, TILE), F32),
        ],
        [d_after, packed, probs, context, fourth, after_conv, depth_low, out_w, qkv_w],
        [norm_gain],
        micros=10,
    )
    d_after_conv, ffn_grads = wave(d_after_conv, ffn_grads, whole=False)
    attn_grads = Chunk(keep_attn, send_attn, (0, *ATTN_BITS))
    attn_grads.start()
    (d_depth,) = call(
        depth_back_kernel,
        [((ffn // LANES, seq + 16, LANES), F32)],
        [],
        [d_after_conv, point_w],
        [],
    )
    (d_after_conv, d_depth), attn_grads = wave((d_after_conv, d_depth), attn_grads, whole=True)
    d_left, taps_right, small_conv = call(
        middle_back_kernel,
        [((seq, ffn), BF16), ((3, seq, half), BF16), ((16, ffn), F32)],
        [
            ((ffn // LANES, seq, LANES), F32),
            ((2, seq, LANES), F32),
            ((seq + 16, half), F32),
            ((2, ffn), F32),
            ((seq, LANES), F32),
            ((ffn // LANES, 8, LANES), F32),
        ],
        [lengths, d_depth, left_pre, right_pre, vhat, rates],
        [mid_gain, mid_bias, depth_weight],
        micros=0,
        scalars=1,
    )
    d_second, keep_conv, send_conv = call(
        conv_back_kernel,
        [((seq, width), F32)] + slot_outs(ffn // 2 // TILE * rows + 3 * rows // 2, 1),
        [((ffn // 2 // TILE, width, TILE), F32), ((3, width, LANES), F32)],
        [lengths, d_left, taps_right, second, left_w, conv_w],
        [],
        micros=0,
        scalars=1,
    )
    conv_grads = Chunk(keep_conv, send_conv, (0, *CONV_BITS))
    conv_grads.start()
    d_second, ffn_grads, attn_grads = wave(d_second, ffn_grads, attn_grads, whole=False)
    d_second, conv_grads = wave(d_second, conv_grads)
    d_after_glu, d_first, keep_glu, send_glu = call(
        glu_back_kernel,
        [((seq, width), F32)] * 2 + slot_outs(width // TILE * rows + 16, 2),
        [
            ((seq, 2 * width), BF16),
            ((2, 32, LANES), F32),
            ((GROUPS, 16, 2 * LANES), F32),
            ((width // TILE, width, TILE), F32),
        ],
        [
            d_second,
            d_after_conv,
            after_glu,
            joined,
            first_norm,
            stream,
            small_ffn,
            small_attn,
            small_conv,
            glu_w,
        ],
        [norm_gain],
        micros=7,
    )
    glu_grads = Chunk(keep_glu, send_glu, (0, *GLU_BITS))
    glu_grads.start()
    held = received(d_after_glu, ffn_grads, attn_grads)
    held, glu_grads = wave(held, glu_grads)
    held, early = wave(held, ffn_grads, attn_grads, joined=True)
    held, conv_grads = wave(held, conv_grads)
    held, glu_grads = wave(held, glu_grads)
    held, late = wave(held, conv_grads, glu_grads, joined=True)
    held, early = wave(held, early)
    out_tokens, grad_tokens = call(
        tokens_kernel,
        [((part, width), BF16), ((part, width), F32)],
        [],
        [after_attn, hidden, ffn_out_w, held, d_first, stream],
        [norm_gain, ffn_out_bias],
    )
    grad_tokens, late = wave(grad_tokens, late)
    other = early.got[0]
    ffn_out, ffn_in, out, qkv, point = call(
        finish_early_kernel,
        [
            ((per_row, width), F32),
            ((rows, ffn), F32),
            ((rows, width), F32),
            ((rows, 3 * width), F32),
            ((per_row, half), F32),
        ],
        [],
        [early.keep, other],
        [],
    )
    (
        left,
        conv,
        glu,
        g_gains,
        g_shifts,
        g_depth,
        g_mid_gain,
        g_mid_bias,
        g_left_bias,
        g_ffn_in_bias,
        g_glu_bias,
        g_ffn_out_bias,
        g_conv_bias,
        g_point_bias,
    ) = call(
        finish_late_kernel,
        [
            ((rows, ffn), F32),
            ((3, rows, half), F32),
            ((rows, 2 * width), F32),
            ((4, rows), F32),
            ((4, rows), F32),
            ((9, LANES), F32),
            ((LANES,), F32),
            ((LANES,), F32),
            ((LANES,), F32),
            ((LANES,), F32),
            ((2 * rows,), F32),
            ((rows,), F32),
            ((half,), F32),
            ((half,), F32),
        ],
        [],
        [late.keep, late.got[0]],
        [],
    )
    results = (
        (glu, 0),
        (g_glu_bias, 0),
        (g_gains, 1),
        (g_shifts, 1),
        (g_mid_gain, 0),
        (g_mid_bias, 0),
        (left, 0),
        (g_left_bias, 0),
        (conv, 1),
        (g_conv_bias, None),
        (g_depth, 1),
        (point, 0),
        (g_point_bias, None),
        (qkv, 0),
        (out, 0),
        (ffn_in, 0),
        (g_ffn_in_bias, 0),
        (ffn_out, 0),
        (g_ffn_out_bias, 0),
    )
    final = []
    for value, axis in results:
        if axis is not None and below > 1:
            size = value.shape[axis] // below
            value = lax.dynamic_slice_in_dim(value, lax.axis_index("dp") % below * size, size, axis)
        final.append(value)
    return (out_tokens[None], grad_tokens[None], *final)


def solution(mesh):
    return jax.shard_map(
        per_device,
        mesh=mesh,
        in_specs=(P("dp", "head", None), P("dp"), P("dp", "head", None)) + (P(),) * 19,
        out_specs=(
            P("dp", "head", None),
            P("dp", "head", None),
            P("dp", None),
            P("dp"),
            P(None, "dp"),
            P(None, "dp"),
            P("dp"),
            P("dp"),
            P("dp", None),
            P("dp"),
            P(None, "dp", None),
            P(),
            P(None, "dp"),
            P("dp", None),
            P(),
            P("dp", None),
            P("dp", None),
            P("dp", None),
            P("dp"),
            P("dp", None),
            P("dp"),
        ),
        check_vma=False,
    )
```

```python
import functools

import jax
import jax.numpy as jnp
from jax import lax
from jax.experimental import pallas as pl
from jax.experimental.pallas import tpu as pltpu
from jax.sharding import PartitionSpec as P

HEAD_DIM = 64
EPSILON = 1e-06
LANES = 128
TILE = 256
GROUPS = 16
F32 = jnp.float32
BF16 = jnp.bfloat16
VMEM_BYTES = 28 * 1024 * 1024
FFN_BITS = (1, 2, 3)
ATTN_BITS = (2, 1, 3)
CONV_BITS = (1, 2, 3)
GLU_BITS = (2, 1, 3)


def mm(a, b):
    return lax.dot_general(a, b, (((1,), (0,)), ((), ())), preferred_element_type=F32)


def mm_nt(a, b):
    return lax.dot_general(a, b, (((1,), (1,)), ((), ())), preferred_element_type=F32)


def mm_tn(a, b):
    return lax.dot_general(a, b, (((0,), (0,)), ((), ())), preferred_element_type=F32)


def mean(v):
    return jnp.mean(v, axis=-1, keepdims=True)


def normalized(v):
    centred = v - mean(v)
    rate = lax.rsqrt(mean(centred * centred) + EPSILON)
    return centred * rate, rate


def norm_back(vhat, rate, gained):
    return (gained - mean(gained) - vhat * mean(gained * vhat)) * rate


def sum_tokens(v):
    return jnp.sum(v, axis=0, keepdims=True)


def part_sums(v):
    return jnp.sum(v.reshape(v.shape[0] // 8, 8, v.shape[1]), axis=0)


def row_blocks(total, step, body, carry=0, unroll=1):
    def visit(i, c):
        return body(pl.multiple_of(i * step, step), c)

    return lax.fori_loop(0, total // step, visit, carry, unroll=unroll)


def valid_rows(start, count, length):
    places = start + lax.broadcasted_iota(jnp.int32, (count, 1), 0)
    return (places < length).astype(F32)


def col(n, width=TILE):
    return slice(n * width, (n + 1) * width)


def vector(ref):
    return ref[...].astype(F32).reshape(1, ref.shape[0])


def slot_block(p, sent, bits):
    group = lax.axis_index("dp") // (lax.axis_size("dp") // GROUPS)
    wanted = ((p >> 2) & 1) << bits[0] | ((p >> 1) & 1) << bits[1] | (p & 1) << bits[2]
    return group ^ (wanted | sent)


def for_slots(keep, send, bits, body, unroll=1):
    count = GROUPS // 2 // len(send)
    for i, piece in enumerate(send):

        def visit(q, c, i=i, piece=piece):
            p = i * count + q
            body(p, slot_block(p, 0, bits), keep)
            body(q, slot_block(p, 1, bits), piece)
            return c

        lax.fori_loop(0, count, visit, 0, unroll=unroll)


def place_rows(grads, keep, send, bits, at, rows):
    def one(p, block, out):
        source = pl.ds(pl.multiple_of(block * rows, rows), rows)
        for j, grad in enumerate(grads):
            out[p, at + j * rows : at + (j + 1) * rows, :] = grad[source, :].astype(BF16)

    for_slots(keep, send, bits, one)


def gated(tokens, at, place, length, gain, shift, glu_b, glu_w, first, joined, after_glu, second):
    part, width = tokens.shape

    def first_rows(r, c):
        vhat, _ = normalized(tokens[pl.ds(r, 64), :].astype(F32))
        first[pl.ds(pl.multiple_of(at + r, 64), 64), :] = (vhat * gain[0] + shift[0]).astype(BF16)
        return c

    row_blocks(part, 64, first_rows, unroll=2)
    every = pl.ds(at, part)
    for n in range(2 * width // TILE):
        joined[every, col(n)] = mm(first[every, :], glu_w[:, col(n)]) + glu_b[:, col(n)]

    def glu_rows(r, c):
        rows = pl.ds(pl.multiple_of(at + r, 32), 32)
        gate = jax.nn.sigmoid(joined[rows, width:])
        joined[rows, width:] = gate
        v = tokens[pl.ds(r, 32), :].astype(F32) + joined[rows, :width] * gate
        after_glu[rows, :] = v
        vhat, _ = normalized(v)
        valid = valid_rows(place + r, 32, length)
        second[rows, :] = ((vhat * gain[1] + shift[1]) * valid).astype(BF16)
        return c

    row_blocks(part, 32, glu_rows, unroll=4)


def open_kernel(lengths, far, first, joined, after_glu, second):
    mine, gains, shifts, glu_bias, glu_w, conv_w = far
    part = first.shape[0]
    tokens, gains, shifts = mine(), gains(), shifts()
    gain = [gains[k : k + 1, :].astype(F32) for k in range(2)]
    shift = [shifts[k : k + 1, :].astype(F32) for k in range(2)]
    place = lax.axis_index("head") * part
    glu_b, glu_w = vector(glu_bias()), glu_w()
    gated(tokens, 0, place, lengths[0], gain, shift, glu_b, glu_w, first, joined, after_glu, second)
    conv_w()


def forward_kernel(
    lengths,
    other,
    mine,
    own_first,
    own_joined,
    own_after_glu,
    own_second,
    glu_w,
    conv_w,
    far,
    stream,
    first,
    joined,
    after_glu,
    second,
    left_pre,
    right_pre,
    depth_low,
    after_conv,
    fourth,
    packed,
    probs,
    context,
    after_attn,
    fifth,
    hidden,
    vhat,
    rates,
    third,
    sides,
    mid_row,
    mask,
):
    part, width = other.shape
    seq = 2 * part
    ffn = left_pre.shape[1]
    half = right_pre.shape[1]
    side = lax.axis_index("head")
    length = lengths[0]
    own = pl.ds(pl.multiple_of(side * part, part), part)
    opposite = pl.multiple_of((1 - side) * part, part)
    (
        gains,
        shifts,
        glu_bias,
        conv_bias,
        left_bias,
        left_w,
        mid_gain,
        mid_bias,
        depth_w,
        point_bias,
        point_w,
        qkv_w,
        out_w,
        ffn_in_bias,
        ffn_in_w,
        ffn_out_w,
    ) = far
    for whole, piece in (
        (stream, mine),
        (first, own_first),
        (joined, own_joined),
        (after_glu, own_after_glu),
        (second, own_second),
    ):
        whole[own, :] = piece[...]
    stream[pl.ds(opposite, part), :] = other[...]
    gains, shifts = gains(), shifts()
    gain = [gains[k : k + 1, :].astype(F32) for k in range(4)]
    shift = [shifts[k : k + 1, :].astype(F32) for k in range(4)]
    gated(
        other, opposite, opposite, length, gain, shift, vector(glu_bias()), glu_w, first, joined, after_glu, second
    )
    blank = jnp.zeros((8, half), F32)
    for k in range(2):
        sides[k, 0:8, :] = blank
        sides[k, 8 + seq : 16 + seq, :] = blank
    sides[0, 8 : 8 + seq, :] = mm(second[...], conv_w[0])
    sides[1, 8 : 8 + seq, :] = mm(second[...], conv_w[2])
    right_pre[...] = mm(second[...], conv_w[1]) + vector(conv_bias())
    right_pre[...] = right_pre[...] + sides[0, 7 : 7 + seq, :] + sides[1, 9 : 9 + seq, :]
    left_b, left_w = vector(left_bias()), left_w()
    for n in range(ffn // TILE):
        left_pre[:, col(n)] = mm(second[...], left_w[:, col(n)]) + left_b[:, col(n)]
    mid_row[0:1, :], mid_row[1:2, :] = vector(mid_gain()), vector(mid_bias())
    depth_w = depth_w()
    chunks = ffn // LANES
    edge = jnp.zeros((8, LANES), F32)
    third[0:8, :] = edge
    third[8 + seq : 16 + seq, :] = edge
    mask[...] = (lax.broadcasted_iota(jnp.int32, (seq, LANES), 0) < length).astype(F32)

    def mid_rows(r, c):
        rows = pl.ds(r, 16)
        v, rate = normalized(combine(left_pre[rows, :], right_pre[rows, :]))
        rates[rows, :] = jnp.broadcast_to(rate, (16, LANES))
        for k in range(chunks):
            vhat[k, rows, :] = v[:, col(k, LANES)]
        return c

    row_blocks(seq, 16, mid_rows, unroll=8)

    def depth_lanes(k, c):
        lanes = pl.ds(pl.multiple_of(k * LANES, LANES), LANES)
        taps = depth_w[:, lanes].astype(F32)
        mid_gains, mid_shifts = mid_row[0:1, lanes], mid_row[1:2, lanes]
        step = 64
        for r in range(0, seq, step):
            block = slice(r, r + step)
            third[8 + r : 8 + r + step, :] = (vhat[k, block, :] * mid_gains + mid_shifts) * mask[block, :]
        for r in range(0, seq, step):
            total = third[4 + r : 4 + r + step, :] * taps[0:1, :]
            for j in range(1, 9):
                total = total + third[4 + j + r : 4 + j + r + step, :] * taps[j : j + 1, :]
            depth_low[r : r + step, lanes] = total.astype(BF16)
        return c

    lax.fori_loop(0, chunks, depth_lanes, 0, unroll=2)
    after_conv[:, :half] = (
        after_glu[:, :half] + mm(depth_low[...], point_w()[...]) + vector(point_bias())
    )
    after_conv[:, half:] = after_glu[:, half:]

    def fourth_rows(r, c):
        rows = pl.ds(r, 64)
        vhat, _ = normalized(after_conv[rows, :])
        fourth[rows, :] = (vhat * gain[2] + shift[2]).astype(BF16)
        return c

    row_blocks(seq, 64, fourth_rows, unroll=4)
    qkv_w = qkv_w()
    for n in range(3 * width // TILE):
        packed[:, col(n)] = mm(fourth[...], qkv_w[:, col(n)]).astype(BF16)

    low_lanes = lax.broadcasted_iota(jnp.int32, (1, LANES), 1) < HEAD_DIM
    scale = HEAD_DIM ** (-0.5)

    def head_pair(p, c):
        lanes = pl.ds(pl.multiple_of(p * LANES, LANES), LANES)
        q = packed[:, lanes].astype(F32) * scale
        k = packed[:, pl.ds(pl.multiple_of(width + p * LANES, LANES), LANES)]
        v = packed[:, pl.ds(pl.multiple_of(2 * width + p * LANES, LANES), LANES)]
        open_keys = lax.broadcasted_iota(jnp.int32, (seq, 1), 0) < length
        results = []
        for e in range(2):
            q_one = jnp.where(low_lanes if e == 0 else ~low_lanes, q, 0.0).astype(BF16)
            s = jnp.where(open_keys, mm_nt(k, q_one), -1000000000.0)
            raised = jnp.exp(s - jnp.max(s, axis=0, keepdims=True))
            chance = raised * (1.0 / jnp.sum(raised, axis=0, keepdims=True))
            probs[2 * p + e] = chance
            results.append(mm_tn(v, chance.astype(BF16)))
        both = jnp.concatenate([results[0][:HEAD_DIM], results[1][HEAD_DIM:]], axis=0)
        context[:, lanes] = both.T.astype(BF16)
        return c

    lax.fori_loop(0, width // LANES, head_pair, 0, unroll=4)
    out_w = out_w()
    for n in range(width // TILE):
        after_attn[:, col(n)] = after_conv[:, col(n)] + mm(context[...], out_w[:, col(n)])

    def fifth_rows(r, c):
        rows = pl.ds(r, 64)
        vhat, _ = normalized(after_attn[rows, :])
        fifth[rows, :] = (vhat * gain[3] + shift[3]).astype(BF16)
        return c

    row_blocks(seq, 64, fifth_rows, unroll=4)
    ffn_in_b, ffn_in_w = vector(ffn_in_bias()), ffn_in_w()
    for n in range(ffn // TILE):
        pre = mm(fifth[...], ffn_in_w[:, col(n)]) + ffn_in_b[:, col(n)]
        hidden[:, col(n)] = jnp.where(pre > 0.0, pre, 0.0).astype(BF16)
    ffn_out_w()


def ffn_back_kernel(
    cot_other,
    after_attn,
    fifth,
    hidden,
    ffn_in_w,
    ffn_out_w,
    far,
    d_after,
    small,
    keep,
    send,
    cot,
    d_hidden,
    d_fifth,
    grad,
):
    seq, width = fifth.shape
    part = seq // 2
    ffn = hidden.shape[1]
    side = lax.axis_index("head")
    cot_mine, gains = far
    own = pl.ds(pl.multiple_of(side * part, part), part)
    opposite = pl.ds(pl.multiple_of((1 - side) * part, part), part)
    cot[opposite, :] = cot_other[...]
    cot[own, :] = cot_mine()[...]
    for n in range(ffn // TILE):
        back = mm_nt(cot[...], ffn_out_w[col(n), :])
        back = jnp.where(hidden[:, col(n)].astype(F32) > 0.0, back, 0.0).astype(BF16)
        d_hidden[:, col(n)] = back
        small[0:1, col(n)] = sum_tokens(back.astype(F32))
    for n in range(width // TILE):
        d_fifth[:, col(n)] = mm_nt(d_hidden[...], ffn_in_w[col(n), :])

    cot_half = cot[:, pl.ds(pl.multiple_of(side * (width // 2), width // 2), width // 2)]
    per_row = ffn // GROUPS
    gain = gains()[3:4, :].astype(F32)
    sums = [jnp.zeros((8, width), F32)] * 3
    for p in range(GROUPS // 2):
        block = slice(p * seq // 8, (p + 1) * seq // 8)
        vhat, rate = normalized(after_attn[block, :])
        e = d_fifth[block, :]
        given = cot[block, :].astype(F32)
        d_after[block, :] = given + norm_back(vhat, rate, e * gain)
        sums = [total + part_sums(v) for total, v in zip(sums, (e * vhat, e, given))]
        count = GROUPS // 2 // len(send)
        for sent, out, place in ((0, keep, p), (1, send[p // count], p % count)):
            at = pl.multiple_of(slot_block(p, sent, FFN_BITS) * per_row, per_row)
            out[place, 0:per_row, :] = mm_tn(hidden[:, pl.ds(at, per_row)], cot_half).astype(BF16)
    for k in range(3):
        small[1:2, k * width : (k + 1) * width] = sum_tokens(sums[k])

    rows = width // GROUPS
    for j in range(ffn // 2 // TILE):
        at = pl.multiple_of(side * (ffn // 2) + j * TILE, TILE)
        grad[j] = mm_tn(fifth[...], d_hidden[:, pl.ds(at, TILE)])
    count = ffn // 2 // TILE
    place_rows([grad.at[j] for j in range(count)], keep, send, FFN_BITS, per_row, rows)


def combine(left_pre, right_pre):
    half = right_pre.shape[1]
    left = jnp.maximum(left_pre, 0.0)
    return jnp.concatenate([left[:, :half] + jnp.maximum(right_pre, 0.0), left[:, half:]], axis=1)


def attention_back_kernel(
    d_after,
    packed,
    probs,
    context,
    fourth,
    after_conv,
    depth_low,
    out_w,
    qkv_w,
    far,
    d_after_conv,
    small,
    keep,
    send,
    d_attn,
    d_context,
    d_packed,
    d_fourth,
    d_sep,
    grad,
):
    seq, width = d_after.shape
    side = lax.axis_index("head")
    (gains,) = far
    half = d_sep.shape[1]
    ffn = depth_low.shape[1]
    rows = width // GROUPS
    d_attn[...] = d_after[...].astype(BF16)
    for n in range(width // TILE):
        d_context[:, col(n)] = mm_nt(d_attn[...], out_w[col(n), :]).astype(BF16)
    low_lanes = lax.broadcasted_iota(jnp.int32, (1, LANES), 1) < HEAD_DIM
    scale = HEAD_DIM ** (-0.5)

    def head_pair(p, c):
        lanes = pl.ds(pl.multiple_of(p * LANES, LANES), LANES)
        k_lanes = pl.ds(pl.multiple_of(width + p * LANES, LANES), LANES)
        v_lanes = pl.ds(pl.multiple_of(2 * width + p * LANES, LANES), LANES)
        q = packed[:, lanes]
        k = packed[:, k_lanes]
        v = packed[:, v_lanes].astype(F32)
        given = d_context[:, lanes]
        dq, dk, dv = [], [], []
        for e in range(2):
            one = jnp.where(low_lanes if e == 0 else ~low_lanes, v, 0.0).astype(BF16)
            chance = probs[2 * p + e]
            d_probs = mm_nt(one, given)
            delta = jnp.sum(d_probs * chance, axis=0, keepdims=True)
            d_scores = (chance * (d_probs - delta)).astype(BF16)
            dv.append(mm(chance.astype(BF16), given))
            dk.append(mm(d_scores, q))
            dq.append(mm_tn(k, d_scores))
        both = jnp.concatenate([dq[0][:HEAD_DIM], dq[1][HEAD_DIM:]], axis=0)
        d_packed[:, lanes] = (both.T * scale).astype(BF16)
        d_packed[:, k_lanes] = (jnp.where(low_lanes, dk[0], dk[1]) * scale).astype(BF16)
        d_packed[:, v_lanes] = jnp.where(low_lanes, dv[0], dv[1]).astype(BF16)
        return c

    lax.fori_loop(0, width // LANES, head_pair, 0, unroll=4)
    for n in range(width // TILE):
        d_fourth[:, col(n)] = mm_nt(d_packed[...], qkv_w[col(n), :])
    gain = gains()[2:3, :].astype(F32)

    sums = [jnp.zeros((8, width), F32)] * 2
    g_point = jnp.zeros((8, half), F32)
    at = pl.multiple_of(side * (width // 2), width // 2)
    sides = [(context, d_attn, at)]
    for j in range(3 * width // 2 // TILE):
        sides.append((fourth, d_packed, pl.multiple_of(side * (3 * width // 2) + j * TILE, TILE)))
    for p in range(2 * len(sides)):
        block = slice(p * seq // 8, (p + 1) * seq // 8)
        vhat, rate = normalized(after_conv[block, :])
        e = d_fourth[block, :]
        total = d_after[block, :] + norm_back(vhat, rate, e * gain)
        d_after_conv[block, :] = total
        sep = total[:, :half].astype(BF16)
        d_sep[block, :] = sep
        sums = [total + part_sums(v) for total, v in zip(sums, (e * vhat, e))]
        g_point = g_point + part_sums(sep.astype(F32))
        values, incoming, at = sides[p // 2]
        part = slice(p % 2 * (width // 2), (p % 2 + 1) * (width // 2))
        grad[p // 2, part, :] = mm_tn(values[:, part], incoming[:, pl.ds(at, TILE)])
    small[0:1, 0:width] = sum_tokens(sums[0])
    small[0:1, width : 2 * width] = sum_tokens(sums[1])
    small[0:1, 2 * width : 2 * width + half] = sum_tokens(g_point)
    place_rows([grad.at[j] for j in range(len(sides))], keep, send, ATTN_BITS, 0, rows)
    sep_half = d_sep[:, pl.ds(pl.multiple_of(side * (half // 2), half // 2), half // 2)]
    per_row = ffn // GROUPS

    def point_slot(p, block, out):
        g = mm_tn(
            depth_low[:, pl.ds(pl.multiple_of(block * per_row, per_row), per_row)], sep_half
        ).astype(BF16)
        out[p, 4 * rows : 4 * rows + per_row // 2, 0:LANES] = g[: per_row // 2]
        out[p, 4 * rows : 4 * rows + per_row // 2, LANES : 2 * LANES] = g[per_row // 2 :]

    for_slots(keep, send, ATTN_BITS, point_slot, unroll=8)


def middle_back_kernel(
    lengths,
    d_after_conv,
    left_pre,
    right_pre,
    vhat3,
    rates,
    point_w,
    far,
    d_left,
    taps_right,
    small,
    d_depth,
    d_third,
    sums,
    d_right,
    mid_row,
    mask,
    left_sums,
):
    seq, width = d_after_conv.shape
    ffn = left_pre.shape[1]
    half = right_pre.shape[1]
    length = lengths[0]
    mid_gain, mid_bias, depth_w = far
    chunks = ffn // LANES
    edge = jnp.zeros((8, LANES), F32)
    for k in range(chunks):
        d_depth[k, 0:8, :] = edge
        d_depth[k, 8 + seq : 16 + seq, :] = edge
    d_sep = d_after_conv[:, :half].astype(BF16)
    for n in range(ffn // TILE):
        block = mm_nt(d_sep, point_w[col(n), :])
        for m in range(TILE // LANES):
            d_depth[n * (TILE // LANES) + m, 8 : 8 + seq, :] = block[:, col(m, LANES)]

    mid_row[0:1, :], mid_row[1:2, :] = vector(mid_gain()), vector(mid_bias())
    depth_w = depth_w()
    mask[...] = (lax.broadcasted_iota(jnp.int32, (seq, LANES), 0) < length).astype(F32)
    sums[...] = jnp.zeros(sums.shape, F32)
    step = 64

    def depth_lanes(k, c):
        lanes = pl.ds(pl.multiple_of(k * LANES, LANES), LANES)
        taps = depth_w[:, lanes].astype(F32)
        mid_lanes, low_lanes = mid_row[0:1, lanes], mid_row[1:2, lanes]
        totals = [jnp.zeros((8, LANES), F32)] * 11
        for r in range(0, seq, step):
            block = slice(r, r + step)
            vhat = vhat3[k, block, :]
            here = (vhat * mid_lanes + low_lanes) * mask[block, :]
            total = None
            for j in range(9):
                moved = d_depth[k, 12 - j + r : 12 - j + r + step, :]
                totals[j] = totals[j] + part_sums(moved * here)
                term = moved * taps[j : j + 1, :]
                total = term if total is None else total + term
            total = total * mask[block, :]
            totals[9] = totals[9] + part_sums(total * vhat)
            totals[10] = totals[10] + part_sums(total)
            gained = total * mid_lanes
            d_third[k, block, :] = gained
            sums[0, block, :] = sums[0, block, :] + gained
            sums[1, block, :] = sums[1, block, :] + gained * vhat
        for j in range(11):
            small[j : j + 1, lanes] = sum_tokens(totals[j])
        return c

    lax.fori_loop(0, chunks, depth_lanes, 0, unroll=2)
    inverse = 1.0 / ffn
    sums[0] = jnp.broadcast_to(jnp.sum(sums[0], axis=-1, keepdims=True) * inverse, (seq, LANES))
    sums[1] = jnp.broadcast_to(jnp.sum(sums[1], axis=-1, keepdims=True) * inverse, (seq, LANES))

    def combined_lanes(k):
        return (d_third[k] - sums[0] - vhat3[k] * sums[1]) * rates[...]

    left_sums[...] = jnp.zeros(left_sums.shape, F32)
    for r in range(0, seq, step):
        block = slice(r, r + step)
        first, second, rate = sums[0, block, :], sums[1, block, :], rates[block, :]

        def left_lanes(k, c, block=block, first=first, second=second, rate=rate):
            lanes = pl.ds(pl.multiple_of(k * LANES, LANES), LANES)
            v = (d_third[k, block, :] - first - vhat3[k, block, :] * second) * rate
            v = jnp.where(left_pre[block, lanes] > 0.0, v, 0.0).astype(BF16)
            d_left[block, lanes] = v
            left_sums[k] = left_sums[k] + part_sums(v.astype(F32))
            return c

        lax.fori_loop(0, chunks, left_lanes, 0, unroll=2)
    for k in range(chunks):
        small[11:12, col(k, LANES)] = sum_tokens(left_sums[k])
    blank = jnp.zeros((8, half), F32)
    d_right[0:8, :] = blank
    d_right[8 + seq : 16 + seq, :] = blank
    for k in range(half // LANES):
        v = jnp.where(right_pre[:, col(k, LANES)] > 0.0, combined_lanes(k), 0.0).astype(BF16)
        v = v.astype(F32)
        d_right[8 : 8 + seq, col(k, LANES)] = v
        small[12:13, col(k, LANES)] = sum_tokens(v)
    taps_right[0] = d_right[9 : 9 + seq, :].astype(BF16)
    taps_right[1] = d_right[8 : 8 + seq, :].astype(BF16)
    taps_right[2] = d_right[7 : 7 + seq, :].astype(BF16)


def conv_back_kernel(
    lengths,
    d_left,
    taps_right,
    second,
    left_w,
    conv_w,
    far,
    d_second,
    keep,
    send,
    grad,
    grad_conv,
):
    seq, width = d_second.shape
    ffn = d_left.shape[1]
    half = taps_right.shape[2]
    side = lax.axis_index("head")
    valid = valid_rows(0, seq, lengths[0])
    rows = width // GROUPS
    for j in range(ffn // 2 // TILE):
        at = pl.multiple_of(side * (ffn // 2) + j * TILE, TILE)
        grad[j] = mm_tn(second[...], d_left[:, pl.ds(at, TILE)])
    place_rows([grad.at[j] for j in range(ffn // 2 // TILE)], keep, send, CONV_BITS, 0, rows)
    start = ffn // 2 // TILE * rows
    half_lanes = pl.ds(pl.multiple_of(side * (half // 2), half // 2), half // 2)
    for tap in range(3):
        grad_conv[tap] = mm_tn(second[...], taps_right[tap, :, half_lanes])

    def conv_slot(p, block, out):
        at = pl.multiple_of(block * rows, rows)
        middle = pl.multiple_of(block * rows + rows // 2, rows // 2)
        h = rows // 2
        out[p, start : start + rows, 0:LANES] = grad_conv[0, pl.ds(at, rows), :].astype(BF16)
        out[p, start + rows : start + rows + h, 0:LANES] = grad_conv[1, pl.ds(at, h), :].astype(BF16)
        out[p, start : start + h, LANES : 2 * LANES] = grad_conv[1, pl.ds(middle, h), :].astype(BF16)
        out[p, start + h : start + h + rows, LANES : 2 * LANES] = grad_conv[
            2, pl.ds(at, rows), :
        ].astype(BF16)

    for_slots(keep, send, CONV_BITS, conv_slot)
    for n in range(width // TILE):
        total = mm_nt(d_left[...], left_w[col(n), :])
        for tap in range(3):
            total = total + mm_nt(taps_right[tap], conv_w[tap, col(n), :])
        d_second[:, col(n)] = total * valid


def glu_back_kernel(
    d_second,
    d_after_conv,
    after_glu,
    joined,
    first,
    stream,
    small_ffn,
    small_attn,
    small_conv,
    glu_w,
    far,
    d_after_glu,
    d_first,
    keep,
    send,
    d_joined,
    rolled,
    blocks,
    grad,
):
    seq, width = d_second.shape
    side = lax.axis_index("head")
    gains = far[0]()
    gain = [gains[k : k + 1, :].astype(F32) for k in range(2)]

    def glu_rows(r, c):
        g_gain, g_shift, g_value, g_gate = c
        rows = pl.ds(r, 32)
        vhat, rate = normalized(after_glu[rows, :])
        e = d_second[rows, :]
        total = d_after_conv[rows, :] + norm_back(vhat, rate, e * gain[1])
        d_after_glu[rows, :] = total
        value = joined[rows, :width]
        gate = joined[rows, width:]
        d_value = (total * gate).astype(BF16)
        d_gate = (total * value * gate * (1.0 - gate)).astype(BF16)
        d_joined[rows, :width] = d_value
        d_joined[rows, width:] = d_gate
        return (
            g_gain + part_sums(e * vhat),
            g_shift + part_sums(e),
            g_value + part_sums(d_value.astype(F32)),
            g_gate + part_sums(d_gate.astype(F32)),
        )

    nothing = jnp.zeros((8, width), F32)
    sums = row_blocks(seq, 32, glu_rows, (nothing,) * 4, unroll=8)
    gain_one, shift_one, g_value, g_gate = (sum_tokens(v) for v in sums)
    for n in range(width // TILE):
        d_first[:, col(n)] = mm_nt(d_joined[...], glu_w[col(n), :])

    sums = [nothing] * 2
    rows = width // GROUPS
    columns = [pl.ds(pl.multiple_of(side * width + j * TILE, TILE), TILE) for j in range(width // TILE)]
    for p in range(8):
        block = slice(p * seq // 8, (p + 1) * seq // 8)
        vhat, _ = normalized(stream[block, :].astype(F32))
        e = d_first[block, :]
        sums = [total + part_sums(v) for total, v in zip(sums, (e * vhat, e))]
        if p < 2 * len(columns):
            part_rows = slice(p % 2 * (width // 2), (p % 2 + 1) * (width // 2))
            grad[p // 2, part_rows, :] = mm_tn(first[:, part_rows], d_joined[:, columns[p // 2]])
    gain_zero, shift_zero = (sum_tokens(v) for v in sums)
    place_rows([grad.at[j] for j in range(len(columns))], keep, send, GLU_BITS, 0, rows)

    blocks[...] = jnp.zeros(blocks.shape, F32)
    rolled[...] = jnp.zeros(rolled.shape, F32)
    vectors = (
        (gain_zero, gain_one, small_attn[0:1, 0:width], small_ffn[1:2, 0:width]),
        (shift_zero, shift_one, small_attn[0:1, width : 2 * width], small_ffn[1:2, width : 2 * width]),
    )
    tiles = width // LANES
    lane = lax.broadcasted_iota(jnp.int32, (8, LANES), 1)
    quarter = LANES // tiles
    for kind, four in enumerate(vectors):
        for k, vector in enumerate(four):
            for t in range(tiles):
                rolled[kind, 8 * k + t : 8 * k + t + 1, :] = vector[:, col(t, LANES)]
        for q in range(tiles):
            total = jnp.zeros((8, LANES), F32)
            for k in range(4):
                moved = pltpu.roll(rolled[kind, 8 * k : 8 * k + 8, :], (quarter * (k - q)) % LANES, 1)
                total = jnp.where((lane >= quarter * k) & (lane < quarter * (k + 1)), moved, total)
            for t in range(tiles):
                blocks[tiles * t + q, 13 + kind : 14 + kind, 0:LANES] = total[t : t + 1, :]
    lane = lane[0:1, :]
    g_out = small_ffn[1:2, 2 * width : 3 * width]
    for s in range(GROUPS):
        source = g_value if s < GROUPS // 2 else g_gate
        place = (s % (GROUPS // 2)) * (2 * width // GROUPS)
        block = source[:, place // LANES * LANES : place // LANES * LANES + LANES]
        glu_part = block if place % LANES == 0 else pltpu.roll(block, LANES - place % LANES, 1)
        place = s * (width // GROUPS)
        block = g_out[:, place // LANES * LANES : place // LANES * LANES + LANES]
        moved = (LANES // 2 - place % LANES) % LANES
        out_part = block if moved == 0 else pltpu.roll(block, moved, 1)
        blocks[s, 15:16, 0:LANES] = jnp.where(
            lane < LANES // 2, glu_part, jnp.where(lane < LANES // 2 + quarter, out_part, 0.0)
        )
        blocks[s, 0:12, 0:LANES] = small_conv[0:12, col(s, LANES)]
        blocks[s, 12:13, 0:LANES] = small_ffn[0:1, col(s, LANES)]
        for k in range(2):
            blocks[s, k : k + 1, LANES : 2 * LANES] = small_conv[12:13, col(k, LANES)]
            blocks[s, 2 + k : 3 + k, LANES : 2 * LANES] = small_attn[
                0:1, 2 * width + k * LANES : 2 * width + (k + 1) * LANES
            ]
    start = width // TILE * rows

    def small_slot(p, block, out):
        out[p, start : start + 16, :] = blocks[block].astype(BF16)

    for_slots(keep, send, GLU_BITS, small_slot)


def tokens_kernel(after_attn, hidden, ffn_out_w, d_after_glu, d_first, stream, far, out_tokens, grad_tokens):
    part, width = out_tokens.shape
    gains, ffn_out_bias = far
    at = pl.multiple_of(lax.axis_index("head") * part, part)
    own = pl.ds(at, part)
    gain, bias = gains()[0:1, :].astype(F32), vector(ffn_out_bias())
    for n in range(width // TILE):
        out_tokens[:, col(n)] = (
            after_attn[own, col(n)] + mm(hidden[own, :], ffn_out_w[:, col(n)]) + bias[:, col(n)]
        ).astype(BF16)

    def rows(r, c):
        block = pl.ds(pl.multiple_of(at + r, 32), 32)
        vhat, rate = normalized(stream[block, :].astype(F32))
        grad_tokens[pl.ds(r, 32), :] = d_after_glu[block, :] + norm_back(vhat, rate, d_first[block, :] * gain)
        return c

    row_blocks(part, 32, rows, unroll=2)


def add_kernel(keeps, gots, far, keep, send):
    at = 0
    for kept, got in zip(keeps, gots):
        rows = kept.shape[1]
        half = kept.shape[0] // 2
        count = kept.shape[0] // len(got)
        for i in range(kept.shape[0]):
            total = kept[i].astype(F32) + got[i // count][i % count].astype(F32)
            out = keep if i < half else send
            out[i % half, at : at + rows, :] = total.astype(BF16)
        at += rows


def finish_early_kernel(mine, other, far, ffn_out, ffn_in, out, qkv, point):
    side = lax.axis_index("head")
    per_row, width = ffn_out.shape
    rows = ffn_in.shape[0]
    for who, grads in ((side, mine), (1 - side, other)):
        count = ffn_in.shape[1] // 2 // TILE
        at = pl.ds(pl.multiple_of(who * TILE, TILE), TILE)
        start = per_row + count * rows
        ffn_out[:, at] = grads[0:per_row, :].astype(F32)
        out[:, at] = grads[start : start + rows, :].astype(F32)
        for j in range(count):
            at = pl.ds(pl.multiple_of((who * count + j) * TILE, TILE), TILE)
            ffn_in[:, at] = grads[per_row + j * rows : per_row + (j + 1) * rows, :].astype(F32)
        count = qkv.shape[1] // 2 // TILE
        for j in range(count):
            at = pl.ds(pl.multiple_of((who * count + j) * TILE, TILE), TILE)
            qkv[:, at] = grads[start + (1 + j) * rows : start + (2 + j) * rows, :].astype(F32)
        start = start + (1 + count) * rows
        at = pl.ds(pl.multiple_of(who * LANES, LANES), LANES)
        point[0 : per_row // 2, at] = grads[start : start + per_row // 2, 0:LANES].astype(F32)
        point[per_row // 2 :, at] = grads[start : start + per_row // 2, LANES : 2 * LANES].astype(F32)


def finish_late_kernel(
    mine,
    other,
    far,
    left,
    conv,
    glu,
    gains,
    shifts,
    depth,
    mid_gain,
    mid_bias,
    left_bias,
    ffn_in_bias,
    glu_bias,
    ffn_out_bias,
    conv_bias,
    point_bias,
):
    side = lax.axis_index("head")
    rows = glu.shape[0]
    h = rows // 2
    count = left.shape[1] // 2 // TILE
    behind = count * rows + 3 * h
    wide = glu.shape[1] // 2 // TILE
    for who, grads in ((side, mine), (1 - side, other)):
        for j in range(count):
            at = pl.ds(pl.multiple_of((who * count + j) * TILE, TILE), TILE)
            left[:, at] = grads[j * rows : (j + 1) * rows, :].astype(F32)
        start = count * rows
        at = pl.ds(pl.multiple_of(who * LANES, LANES), LANES)
        low = grads[start : start + 3 * h, 0:LANES].astype(F32)
        high = grads[start : start + 3 * h, LANES : 2 * LANES].astype(F32)
        conv[0, :, at] = low[0:rows]
        conv[1, 0:h, at] = low[rows:]
        conv[1, h:rows, at] = high[0:h]
        conv[2, :, at] = high[h:]
        for j in range(wide):
            at = pl.ds(pl.multiple_of((who * wide + j) * TILE, TILE), TILE)
            glu[:, at] = grads[behind + j * rows : behind + (j + 1) * rows, :].astype(F32)
    start = behind + wide * rows
    block = mine[start : start + 16, :].astype(F32)
    depth[...] = block[0:9, 0:LANES]
    for k in range(4):
        gains[k : k + 1, :] = block[13:14, k * rows : (k + 1) * rows]
        shifts[k : k + 1, :] = block[14:15, k * rows : (k + 1) * rows]
    mid_gain[...] = block[9, 0:LANES]
    mid_bias[...] = block[10, 0:LANES]
    left_bias[...] = block[11, 0:LANES]
    ffn_in_bias[...] = block[12, 0:LANES]
    glu_bias[...] = block[15, 0 : 2 * rows]
    ffn_out_bias[...] = block[15, 2 * rows : 3 * rows]
    for k in range(2):
        conv_bias[col(k, LANES)] = block[k, LANES : 2 * LANES]
        point_bias[col(k, LANES)] = block[2 + k, LANES : 2 * LANES]


def call(kernel, outs, scratch, near, far, micros=0, scalars=0, kept=()):
    smem = pl.BlockSpec(memory_space=pltpu.SMEM)
    vmem = pl.BlockSpec(memory_space=pltpu.VMEM)
    anywhere = pl.BlockSpec(memory_space=pltpu.HBM)

    near, inside = jax.tree.flatten(near)
    outs, outside = jax.tree.flatten(outs, is_leaf=lambda v: isinstance(v, tuple))
    own = len(outs)
    outs = outs + [(far[i].shape, far[i].dtype) for i in kept]

    def body(*refs):
        inputs = inside.unflatten(refs[: len(near)])
        sources = refs[len(near) : len(near) + len(far)]
        first = len(near) + len(far)
        results = outside.unflatten(refs[first : first + own])
        held = refs[first + own : first + len(outs)]
        rest = refs[first + len(outs) :]
        if not far:
            kernel(*inputs, (), *results, *rest)
            return
        *rest, done = rest
        fresh = iter(rest[len(scratch) :])
        buffers = [held[kept.index(i)] if i in kept else next(fresh) for i in range(len(far))]
        copies = [
            pltpu.make_async_copy(source, buffer, done.at[i])
            for i, (source, buffer) in enumerate(zip(sources, buffers))
        ]
        for copy in copies:
            copy.start()

        def fetched(copy, buffer):
            def get():
                copy.wait()
                return buffer

            return get

        kernel(*inputs, tuple(map(fetched, copies, buffers)), *results, *rest[: len(scratch)])

    temporaries = [pltpu.VMEM(shape, dtype) for shape, dtype in scratch]
    if far:
        temporaries += [pltpu.VMEM(v.shape, v.dtype) for i, v in enumerate(far) if i not in kept]
        temporaries.append(pltpu.SemaphoreType.DMA((len(far),)))
    results = pl.pallas_call(
        body,
        out_shape=tuple(jax.ShapeDtypeStruct(shape, dtype) for shape, dtype in outs),
        in_specs=[smem] * scalars + [vmem] * (len(near) - scalars) + [anywhere] * len(far),
        out_specs=(vmem,) * len(outs),
        scratch_shapes=temporaries,
        compiler_params=pltpu.CompilerParams(vmem_limit_bytes=VMEM_BYTES),
        cost_estimate=pl.CostEstimate(
            flops=micros * 10**9, transcendentals=0, bytes_accessed=micros * 3 * 10**6
        ),
        name=kernel.__name__,
    )(*near, *[pltpu.with_memory_space_constraint(v, pltpu.HBM) for v in far])
    return [*outside.unflatten(results[:own]), *results[own:]]


def per_device(
    tokens,
    lengths,
    cotangent,
    glu_weight,
    glu_bias,
    norm_gain,
    norm_bias,
    mid_gain,
    mid_bias,
    left_weight,
    left_bias,
    conv_weight,
    conv_bias,
    depth_weight,
    point_weight,
    point_bias,
    qkv_weight,
    out_weight,
    ffn_in_weight,
    ffn_in_bias,
    ffn_out_weight,
    ffn_out_bias,
):
    row_count, part, width = tokens.shape
    assert row_count == 1 and lax.axis_size("head") == 2
    seq = 2 * part
    shards = lax.axis_size("dp")
    below = shards // GROUPS
    assert below * GROUPS == shards
    heads = width // HEAD_DIM
    half = conv_weight.shape[2]
    ffn = left_weight.shape[1]
    swap = [(0, 1), (1, 0)]
    mine = tokens[0]
    cot_mine = cotangent[0]
    other = lax.ppermute(mine, "head", swap)
    cot_other = lax.ppermute(cot_mine, "head", swap)

    def slot_outs(rows, pieces=1):
        count = GROUPS // 2
        return [((count, rows, TILE), BF16), [((count // pieces, rows, TILE), BF16)] * pieces]

    rows = width // GROUPS
    per_row = ffn // GROUPS
    ffn_rows = per_row + ffn // 2 // TILE * rows
    own_first, own_joined, own_after_glu, own_second, mine, glu_w, conv_w = call(
        open_kernel,
        [
            ((part, width), BF16),
            ((part, 2 * width), F32),
            ((part, width), F32),
            ((part, width), BF16),
        ],
        [],
        [lengths],
        [mine, norm_gain, norm_bias, glu_bias, glu_weight, conv_weight],
        micros=1,
        scalars=1,
        kept=(0, 4, 5),
    )
    (
        stream,
        first_norm,
        joined,
        after_glu,
        second,
        left_pre,
        right_pre,
        depth_low,
        after_conv,
        fourth,
        packed,
        probs,
        context,
        after_attn,
        fifth,
        hidden,
        vhat,
        rates,
        left_w,
        point_w,
        qkv_w,
        out_w,
        ffn_in_w,
        ffn_out_w,
    ) = call(
        forward_kernel,
        [
            ((seq, width), BF16),
            ((seq, width), BF16),
            ((seq, 2 * width), F32),
            ((seq, width), F32),
            ((seq, width), BF16),
            ((seq, ffn), F32),
            ((seq, half), F32),
            ((seq, ffn), BF16),
            ((seq, width), F32),
            ((seq, width), BF16),
            ((seq, 3 * width), BF16),
            ((heads, seq, seq), F32),
            ((seq, width), BF16),
            ((seq, width), F32),
            ((seq, width), BF16),
            ((seq, ffn), BF16),
            ((ffn // LANES, seq, LANES), F32),
            ((seq, LANES), F32),
        ],
        [
            ((seq + 16, LANES), F32),
            ((2, seq + 16, half), F32),
            ((2, ffn), F32),
            ((seq, LANES), F32),
        ],
        [
            lengths,
            other,
            mine,
            own_first,
            own_joined,
            own_after_glu,
            own_second,
            glu_w,
            conv_w,
        ],
        [
            norm_gain,
            norm_bias,
            glu_bias,
            conv_bias,
            left_bias,
            left_weight,
            mid_gain,
            mid_bias,
            depth_weight,
            point_bias,
            point_weight,
            qkv_weight,
            out_weight,
            ffn_in_bias,
            ffn_in_weight,
            ffn_out_weight,
        ],
        micros=14,
        scalars=1,
        kept=(5, 10, 11, 12, 14, 15),
    )
    d_after, small_ffn, keep_ffn, send_ffn = call(
        ffn_back_kernel,
        [((seq, width), F32), ((8, ffn), F32)] + slot_outs(ffn_rows),
        [
            ((seq, width), BF16),
            ((seq, ffn), BF16),
            ((seq, width), F32),
            ((ffn // 2 // TILE, width, TILE), F32),
        ],
        [cot_other, after_attn, fifth, hidden, ffn_in_w, ffn_out_w],
        [cot_mine, norm_gain],
        micros=5,
    )

    class Chunk:
        def __init__(self, keep, send, bits):
            self.keep, self.send, self.bits = keep, send, list(bits)

        def start(self):
            if not self.bits:
                self.got = [lax.ppermute(self.keep, "head", swap)]
                return
            step = below << self.bits.pop(0)
            pairs = [(i, i ^ step) for i in range(shards)]
            self.got = [lax.ppermute(v, "dp", pairs) for v in self.send]

    def last_sum(keep, got):
        total = (keep[0].astype(F32) + got[0].astype(F32)).astype(BF16)
        step = 1
        while step < below:
            total = total + lax.ppermute(total, "dp", [(i, i ^ step) for i in range(shards)])
            step *= 2
        return total

    def added(*chunks, whole=False):
        keep = chunks[0].keep
        if keep.shape[0] == 1:
            return last_sum(keep, chunks[0].got[0]), None
        if len(chunks) == 1 and len(chunks[0].got) < 3 and not whole:
            (c,) = chunks
            n = keep.shape[0] // 2
            got = c.got if len(c.got) == 2 else (c.got[0][:n], c.got[0][n:])
            return tuple(
                (keep[half * n : half * n + n].astype(F32) + got[half].astype(F32)).astype(BF16)
                for half in range(2)
            )
        shape = ((keep.shape[0] // 2, sum(c.keep.shape[1] for c in chunks), TILE), BF16)
        return call(
            add_kernel, [shape, shape], [], [[c.keep for c in chunks], [c.got for c in chunks]], []
        )

    def received(held, *chunks):
        held, gots = lax.optimization_barrier((held, [c.got for c in chunks]))
        for c, got in zip(chunks, gots):
            c.got = got
        return held

    def wave(held, *chunks, joined=False, whole=True):
        held = received(held, *chunks)
        groups = [chunks] if joined else [(c,) for c in chunks]
        nexts = [Chunk(*added(*group, whole=whole), group[0].bits) for group in groups]
        held, keeps = lax.optimization_barrier((held, [(c.keep, c.send) for c in nexts]))
        for c, (keep, send) in zip(nexts, keeps):
            c.keep, c.send = keep, [send]
            c.start()
        return (held, *nexts)

    ffn_grads = Chunk(keep_ffn, send_ffn, (0, *FFN_BITS))
    ffn_grads.start()
    d_after_conv, small_attn, keep_attn, send_attn = call(
        attention_back_kernel,
        [((seq, width), F32), ((8, ffn), F32)] + slot_outs(4 * rows + per_row // 2),
        [
            ((seq, width), BF16),
            ((seq, width), BF16),
            ((seq, 3 * width), BF16),
            ((seq, width), F32),
            ((seq, half), BF16),
            ((4, width, TILE), F32),
        ],
        [d_after, packed, probs, context, fourth, after_conv, depth_low, out_w, qkv_w],
        [norm_gain],
        micros=10,
    )
    d_after_conv, ffn_grads = wave(d_after_conv, ffn_grads, whole=False)
    attn_grads = Chunk(keep_attn, send_attn, (0, *ATTN_BITS))
    attn_grads.start()
    d_after_conv, attn_grads = wave(d_after_conv, attn_grads, whole=True)
    d_left, taps_right, small_conv = call(
        middle_back_kernel,
        [((seq, ffn), BF16), ((3, seq, half), BF16), ((16, ffn), F32)],
        [
            ((ffn // LANES, seq + 16, LANES), F32),
            ((ffn // LANES, seq, LANES), F32),
            ((2, seq, LANES), F32),
            ((seq + 16, half), F32),
            ((2, ffn), F32),
            ((seq, LANES), F32),
            ((ffn // LANES, 8, LANES), F32),
        ],
        [lengths, d_after_conv, left_pre, right_pre, vhat, rates, point_w],
        [mid_gain, mid_bias, depth_weight],
        micros=0,
        scalars=1,
    )
    d_second, keep_conv, send_conv = call(
        conv_back_kernel,
        [((seq, width), F32)] + slot_outs(ffn // 2 // TILE * rows + 3 * rows // 2, 1),
        [((ffn // 2 // TILE, width, TILE), F32), ((3, width, LANES), F32)],
        [lengths, d_left, taps_right, second, left_w, conv_w],
        [],
        micros=0,
        scalars=1,
    )
    conv_grads = Chunk(keep_conv, send_conv, (0, *CONV_BITS))
    conv_grads.start()
    d_second, ffn_grads, attn_grads = wave(d_second, ffn_grads, attn_grads, whole=False)
    d_second, conv_grads = wave(d_second, conv_grads)
    d_after_glu, d_first, keep_glu, send_glu = call(
        glu_back_kernel,
        [((seq, width), F32)] * 2 + slot_outs(width // TILE * rows + 16, 2),
        [
            ((seq, 2 * width), BF16),
            ((2, 32, LANES), F32),
            ((GROUPS, 16, 2 * LANES), F32),
            ((width // TILE, width, TILE), F32),
        ],
        [
            d_second,
            d_after_conv,
            after_glu,
            joined,
            first_norm,
            stream,
            small_ffn,
            small_attn,
            small_conv,
            glu_w,
        ],
        [norm_gain],
        micros=7,
    )
    glu_grads = Chunk(keep_glu, send_glu, (0, *GLU_BITS))
    glu_grads.start()
    held = received(d_after_glu, ffn_grads, attn_grads)
    held, glu_grads = wave(held, glu_grads)
    held, early = wave(held, ffn_grads, attn_grads, joined=True)
    held, conv_grads = wave(held, conv_grads)
    held, glu_grads = wave(held, glu_grads)
    held, late = wave(held, conv_grads, glu_grads, joined=True)
    held, early = wave(held, early)
    out_tokens, grad_tokens = call(
        tokens_kernel,
        [((part, width), BF16), ((part, width), F32)],
        [],
        [after_attn, hidden, ffn_out_w, held, d_first, stream],
        [norm_gain, ffn_out_bias],
    )
    grad_tokens, late = wave(grad_tokens, late)
    other = early.got[0]
    ffn_out, ffn_in, out, qkv, point = call(
        finish_early_kernel,
        [
            ((per_row, width), F32),
            ((rows, ffn), F32),
            ((rows, width), F32),
            ((rows, 3 * width), F32),
            ((per_row, half), F32),
        ],
        [],
        [early.keep, other],
        [],
    )
    (
        left,
        conv,
        glu,
        g_gains,
        g_shifts,
        g_depth,
        g_mid_gain,
        g_mid_bias,
        g_left_bias,
        g_ffn_in_bias,
        g_glu_bias,
        g_ffn_out_bias,
        g_conv_bias,
        g_point_bias,
    ) = call(
        finish_late_kernel,
        [
            ((rows, ffn), F32),
            ((3, rows, half), F32),
            ((rows, 2 * width), F32),
            ((4, rows), F32),
            ((4, rows), F32),
            ((9, LANES), F32),
            ((LANES,), F32),
            ((LANES,), F32),
            ((LANES,), F32),
            ((LANES,), F32),
            ((2 * rows,), F32),
            ((rows,), F32),
            ((half,), F32),
            ((half,), F32),
        ],
        [],
        [late.keep, late.got[0]],
        [],
    )
    results = (
        (glu, 0),
        (g_glu_bias, 0),
        (g_gains, 1),
        (g_shifts, 1),
        (g_mid_gain, 0),
        (g_mid_bias, 0),
        (left, 0),
        (g_left_bias, 0),
        (conv, 1),
        (g_conv_bias, None),
        (g_depth, 1),
        (point, 0),
        (g_point_bias, None),
        (qkv, 0),
        (out, 0),
        (ffn_in, 0),
        (g_ffn_in_bias, 0),
        (ffn_out, 0),
        (g_ffn_out_bias, 0),
    )
    final = []
    for value, axis in results:
        if axis is not None and below > 1:
            size = value.shape[axis] // below
            value = lax.dynamic_slice_in_dim(value, lax.axis_index("dp") % below * size, size, axis)
        final.append(value)
    return (out_tokens[None], grad_tokens[None], *final)


def solution(mesh):
    return jax.shard_map(
        per_device,
        mesh=mesh,
        in_specs=(P("dp", "head", None), P("dp"), P("dp", "head", None)) + (P(),) * 19,
        out_specs=(
            P("dp", "head", None),
            P("dp", "head", None),
            P("dp", None),
            P("dp"),
            P(None, "dp"),
            P(None, "dp"),
            P("dp"),
            P("dp"),
            P("dp", None),
            P("dp"),
            P(None, "dp", None),
            P(),
            P(None, "dp"),
            P("dp", None),
            P(),
            P("dp", None),
            P("dp", None),
            P("dp", None),
            P("dp"),
            P("dp", None),
            P("dp"),
        ),
        check_vma=False,
    )
```
